128 devices in a mesh: gx: 32 (over z, y, core), gy: 4 (over x).
Axes of the slice: x: 4, y: 4, z: 4, core: 2. Of those that a mesh axis runs over, the one named last changes fastest.
Arguments:
- initial_state: float32 [32, 2, 256, 4096], P(None, None, 'gy', 'gx'), may hold values from -34 to 34
- velocity: float32 [3, 2, 256, 4096], P(None, None, 'gy', 'gx'), may hold values from -0.3 to 0.3
- diffusivity: float32 [32], replicated, may hold values from 0.02 to 0.15
- reaction_rate: float32 [32], replicated, may hold values from 0.05 to 0.5
- start_basis: bfloat16 [4096, 128], replicated, may hold values from -0.09375 to 0.09375
Outputs:
- evolved: float32 [32, 2, 256, 4096], P(None, None, 'gy', 'gx')
- factor: bfloat16 [4096, 128], P(('gx', 'gy'))
- subspace_core: float32 [32, 2, 256, 128], P('gx', None, 'gy')
The draws below stay inside these ranges and needn't reach their ends.
All inputs are finite; a program needn't handle non-finite values.
Results may differ from the reference program's by a relative error of at most 0.012.
Values may be sent and summed in bfloat16 or wider, within the bound.
A program may use at most 64 MiB of HBM per device.

```python
import math
import jax
import jax.numpy as jnp
from jax import lax

SPECIES = 32
RANK = 128
SECTIONS = 4
NS_STEPS = 5
NZ = 2
NX = 4096
NY = 256


def draw_initial_state(key, part):
    subkeys = jax.random.split(jax.random.fold_in(key, 11), 3)
    values = jax.random.truncated_normal(subkeys[0], -4.0, 4.0, (SPECIES, NZ, NY, NX), jnp.float32)
    row_scale = jnp.exp(math.log(3.0) * jnp.arange(NX, dtype=jnp.float32) / NX)
    species = jnp.exp(jax.random.uniform(subkeys[2], (SPECIES,), jnp.float32, math.log(0.5), math.log(2.0)))
    return values * species[:, None, None, None] * row_scale


def steps_of(key, dims, pieces, low, largest):
    level = 1.0
    for axis_at, blocks in pieces:
        draws = jax.random.uniform(jax.random.fold_in(jax.random.fold_in(key, 6), axis_at), (blocks,), jnp.float32, low / len(pieces), largest / len(pieces))
        level = level * jnp.repeat(jnp.exp(draws), dims[axis_at] // blocks).reshape((-1,) + (1,) * (len(dims) - 1 - axis_at))
    return level


def bell_draw(stream_key, shape, spread, limit, held_as=jnp.bfloat16):
    entries = spread * jax.random.normal(stream_key, shape, jnp.float32)
    return jnp.clip(entries, min=-limit, max=limit).astype(held_as)


def setup_inputs(seed: int = 0) -> dict:
    key_of = jax.random.split(jax.random.key(seed), 6)
    return {
        "initial_state": draw_initial_state(jax.random.fold_in(key_of[5], 71), 0),
        "velocity": jnp.clip(jax.random.uniform(key_of[1], (3, NZ, NY, NX), jnp.float32, -0.3, 0.3) * steps_of(key_of[1], (3, NZ, NY, NX), ((2, 4), (3, 32)), -0.4, 0.0), -0.3, 0.3),
        "diffusivity": jnp.clip(jnp.exp(jax.random.uniform(key_of[2], (SPECIES,), jnp.float32, math.log(0.02), math.log(0.15))), 0.02, 0.15),
        "reaction_rate": jnp.clip(jnp.exp(jax.random.uniform(key_of[3], (SPECIES,), jnp.float32, math.log(0.05), math.log(0.5))), 0.05, 0.5),
        "start_basis": bell_draw(key_of[4], (NX, RANK), NX ** -0.5, 0.09375),
    }


def advance(field_now, velocity, diffusivity, reaction_rate):
    walled = jnp.pad(field_now, ((1, 1), (0, 0), (0, 0)))
    upper_side = walled[2:]
    lower_side = walled[:-2]
    north_side = jnp.roll(field_now, -1, axis=1)
    south_side = jnp.roll(field_now, 1, axis=1)
    east_side = jnp.roll(field_now, -1, axis=2)
    west_side = jnp.roll(field_now, 1, axis=2)
    laplacian = east_side + west_side + north_side + south_side + upper_side + lower_side - 6.0 * field_now
    transport = velocity[0] * (east_side - west_side) + velocity[1] * (north_side - south_side) + velocity[2] * (upper_side - lower_side)
    decay = reaction_rate * field_now * field_now * field_now / (1.0 + field_now * field_now)
    return field_now + diffusivity * laplacian - 0.5 * transport - decay

def reference(initial_state, velocity, diffusivity, reaction_rate, start_basis):

    def evolve(inputs):
        field_now, kappa_one, rate_one = inputs
        for section_index in range(SECTIONS):
            field_now = advance(field_now, velocity, kappa_one, rate_one)
        return field_now
    evolved = lax.map(evolve, (initial_state, diffusivity, reaction_rate))
    columns = evolved.astype(jnp.bfloat16).reshape(SPECIES * NZ * NY, NX)
    project = jnp.dot(columns, start_basis, preferred_element_type=jnp.float32).astype(jnp.bfloat16)
    images = lax.dot_general(columns, project, (((0,), (0,)), ((), ())), preferred_element_type=jnp.float32)
    highest = lax.Precision.HIGHEST
    identity = jnp.eye(RANK, dtype=jnp.float32)
    gram_matrix = jnp.dot(images.T, images, precision=highest)
    scaling = jnp.sqrt(NX / (jnp.trace(gram_matrix) + 1e-06))
    factor = images * scaling
    for section_index in range(NS_STEPS):
        gram_matrix = jnp.dot(factor.T, factor, precision=highest) / NX
        factor = jnp.dot(factor, 1.5 * identity - 0.5 * gram_matrix, precision=highest)
    factor = factor.astype(jnp.bfloat16)
    subspace_core = jnp.dot(columns, factor, preferred_element_type=jnp.float32) / math.sqrt(NX)
    return (evolved, factor, subspace_core.reshape(SPECIES, NZ, NY, RANK))
```

```python
import jax
import jax.numpy as jnp
from jax import lax
from jax.experimental import pallas as pl
from jax.experimental.pallas import tpu as pltpu
from jax.sharding import PartitionSpec as P

SECTIONS = 4
NS_STEPS = 5
GROUPS = 4
MESH = pl.DeviceIdType.MESH
F32 = jnp.float32
BF16 = jnp.bfloat16


def rolled(x, shift):
    return pltpu.roll(x, shift, 1)


def full_dot(a, b):
    return jnp.dot(a, b, precision=lax.Precision.HIGHEST, preferred_element_type=F32)


def kernel(
    init_hbm, vel_hbm, kappa_ref, rate_ref, basis_hbm,
    evolved_hbm, factor_ref, core_ref,
    state, vel, basis, edge_acc, x_send, x_left, x_right, y_send, y_recv,
    own_cols, own_t, cols, proj, image_part, image_all, image_own, mixing,
    load_sem, out_sem, xs_sem, xr_sem, ys_sem, yr_sem, as_sem, ar_sem, gs_sem, gr_sem, is_sem, ir_sem,
):
    species = state.shape[1]
    ny = state.shape[3] - 16
    per = species // GROUPS
    ngx, ngy = lax.axis_size("gx"), lax.axis_size("gy")
    gx, gy = lax.axis_index("gx"), lax.axis_index("gy")
    right, left = lax.rem(gx + 1, ngx), lax.rem(gx + ngx - 1, ngx)
    north, south = lax.rem(gy + 1, ngy), lax.rem(gy + ngy - 1, ngy)
    lane = lax.broadcasted_iota(jnp.int32, (ny, 128), 1)

    def load_state(g):
        return pltpu.make_async_copy(
            init_hbm.at[pl.ds(g * per, per)],
            state.at[0, pl.ds(g * per, per), :, pl.ds(8, ny), :],
            load_sem.at[g],
        )

    load_vel = pltpu.make_async_copy(vel_hbm, vel, load_sem.at[GROUPS])
    load_basis = pltpu.make_async_copy(basis_hbm, basis, load_sem.at[GROUPS + 1])
    for g in range(GROUPS):
        load_state(g).start()
    load_vel.start()
    load_basis.start()

    barrier = pltpu.get_barrier_semaphore()

    @pl.loop(1, ngx)
    def _(d):
        pl.semaphore_signal(barrier, 1, device_id={"gx": lax.rem(gx + d, ngx)}, device_id_type=MESH)

    @pl.loop(1, ngy)
    def _(d):
        pl.semaphore_signal(barrier, 1, device_id={"gy": lax.rem(gy + d, ngy)}, device_id_type=MESH)

    def x_copy(e, to_left):
        return pltpu.make_async_remote_copy(
            src_ref=x_send.at[e],
            dst_ref=(x_right if to_left else x_left).at[e],
            send_sem=xs_sem.at[int(to_left)],
            recv_sem=xr_sem.at[int(to_left), e],
            device_id={"gx": left if to_left else right},
            device_id_type=MESH,
        )

    def y_copy(e, to_south):
        d = int(to_south)
        return pltpu.make_async_remote_copy(
            src_ref=y_send.at[d, e],
            dst_ref=y_recv.at[d, e],
            send_sem=ys_sem.at[d],
            recv_sem=yr_sem.at[d, e],
            device_id={"gy": south if to_south else north},
            device_id_type=MESH,
        )

    def pack(e, j, z, new):
        mask = (lane == 2 * j) | (lane == 2 * j + 1)
        rows = pl.ds(z * ny, ny)
        edge_acc[rows, :] = jnp.where(mask, rolled(new, 2 * j + 1), edge_acc[rows, :])
        y_send[0, e, pl.ds(2 * j + z, 1), :] = new[ny - 1 :, :]
        y_send[1, e, pl.ds(2 * j + z, 1), :] = new[:1, :]

    def send_edges(e):
        x_send[e] = edge_acc[...].astype(x_send.dtype)
        x_copy(e, True).start()
        x_copy(e, False).start()
        y_copy(e, True).start()
        y_copy(e, False).start()

    def column_copy(s):
        return pltpu.make_async_remote_copy(
            src_ref=own_cols.at[s],
            dst_ref=cols.at[gx],
            send_sem=as_sem,
            recv_sem=ar_sem.at[gx],
            device_id={"gx": s},
            device_id_type=MESH,
        )

    edge_acc[...] = jnp.zeros_like(edge_acc)

    for g in range(GROUPS):
        load_state(g).wait()

        @pl.loop(0, per)
        def _(j):
            for z in range(2):
                pack(g, j, z, state[0, g * per + j, z, pl.ds(8, ny), :])

        if g == 0:
            pl.semaphore_wait(barrier, ngx + ngy - 2)
        send_edges(g)

    load_vel.wait()
    vel[...] = vel[...] * 0.5
    vel[2, 1] = -vel[2, 1]

    @pl.loop(0, SECTIONS * GROUPS)
    def _(e):
        k, g = e // GROUPS, lax.rem(e, GROUPS)
        now = lax.rem(k, 2)
        x_copy(e, True).wait_recv()
        x_copy(e, False).wait_recv()
        y_copy(e, True).wait_recv()
        y_copy(e, False).wait_recv()

        wide = lax.broadcasted_iota(jnp.int32, edge_acc.shape, 1)
        edge_acc[...] = jnp.where(
            lax.rem(wide, 2) == 0, x_left[e].astype(F32), x_right[e].astype(F32)
        )

        @pl.loop(0, per)
        def _(j):
            s = g * per + j
            for z in range(2):
                state[now, s, z, pl.ds(7, 1), :] = y_recv[0, e, pl.ds(2 * j + z, 1), :]
                state[now, s, z, pl.ds(8 + ny, 1), :] = y_recv[1, e, pl.ds(2 * j + z, 1), :]
            kappa, rate = kappa_ref[s], rate_ref[s]
            middle = 1.0 - 6.0 * kappa - rate
            for z in range(2):
                c = state[now, s, z, pl.ds(8, ny), :]
                other = state[now, s, 1 - z, pl.ds(8, ny), :]
                up = state[now, s, z, pl.ds(9, ny), :]
                down = state[now, s, z, pl.ds(7, ny), :]
                halo = rolled(edge_acc[pl.ds(z * ny, ny), :], 127 - 2 * j)
                east = rolled(jnp.where(lane == 0, halo, c), 127)
                west = rolled(jnp.where(lane == 127, halo, c), 1)
                d = 1.0 + c * c
                seed = pl.reciprocal(d, approx=True)
                inverse = seed * (2.0 - d * seed)
                new = (
                    c * (middle + rate * inverse)
                    + kappa * ((east + west) + (up + down))
                    + (kappa - vel[2, z]) * other
                    - vel[0, z] * (east - west)
                    - vel[1, z] * (up - down)
                )
                state[1 - now, s, z, pl.ds(8, ny), :] = new

        @pl.when(k < SECTIONS - 1)
        def _():
            @pl.loop(0, per)
            def _(j):
                for z in range(2):
                    pack(e + GROUPS, j, z, state[1 - now, g * per + j, z, pl.ds(8, ny), :])

            send_edges(e + GROUPS)

        @pl.when(k == SECTIONS - 1)
        def _():
            @pl.loop(0, per)
            def _(j):
                s = g * per + j
                for z in range(2):
                    own_cols[s, pl.ds(z * ny, ny), :] = state[0, s, z, pl.ds(8, ny), :].astype(BF16)

            @pl.loop(0, per)
            def _(j):
                s = g * per + lax.rem(j + gx, per)

                @pl.when(s != gx)
                def _():
                    column_copy(s).start()

            pltpu.make_async_copy(
                state.at[0, pl.ds(g * per, per), :, pl.ds(8, ny), :],
                evolved_hbm.at[pl.ds(g * per, per)],
                out_sem,
            ).start()

    def column_arrival(j):
        return pltpu.make_async_copy(cols.at[j], cols.at[j], ar_sem.at[j])

    cols[gx] = own_cols[gx]

    @pl.loop(0, species)
    def _(s):
        own_t[s] = own_cols[s].T

    load_basis.wait()

    def project_step(j):
        rows = pl.ds(pl.multiple_of(j * 128, 128), 128)
        return jnp.dot(cols[j], basis[rows, :], preferred_element_type=F32)

    def project_next(d, total):
        j = lax.rem(gx + ngx - d, ngx)
        column_arrival(j).wait()
        return total + project_step(j)

    project = lax.fori_loop(1, ngx, project_next, project_step(gx))
    proj[gx] = project.astype(BF16)

    core = lax.rem(gx, 2)
    stride_a = 2 + 6 * core
    stride_b = 8 - 6 * core
    pos_a = lax.rem(gx // stride_a, 4)
    pos_b = lax.rem(gx // stride_b, 4)
    sibling = gx + 1 - 2 * core

    def slot_of(a, b):
        return lax.rem(a, 4) * stride_a + lax.rem(b, 4) * stride_b + core

    def gather(held, which, use):
        def send(slot, peer):
            pltpu.make_async_remote_copy(
                src_ref=held.at[slot],
                dst_ref=held.at[slot],
                send_sem=gs_sem.at[which],
                recv_sem=gr_sem.at[which, slot],
                device_id={"gx": peer},
                device_id_type=MESH,
            ).start()

        def arrival(slot):
            pltpu.make_async_copy(held.at[slot], held.at[slot], gr_sem.at[which, slot]).wait()

        order = (1, 3, 2)
        for d in order:
            send(gx, slot_of(pos_a + d, pos_b))
        for d in order:
            send(gx, slot_of(pos_a, pos_b + d))
        send(gx, sibling)
        total = use(gx)
        for d in order:
            slot = slot_of(pos_a + d, pos_b)
            arrival(slot)
            for f in order:
                send(slot, slot_of(pos_a, pos_b + f))
            send(slot, sibling)
            total += use(slot)
        for d in (0, 1, 3, 2):
            for f in order:
                slot = slot_of(pos_a + d, pos_b + f)
                arrival(slot)
                send(slot, sibling)
                total += use(slot)

        def other(i, total):
            slot = 2 * i + 1 - core
            arrival(slot)
            return total + use(slot)

        return lax.fori_loop(0, ngx // 2, other, total)

    def gather_done(held, which):
        for size in (16, 15):
            part = held.at[pl.ds(0, size)]
            pltpu.make_async_copy(part, part, gs_sem.at[which]).wait()

    part = gather(proj, 0, lambda s: jnp.dot(own_t[s], proj[s], preferred_element_type=F32))

    image_part[gy] = part.astype(BF16)

    def image_copy(d):
        return pltpu.make_async_remote_copy(
            src_ref=image_part.at[gy],
            dst_ref=image_part.at[gy],
            send_sem=is_sem.at[d],
            recv_sem=ir_sem.at[gy],
            device_id={"gy": lax.rem(gy + d, ngy)},
            device_id_type=MESH,
        )

    for d in (1, 3, 2):
        image_copy(d).start()
    for d in (1, 3, 2):
        slot = lax.rem(gy + d, ngy)
        pltpu.make_async_copy(image_part.at[slot], image_part.at[slot], ir_sem.at[slot]).wait()
    image_own[...] = (image_part[0].astype(F32) + image_part[1].astype(F32)) + (
        image_part[2].astype(F32) + image_part[3].astype(F32)
    )
    image_all[gx] = image_own[...].astype(BF16)

    contract_rows = (((0,), (0,)), ((), ()))

    def use_image(s):
        block = image_all[s]
        gram = lax.dot_general(block, block, contract_rows, preferred_element_type=F32)
        carried = jnp.dot(cols[s], block, preferred_element_type=F32)
        return jnp.concatenate([gram, carried], axis=0)

    both = gather(image_all, 1, use_image)
    gram, carried = both[:128], both[128:]

    row = lax.broadcasted_iota(jnp.int32, (128, 128), 0)
    column = lax.broadcasted_iota(jnp.int32, (128, 128), 1)
    identity = jnp.where(row == column, 1.0, 0.0).astype(F32)
    count = 128.0 * ngx
    trace = jnp.sum(gram * identity, keepdims=True)
    squared = count / (trace + 1e-6)
    gram = gram * (squared / count)
    mix = jnp.sqrt(squared) * identity
    for step in range(NS_STEPS):
        poly = 1.5 * identity - 0.5 * gram
        mix = full_dot(mix, poly)
        if step < NS_STEPS - 1:
            gram = full_dot(poly, full_dot(gram, poly))
    mixing[...] = mix

    rows = pl.ds(pl.multiple_of(gy * 32, 32), 32)
    factor_ref[...] = full_dot(image_own[rows, :], mix).astype(BF16)
    result = full_dot(carried, mix) * (count ** -0.5)
    core_ref[0, 0] = result[:ny]
    core_ref[0, 1] = result[ny:]

    for d in range(2):
        pltpu.make_async_copy(x_send, x_send, xs_sem.at[d]).wait()
        pltpu.make_async_copy(y_send.at[d], y_send.at[d], ys_sem.at[d]).wait()
    for g in range(GROUPS):
        pltpu.make_async_copy(
            state.at[0, pl.ds(g * per, per), :, pl.ds(8, ny), :],
            evolved_hbm.at[pl.ds(g * per, per)],
            out_sem,
        ).wait()
    sent = own_cols.at[pl.ds(0, ngx - 1)]
    pltpu.make_async_copy(sent, sent, as_sem).wait()
    gather_done(proj, 0)
    gather_done(image_all, 1)
    for d in (1, 3, 2):
        image_copy(d).wait_send()


def shards(initial_state, velocity, diffusivity, reaction_rate, start_basis):
    species, nz, ny, nx = initial_state.shape
    ngx, ngy = lax.axis_size("gx"), lax.axis_size("gy")
    rank = start_basis.shape[1]
    exchanges = SECTIONS * GROUPS
    rows = 2 * species // GROUPS
    anywhere = pl.BlockSpec(memory_space=pl.ANY)
    scalars = pl.BlockSpec(memory_space=pltpu.SMEM)
    vmem = pl.BlockSpec(memory_space=pltpu.VMEM)
    dma = pltpu.SemaphoreType.DMA
    return pl.pallas_call(
        kernel,
        out_shape=(
            jax.ShapeDtypeStruct(initial_state.shape, F32),
            jax.ShapeDtypeStruct((ny // 2, rank), BF16),
            jax.ShapeDtypeStruct((1, nz, ny, rank), F32),
        ),
        in_specs=[anywhere, anywhere, scalars, scalars, anywhere],
        out_specs=(anywhere, vmem, vmem),
        scratch_shapes=[
            pltpu.VMEM((2, species, nz, ny + 16, nx), F32),
            pltpu.VMEM((3, nz, ny, nx), F32),
            pltpu.VMEM(start_basis.shape, BF16),
            pltpu.VMEM((nz * ny, nx), F32),
            pltpu.VMEM((exchanges, nz * ny, nx), BF16),
            pltpu.VMEM((exchanges, nz * ny, nx), BF16),
            pltpu.VMEM((exchanges, nz * ny, nx), BF16),
            pltpu.VMEM((2, exchanges, rows, nx), F32),
            pltpu.VMEM((2, exchanges, rows, nx), F32),
            pltpu.VMEM((species, nz * ny, nx), BF16),
            pltpu.VMEM((species, nx, nz * ny), BF16),
            pltpu.VMEM((species, nz * ny, nx), BF16),
            pltpu.VMEM((ngx, nz * ny, rank), BF16),
            pltpu.VMEM((ngy, nx, rank), BF16),
            pltpu.VMEM((ngx, nx, rank), BF16),
            pltpu.VMEM((nx, rank), F32),
            pltpu.VMEM((rank, rank), F32),
            dma((GROUPS + 2,)),
            dma,
            dma((2,)),
            dma((2, exchanges)),
            dma((2,)),
            dma((2, exchanges)),
            dma,
            dma((ngx,)),
            dma((2,)),
            dma((2, ngx)),
            dma((ngy,)),
            dma((ngy,)),
        ],
        compiler_params=pltpu.CompilerParams(
            collective_id=0, has_side_effects=True, vmem_limit_bytes=48 << 20
        ),
    )(initial_state, velocity, diffusivity, reaction_rate, start_basis)


def solution(mesh):
    return jax.shard_map(
        shards,
        mesh=mesh,
        in_specs=(P(None, None, "gy", "gx"), P(None, None, "gy", "gx"), P(), P(), P()),
        out_specs=(P(None, None, "gy", "gx"), P(("gx", "gy"), None), P("gx", None, "gy", None)),
        check_vma=False,
    )
```

```python
import functools

import jax
import jax.numpy as jnp
from jax import lax
from jax.experimental import pallas as pl
from jax.experimental.pallas import tpu as pltpu
from jax.sharding import PartitionSpec as P

SECTIONS = 4
NS_STEPS = 5
GROUPS = 4
UNROLL = 2
VMEM_LIMIT = 32 << 20
MESH = pl.DeviceIdType.MESH
F32 = jnp.float32
BF16 = jnp.bfloat16


def rolled(x, shift):
    return pltpu.roll(x, shift, 1)


def full_dot(a, b):
    return jnp.dot(a, b, precision=lax.Precision.HIGHEST, preferred_element_type=F32)


def kernel(
    init_hbm, vel_hbm, kappa_hbm, rate_hbm, basis_hbm,
    evolved_ref, gram_ref, carried_ref, image_ref,
    state, state_b, vel, kappa_ref, rate_ref, basis, halos, x_send, x_left, x_right, y_send, y_recv,
    own_cols, own_t, cols, proj, image_part, image_all, image_own,
    load_sem, xs_sem, xr_sem, ys_sem, yr_sem, as_sem, ar_sem, gs_sem, gr_sem, is_sem, ir_sem,
):
    species = state.shape[0]
    ny = state.shape[2] - 16
    per = species // GROUPS
    ngx, ngy = lax.axis_size("gx"), lax.axis_size("gy")
    gx, gy = lax.axis_index("gx"), lax.axis_index("gy")
    right, left = lax.rem(gx + 1, ngx), lax.rem(gx + ngx - 1, ngx)
    north, south = lax.rem(gy + 1, ngy), lax.rem(gy + ngy - 1, ngy)
    core = lax.rem(gx, 2)
    half = ngx // 2
    lane = lax.broadcasted_iota(jnp.int32, (ny, 128), 1)
    pair = lane // 2

    def block(x):
        at = lax.rem(x, 2) * half + x // 2
        return pl.ds(pl.multiple_of(at * 128, 128), 128)

    def load_state(g):
        return pltpu.make_async_copy(
            init_hbm.at[pl.ds(g * per, per)],
            state.at[pl.ds(g * per, per), :, pl.ds(8, ny), :],
            load_sem.at[g],
        )

    load_vel = pltpu.make_async_copy(vel_hbm, vel, load_sem.at[GROUPS])
    load_kappa = pltpu.make_async_copy(kappa_hbm, kappa_ref, load_sem.at[GROUPS + 2])
    load_rate = pltpu.make_async_copy(rate_hbm, rate_ref, load_sem.at[GROUPS + 3])
    for g in range(GROUPS):
        load_state(g).start()
    load_kappa.start()
    load_rate.start()
    load_vel.start()

    barrier = pltpu.get_barrier_semaphore()

    @pl.loop(1, ngx)
    def _(d):
        pl.semaphore_signal(barrier, 1, device_id={"gx": lax.rem(gx + d, ngx)}, device_id_type=MESH)

    @pl.loop(1, ngy)
    def _(d):
        pl.semaphore_signal(barrier, 1, device_id={"gy": lax.rem(gy + d, ngy)}, device_id_type=MESH)

    def x_copy(e, to_left):
        return pltpu.make_async_remote_copy(
            src_ref=x_send.at[e],
            dst_ref=(x_right if to_left else x_left).at[e],
            send_sem=xs_sem.at[int(to_left)],
            recv_sem=xr_sem.at[int(to_left), e],
            device_id={"gx": left if to_left else right},
            device_id_type=MESH,
        )

    def y_copy(e, to_south):
        d = int(to_south)
        return pltpu.make_async_remote_copy(
            src_ref=y_send.at[d, e],
            dst_ref=y_recv.at[d, e],
            send_sem=ys_sem.at[d],
            recv_sem=yr_sem.at[d, e],
            device_id={"gy": south if to_south else north},
            device_id_type=MESH,
        )

    def column_copy(s):
        return pltpu.make_async_remote_copy(
            src_ref=own_cols.at[s],
            dst_ref=cols.at[:, block(gx)],
            send_sem=as_sem,
            recv_sem=ar_sem.at[gx],
            device_id={"gx": s},
            device_id_type=MESH,
        )

    def send_edges(e, now, first):
        for z in range(2):
            packed = jnp.zeros((ny, 128), F32)
            for j in range(per):
                cells = now[first + j, z, pl.ds(8, ny), :]
                packed = jnp.where(pair == j, rolled(cells, 2 * j + 1), packed)
                y_send[0, e, pl.ds(2 * j + z, 1), :] = now[first + j, z, pl.ds(7 + ny, 1), :]
                y_send[1, e, pl.ds(2 * j + z, 1), :] = now[first + j, z, pl.ds(8, 1), :]
            x_send[e, pl.ds(z * ny, ny), :] = packed.astype(x_send.dtype)
        x_copy(e, True).start()
        x_copy(e, False).start()
        y_copy(e, True).start()
        y_copy(e, False).start()

    load_state(0).wait()
    pl.semaphore_wait(barrier, ngx + ngy - 2)
    send_edges(0, state, 0)
    for g in range(1, GROUPS):
        load_state(g).wait()

    @pl.loop(1, GROUPS)
    def _(g):
        send_edges(g, state, g * per)

    @pl.loop(0, ngx)
    def _(x):
        pltpu.make_async_copy(
            basis_hbm.at[pl.ds(pl.multiple_of(x * 128, 128), 128)], basis.at[block(x)],
            load_sem.at[GROUPS + 1],
        ).start()

    load_vel.wait()
    vel[...] = vel[...] * 0.5
    vel[2, 1] = -vel[2, 1]
    load_kappa.wait()
    load_rate.wait()

    def advance(k, g, now, new):
        e = k * GROUPS + g
        last = k == SECTIONS - 1
        x_copy(e, True).wait_recv()
        x_copy(e, False).wait_recv()
        y_copy(e, True).wait_recv()
        y_copy(e, False).wait_recv()

        wide = lax.broadcasted_iota(jnp.int32, halos.shape, 1)
        halos[...] = jnp.where(
            lax.rem(wide, 2) == 0,
            rolled(x_right[e].astype(F32), 127),
            rolled(x_left[e].astype(F32), 1),
        )

        for j in range(per):
            for z in range(2):
                now[g * per + j, z, pl.ds(7, 1), :] = y_recv[0, e, pl.ds(2 * j + z, 1), :]
                now[g * per + j, z, pl.ds(8 + ny, 1), :] = y_recv[1, e, pl.ds(2 * j + z, 1), :]

        @pl.loop(0, per, step=UNROLL)
        def _(j0):
            for i in range(UNROLL):
                j = j0 + i
                s = g * per + j
                kappa, rate = kappa_ref[s], rate_ref[s]
                middle = 1.0 - 6.0 * kappa - rate
                for z in range(2):
                    c = now[s, z, pl.ds(8, ny), :]
                    other = now[s, 1 - z, pl.ds(8, ny), :]
                    up = now[s, z, pl.ds(9, ny), :]
                    down = now[s, z, pl.ds(7, ny), :]
                    halo = rolled(halos[pl.ds(z * ny, ny), :], 127 - 2 * j)
                    east = jnp.where(lane == 127, halo, rolled(c, 127))
                    west = jnp.where(lane == 0, halo, rolled(c, 1))
                    result = (
                        c * (middle + rate * (1.0 / (1.0 + c * c)))
                        + kappa * ((east + west) + (up + down))
                        + (kappa - vel[2, z]) * other
                        - vel[0, z] * (east - west)
                        - vel[1, z] * (up - down)
                    )
                    if last:
                        evolved_ref[s, z] = result
                        own_cols[s, pl.ds(z * ny, ny), :] = result.astype(BF16)
                    else:
                        new[s, z, pl.ds(8, ny), :] = result

        if not last:
            send_edges(e + GROUPS, new, g * per)

    buffers = (state, state_b)
    for k in range(SECTIONS - 1):

        @pl.loop(0, GROUPS)
        def _(g):
            advance(k, g, buffers[k % 2], buffers[(k + 1) % 2])

    @pl.loop(0, GROUPS)
    def _(g):
        advance(SECTIONS - 1, g, buffers[(SECTIONS - 1) % 2], None)

        @pl.loop(0, per)
        def _(j):
            s = g * per + lax.rem(j + gx, per)

            @pl.when(s != gx)
            def _():
                column_copy(s).start()

    def column_arrival(x):
        return pltpu.make_async_copy(cols.at[:, block(x)], cols.at[:, block(x)], ar_sem.at[x])

    cols[:, block(gx)] = own_cols[gx]

    @pl.loop(0, species, step=4)
    def _(s):
        for i in range(4):
            own_t[:, block(s + i)] = own_cols[s + i].T

    basis_all = pltpu.make_async_copy(basis_hbm, basis, load_sem.at[GROUPS + 1])
    basis_all.wait()

    @pl.loop(1, ngx)
    def _(d):
        column_arrival(lax.rem(gx + ngx - d, ngx)).wait()

    proj[block(gx), :] = jnp.dot(cols[...], basis[...], preferred_element_type=F32).astype(BF16)

    stride_a = 2 + 6 * core
    stride_b = 8 - 6 * core
    pos_a = lax.rem(gx // stride_a, 4)
    pos_b = lax.rem(gx // stride_b, 4)
    sibling = gx + 1 - 2 * core

    def device_at(a, b):
        return lax.rem(a, 4) * stride_a + lax.rem(b, 4) * stride_b + core

    def gather(held, which, use):
        def send(x, peer):
            pltpu.make_async_remote_copy(
                src_ref=held.at[block(x)],
                dst_ref=held.at[block(x)],
                send_sem=gs_sem.at[which],
                recv_sem=gr_sem.at[which, x],
                device_id={"gx": peer},
                device_id_type=MESH,
            ).start()

        def arrival(x):
            pltpu.make_async_copy(held.at[block(x)], held.at[block(x)], gr_sem.at[which, x]).wait()

        order = (1, 3, 2)
        for d in order:
            send(gx, device_at(pos_a + d, pos_b))
        for d in order:
            send(gx, device_at(pos_a, pos_b + d))
        send(gx, sibling)
        for d in order:
            x = device_at(pos_a + d, pos_b)
            arrival(x)
            for f in order:
                send(x, device_at(pos_a, pos_b + f))
            send(x, sibling)
        for d in (0, 1, 3, 2):
            for f in order:
                x = device_at(pos_a + d, pos_b + f)
                arrival(x)
                send(x, sibling)
        first = use(core)

        @pl.loop(0, half)
        def _(i):
            arrival(2 * i + 1 - core)

        second = use(1 - core)
        return jax.tree.map(jnp.add, first, second)

    def gather_done(held, which):
        part = held.at[pl.ds(0, (ngx - 1) * 128)]
        pltpu.make_async_copy(part, part, gs_sem.at[which]).wait()

    def span(c):
        return pl.ds(pl.multiple_of(c * (half * 128), half * 128), half * 128)

    part = gather(
        proj, 0, lambda c: jnp.dot(own_t[:, span(c)], proj[span(c), :], preferred_element_type=F32)
    )

    image_part[gy] = part.astype(BF16)

    def image_copy(d):
        return pltpu.make_async_remote_copy(
            src_ref=image_part.at[gy],
            dst_ref=image_part.at[gy],
            send_sem=is_sem.at[d],
            recv_sem=ir_sem.at[gy],
            device_id={"gy": lax.rem(gy + d, ngy)},
            device_id_type=MESH,
        )

    for d in (1, 3, 2):
        image_copy(d).start()
    for d in (1, 3, 2):
        slot = lax.rem(gy + d, ngy)
        pltpu.make_async_copy(image_part.at[slot], image_part.at[slot], ir_sem.at[slot]).wait()
    image_own[...] = (image_part[0].astype(F32) + image_part[1].astype(F32)) + (
        image_part[2].astype(F32) + image_part[3].astype(F32)
    )
    image_all[block(gx), :] = image_own[...].astype(BF16)

    contract_rows = (((0,), (0,)), ((), ()))

    def use_image(c):
        x = image_all[span(c), :]
        return (
            lax.dot_general(x, x, contract_rows, preferred_element_type=F32),
            jnp.dot(cols[:, span(c)], x, preferred_element_type=F32),
        )

    gram, carried = gather(image_all, 1, use_image)

    gram_ref[...] = gram
    carried_ref[...] = carried
    rows = pl.ds(pl.multiple_of(gy * 32, 32), 32)
    image_ref[...] = image_own[rows, :]

    for d in range(2):
        pltpu.make_async_copy(x_send, x_send, xs_sem.at[d]).wait()
        pltpu.make_async_copy(y_send.at[d], y_send.at[d], ys_sem.at[d]).wait()
    sent = own_cols.at[pl.ds(0, ngx - 1)]
    pltpu.make_async_copy(sent, sent, as_sem).wait()
    gather_done(proj, 0)
    gather_done(image_all, 1)
    for d in (1, 3, 2):
        image_copy(d).wait_send()


def finish(count, evolved_ref, gram_ref, carried_ref, image_ref, out_hbm, factor_ref, core_ref, sem):
    writing = pltpu.make_async_copy(evolved_ref, out_hbm, sem)
    writing.start()
    row = lax.broadcasted_iota(jnp.int32, (128, 128), 0)
    column = lax.broadcasted_iota(jnp.int32, (128, 128), 1)
    identity = jnp.where(row == column, 1.0, 0.0).astype(F32)
    gram = gram_ref[...]
    trace = jnp.sum(gram * identity, keepdims=True)
    squared = count / (trace + 1e-6)
    gram = gram * (squared / count)
    mix = jnp.sqrt(squared) * identity
    for step in range(NS_STEPS):
        poly = 1.5 * identity - 0.5 * gram
        mix = full_dot(mix, poly)
        if step < NS_STEPS - 1:
            gram = full_dot(poly, full_dot(gram, poly))

    factor_ref[...] = full_dot(image_ref[...], mix).astype(BF16)
    result = full_dot(carried_ref[...], mix) * (count ** -0.5)
    ny = core_ref.shape[2]
    core_ref[0, 0] = result[:ny]
    core_ref[0, 1] = result[ny:]
    writing.wait()


def shards(initial_state, velocity, diffusivity, reaction_rate, start_basis):
    species, nz, ny, nx = initial_state.shape
    ngx, ngy = lax.axis_size("gx"), lax.axis_size("gy")
    rank = start_basis.shape[1]
    operands = (initial_state, velocity, diffusivity, reaction_rate, start_basis)
    exchanges = SECTIONS * GROUPS
    rows = 2 * species // GROUPS
    hbm = pl.BlockSpec(memory_space=pltpu.HBM)
    vmem = pl.BlockSpec(memory_space=pltpu.VMEM)
    dma = pltpu.SemaphoreType.DMA
    evolved, gram, carried, image = pl.pallas_call(
        kernel,
        out_shape=(
            jax.ShapeDtypeStruct(initial_state.shape, F32),
            jax.ShapeDtypeStruct((rank, rank), F32),
            jax.ShapeDtypeStruct((nz * ny, rank), F32),
            jax.ShapeDtypeStruct((nx // ngy, rank), F32),
        ),
        in_specs=[hbm] * 5,
        out_specs=(vmem,) * 4,
        scratch_shapes=[
            pltpu.VMEM((species, nz, ny + 16, nx), F32),
            pltpu.VMEM((species, nz, ny + 16, nx), F32),
            pltpu.VMEM((3, nz, ny, nx), F32),
            pltpu.SMEM((species,), F32),
            pltpu.SMEM((species,), F32),
            pltpu.VMEM(start_basis.shape, BF16),
            pltpu.VMEM((nz * ny, nx), F32),
            pltpu.VMEM((exchanges, nz * ny, nx), BF16),
            pltpu.VMEM((exchanges, nz * ny, nx), BF16),
            pltpu.VMEM((exchanges, nz * ny, nx), BF16),
            pltpu.VMEM((2, exchanges, rows, nx), F32),
            pltpu.VMEM((2, exchanges, rows, nx), F32),
            pltpu.VMEM((species, nz * ny, nx), BF16),
            pltpu.VMEM((nx, species * nz * ny), BF16),
            pltpu.VMEM((nz * ny, ngx * nx), BF16),
            pltpu.VMEM((species * nz * ny, rank), BF16),
            pltpu.VMEM((ngy, nx, rank), BF16),
            pltpu.VMEM((ngx * nx, rank), BF16),
            pltpu.VMEM((nx, rank), F32),
            dma((GROUPS + 4,)),
            dma((2,)),
            dma((2, exchanges)),
            dma((2,)),
            dma((2, exchanges)),
            dma,
            dma((ngx,)),
            dma((2,)),
            dma((2, ngx)),
            dma((ngy,)),
            dma((ngy,)),
        ],
        compiler_params=pltpu.CompilerParams(
            collective_id=0, has_side_effects=True, vmem_limit_bytes=VMEM_LIMIT
        ),
    )(*(pltpu.with_memory_space_constraint(x, pltpu.HBM) for x in operands))
    return pl.pallas_call(
        functools.partial(finish, float(nx * ngx)),
        out_shape=(
            jax.ShapeDtypeStruct(initial_state.shape, F32),
            jax.ShapeDtypeStruct((nx // ngy, rank), BF16),
            jax.ShapeDtypeStruct((1, nz, ny, rank), F32),
        ),
        in_specs=[pl.BlockSpec(memory_space=pl.ANY), vmem, vmem, vmem],
        out_specs=(hbm, vmem, vmem),
        scratch_shapes=[dma],
        compiler_params=pltpu.CompilerParams(vmem_limit_bytes=8 << 20),
    )(evolved, gram, carried, image)


def solution(mesh):
    return jax.shard_map(
        shards,
        mesh=mesh,
        in_specs=(P(None, None, "gy", "gx"), P(None, None, "gy", "gx"), P(), P(), P()),
        out_specs=(P(None, None, "gy", "gx"), P(("gx", "gy"), None), P("gx", None, "gy", None)),
        check_vma=False,
    )
```

```python
import functools

import jax
import jax.numpy as jnp
from jax import lax
from jax.experimental import pallas as pl
from jax.experimental.pallas import tpu as pltpu
from jax.sharding import PartitionSpec as P

SECTIONS = 4
NS_STEPS = 5
GROUPS = 4
UNROLL = 2
VMEM_LIMIT = 32 << 20
MESH = pl.DeviceIdType.MESH
F32 = jnp.float32
BF16 = jnp.bfloat16


def rolled(x, shift):
    return pltpu.roll(x, shift, 1)


def halves(x):
    high = x.astype(BF16)
    return high, (x - high.astype(F32)).astype(BF16)


def full_dot(a, b):
    a_high, a_low = halves(a)
    b_high, b_low = halves(b)
    return jnp.dot(
        jnp.concatenate([a_high, a_high, a_low], axis=1),
        jnp.concatenate([b_high, b_low, b_high], axis=0),
        preferred_element_type=F32,
    )


def tree_sum(terms):
    while len(terms) > 1:
        terms = [a + b for a, b in zip(terms[::2], terms[1::2])]
    return terms[0]


def mixing(gram, count):
    row = lax.broadcasted_iota(jnp.int32, gram.shape, 0)
    column = lax.broadcasted_iota(jnp.int32, gram.shape, 1)
    identity = jnp.where(row == column, 1.0, 0.0).astype(F32)
    trace = jnp.sum(gram * identity, keepdims=True)
    squared = count / (trace + 1e-6)
    gram = gram * (squared / count)
    mix = jnp.sqrt(squared) * identity
    for step in range(NS_STEPS):
        poly = 1.5 * identity - 0.5 * gram
        mix = full_dot(mix, poly)
        if step < NS_STEPS - 1:
            gram = full_dot(poly, full_dot(gram, poly))
    return mix


def kernel(
    init_hbm, vel_hbm, kappa_hbm, rate_hbm, basis_hbm,
    evolved_ref, mix_ref, carried_ref, image_ref,
    state, state_b, vel, kappa_ref, rate_ref, basis, halos, x_send, x_left, x_right, y_send, y_recv,
    pairs, outbox, own_t, part_box, part_sum, carry_box, carry_sum, proj, image_part, image_pair, image_own, gram_part, gram_sum, gram_all,
    load_sem, xs_sem, xr_sem, ys_sem, yr_sem, cs_sem, cr_sem, as_sem, ar_sem, gs_sem, gr_sem, is_sem, ir_sem, ps_sem, pr_sem, ms_sem, mr_sem, ts_sem, tr_sem,
):
    species = state.shape[0]
    ny = state.shape[2] - 16
    per = species // GROUPS
    ngx, ngy = lax.axis_size("gx"), lax.axis_size("gy")
    gx, gy = lax.axis_index("gx"), lax.axis_index("gy")
    right, left = lax.rem(gx + 1, ngx), lax.rem(gx + ngx - 1, ngx)
    north, south = lax.rem(gy + 1, ngy), lax.rem(gy + ngy - 1, ngy)
    core = lax.rem(gx, 2)
    half = ngx // 2
    chip = gx // 2
    sibling = gx + 1 - 2 * core
    own_lanes = pl.ds(pl.multiple_of(core * 128, 128), 128)
    own_slot = core * half
    pairs_per = per // 2
    lane = lax.broadcasted_iota(jnp.int32, (ny, 128), 1)
    pair = lane // 2

    def block(x):
        at = lax.rem(x, 2) * half + x // 2
        return pl.ds(pl.multiple_of(at * 128, 128), 128)

    def load_state(g):
        return pltpu.make_async_copy(
            init_hbm.at[pl.ds(g * per, per)],
            state.at[pl.ds(g * per, per), :, pl.ds(8, ny), :],
            load_sem.at[g],
        )

    load_vel = pltpu.make_async_copy(vel_hbm, vel, load_sem.at[GROUPS])
    load_kappa = pltpu.make_async_copy(kappa_hbm, kappa_ref, load_sem.at[GROUPS + 2])
    load_rate = pltpu.make_async_copy(rate_hbm, rate_ref, load_sem.at[GROUPS + 3])
    for g in range(GROUPS):
        load_state(g).start()
    load_kappa.start()
    load_rate.start()
    load_vel.start()

    barrier = pltpu.get_barrier_semaphore()

    @pl.loop(1, half)
    def _(d):
        peer = lax.rem(gx + 2 * d, ngx)
        pl.semaphore_signal(barrier, 1, device_id={"gx": peer}, device_id_type=MESH)

    for peer in (left, right):
        pl.semaphore_signal(barrier, 1, device_id={"gx": peer}, device_id_type=MESH)

    @pl.loop(1, ngy)
    def _(d):
        peer = lax.rem(gy + d, ngy)
        pl.semaphore_signal(barrier, 1, device_id={"gy": peer}, device_id_type=MESH)
        pl.semaphore_signal(barrier, 1, device_id={"gx": sibling, "gy": peer}, device_id_type=MESH)

    def x_copy(e, to_left):
        return pltpu.make_async_remote_copy(
            src_ref=x_send.at[e],
            dst_ref=(x_right if to_left else x_left).at[e],
            send_sem=xs_sem.at[int(to_left)],
            recv_sem=xr_sem.at[int(to_left), e],
            device_id={"gx": left if to_left else right},
            device_id_type=MESH,
        )

    def y_copy(e, to_south):
        d = int(to_south)
        return pltpu.make_async_remote_copy(
            src_ref=y_send.at[d, e],
            dst_ref=y_recv.at[d, e],
            send_sem=ys_sem.at[d],
            recv_sem=yr_sem.at[d, e],
            device_id={"gy": south if to_south else north},
            device_id_type=MESH,
        )

    def pair_copy(g):
        return pltpu.make_async_remote_copy(
            src_ref=outbox.at[pl.ds(g * pairs_per, pairs_per)],
            dst_ref=pairs.at[pl.ds(g * pairs_per, pairs_per), :, own_lanes],
            send_sem=cs_sem,
            recv_sem=cr_sem.at[g],
            device_id={"gx": sibling},
            device_id_type=MESH,
        )

    def part_copy(box, total, which, i):
        return pltpu.make_async_remote_copy(
            src_ref=box.at[i],
            dst_ref=total.at[chip],
            send_sem=as_sem.at[which],
            recv_sem=ar_sem.at[which, chip],
            device_id={"gx": 2 * i + core},
            device_id_type=MESH,
        )

    def send_parts(box, total, which, first, count, rows):
        cells = pairs[pl.ds(first, count)].reshape(count * pairs.shape[1], pairs.shape[2])
        parts = jnp.dot(cells, rows, preferred_element_type=F32).astype(BF16)
        box[pl.ds(first, count)] = parts.reshape(count, *box.shape[1:])

        @pl.loop(first, first + count)
        def _(i):
            @pl.when(i != chip)
            def _():
                part_copy(box, total, which, i).start()

    def summed(box, total, which):
        @pl.loop(1, half)
        def _(d):
            slot = lax.rem(chip + half - d, half)
            pltpu.make_async_copy(total.at[slot], total.at[slot], ar_sem.at[which, slot]).wait()

        total[chip] = box[chip]
        return tree_sum([total[i].astype(F32) for i in range(half)])

    def pack_edges(e, now, first):
        packed = jnp.zeros((ny, 128), F32)
        for f in range(2 * per):
            field = now.at[first + f // 2, f % 2]
            packed = jnp.where(pair == f, rolled(field[pl.ds(8, ny), :], 2 * f + 1), packed)
            y_send[0, e, pl.ds(f, 1), :] = field[pl.ds(7 + ny, 1), :]
            y_send[1, e, pl.ds(f, 1), :] = field[pl.ds(8, 1), :]
        x_send[e] = packed.astype(x_send.dtype)

    def send_edges(e):
        x_copy(e, True).start()
        x_copy(e, False).start()
        y_copy(e, True).start()
        y_copy(e, False).start()

    for g in range(GROUPS):
        load_state(g).wait()

    @pl.loop(0, GROUPS)
    def _(g):
        pack_edges(g, state, g * per)

    pl.semaphore_wait(barrier, half + 2 * ngy - 1)

    @pl.loop(0, GROUPS)
    def _(g):
        send_edges(g)

    basis_rows = pl.ds(pl.multiple_of(chip * 256, 256), 256)
    load_basis = pltpu.make_async_copy(basis_hbm.at[basis_rows], basis, load_sem.at[GROUPS + 1])
    load_basis.start()
    load_vel.wait()
    vel[...] = vel[...] * 0.5
    vel[2, 1] = -vel[2, 1]
    load_kappa.wait()
    load_rate.wait()

    def advance(k, g, now, new):
        e = k * GROUPS + g
        last = k == SECTIONS - 1
        x_copy(e, True).wait_recv()
        x_copy(e, False).wait_recv()
        y_copy(e, True).wait_recv()
        y_copy(e, False).wait_recv()

        wide = lax.broadcasted_iota(jnp.int32, halos.shape, 1)
        halos[...] = jnp.where(
            lax.rem(wide, 2) == 0,
            rolled(x_right[e].astype(F32), 127),
            rolled(x_left[e].astype(F32), 1),
        )

        for j in range(per):
            for z in range(2):
                now[g * per + j, z, pl.ds(7, 1), :] = y_recv[0, e, pl.ds(2 * j + z, 1), :]
                now[g * per + j, z, pl.ds(8 + ny, 1), :] = y_recv[1, e, pl.ds(2 * j + z, 1), :]

        @pl.loop(0, per, step=UNROLL)
        def _(j0):
            for i in range(UNROLL):
                j = j0 + (lax.rem(core + i, 2) if last else i)
                s = g * per + j
                kappa, rate = kappa_ref[s], rate_ref[s]
                middle = 1.0 - 6.0 * kappa - rate
                for z in range(2):
                    c = now[s, z, pl.ds(8, ny), :]
                    other = now[s, 1 - z, pl.ds(8, ny), :]
                    up = now[s, z, pl.ds(9, ny), :]
                    down = now[s, z, pl.ds(7, ny), :]
                    halo = rolled(halos[...], lax.rem(255 - 4 * j - 2 * z, 128))
                    east = jnp.where(lane == 127, halo, rolled(c, 127))
                    west = jnp.where(lane == 0, halo, rolled(c, 1))
                    result = (
                        c * (middle + rate * (1.0 / (1.0 + c * c)))
                        + kappa * ((east + west) + (up + down))
                        + (kappa - vel[2, z]) * other
                        - vel[0, z] * (east - west)
                        - vel[1, z] * (up - down)
                    )
                    if last:
                        evolved_ref[s, z] = result
                        cells = result.astype(BF16)
                        if i % 2 == 0:
                            pairs[s // 2, pl.ds(z * ny, ny), own_lanes] = cells
                        else:
                            outbox[s // 2, pl.ds(z * ny, ny), :] = cells
                    else:
                        new[s, z, pl.ds(8, ny), :] = result

        if not last:
            pack_edges(e + GROUPS, new, g * per)
            send_edges(e + GROUPS)

    buffers = (state, state_b)
    for k in range(SECTIONS - 1):

        @pl.loop(0, GROUPS)
        def _(g):
            advance(k, g, buffers[k % 2], buffers[(k + 1) % 2])

    load_basis.wait()

    def group_parts(g):
        pair_copy(g).wait_recv()
        send_parts(part_box, part_sum, 0, g * pairs_per, pairs_per, basis[...])

    @pl.loop(0, GROUPS)
    def _(g):
        advance(SECTIONS - 1, g, buffers[(SECTIONS - 1) % 2], None)
        pair_copy(g).start()

        @pl.when(g > 0)
        def _():
            group_parts(g - 1)

    group_parts(GROUPS - 1)

    def turned(at, cells):
        own_t[:, pl.ds(pl.multiple_of(at * 128, 128), 128)] = cells.T

    @pl.loop(0, half, step=2)
    def _(i):
        for k in range(2):
            turned(own_slot + i + k, pairs[i + k, :, own_lanes])
            turned(half - own_slot + i + k, outbox[i + k])

    proj[block(gx), :] = summed(part_box, part_sum, 0).astype(BF16)

    stride_a = 2 + 6 * core
    stride_b = 8 - 6 * core
    pos_a = lax.rem(gx // stride_a, 4)
    pos_b = lax.rem(gx // stride_b, 4)

    def device_at(a, b):
        return lax.rem(a, 4) * stride_a + lax.rem(b, 4) * stride_b + core

    def gather(held, use):
        def send(x, peer):
            pltpu.make_async_remote_copy(
                src_ref=held.at[block(x)],
                dst_ref=held.at[block(x)],
                send_sem=gs_sem,
                recv_sem=gr_sem.at[x],
                device_id={"gx": peer},
                device_id_type=MESH,
            ).start()

        def arrival(x):
            pltpu.make_async_copy(held.at[block(x)], held.at[block(x)], gr_sem.at[x]).wait()

        order = (1, 3, 2)
        for d in order:
            send(gx, device_at(pos_a + d, pos_b))
        for d in order:
            send(gx, device_at(pos_a, pos_b + d))
        send(gx, sibling)
        for d in order:
            x = device_at(pos_a + d, pos_b)
            arrival(x)
            for f in order:
                send(x, device_at(pos_a, pos_b + f))
            send(x, sibling)
        for d in (0, 1, 3, 2):
            for f in order:
                x = device_at(pos_a + d, pos_b + f)
                arrival(x)
                send(x, sibling)
        first = use(core)

        @pl.loop(0, half)
        def _(i):
            arrival(2 * i + 1 - core)

        second = use(1 - core)
        return first + second

    def gather_done(held):
        part = held.at[pl.ds(0, (ngx - 1) * 128)]
        pltpu.make_async_copy(part, part, gs_sem).wait()

    def span(c):
        return pl.ds(pl.multiple_of(c * (half * 128), half * 128), half * 128)

    part = gather(
        proj, lambda c: jnp.dot(own_t[:, span(c)], proj[span(c), :], preferred_element_type=F32)
    )

    image_part[gy] = part.astype(BF16)

    def image_copy(d):
        return pltpu.make_async_remote_copy(
            src_ref=image_part.at[gy],
            dst_ref=image_part.at[gy],
            send_sem=is_sem.at[d],
            recv_sem=ir_sem.at[gy],
            device_id={"gy": lax.rem(gy + d, ngy)},
            device_id_type=MESH,
        )

    for d in (1, 3, 2):
        image_copy(d).start()
    for d in (1, 3, 2):
        slot = lax.rem(gy + d, ngy)
        pltpu.make_async_copy(image_part.at[slot], image_part.at[slot], ir_sem.at[slot]).wait()
    image_own[...] = (image_part[0].astype(F32) + image_part[1].astype(F32)) + (
        image_part[2].astype(F32) + image_part[3].astype(F32)
    )
    image_pair[core] = image_own[...].astype(BF16)

    pair_image_copy = pltpu.make_async_remote_copy(
        src_ref=image_pair.at[core],
        dst_ref=image_pair.at[core],
        send_sem=ps_sem,
        recv_sem=pr_sem,
        device_id={"gx": sibling},
        device_id_type=MESH,
    )
    pair_image_copy.start()
    pair_image_copy.wait_recv()
    both = jnp.concatenate([image_pair[0], image_pair[1]], axis=0)

    gram_part[...] = lax.dot_general(both, both, (((0,), (0,)), ((), ())), preferred_element_type=F32)
    def share(y, c):
        return pl.ds(pl.multiple_of(y * 32 + c * 16, 16), 16)

    own_share = share(gy, core)
    gram_sum[chip] = gram_part[own_share, :]

    def gram_copy(d):
        return pltpu.make_async_remote_copy(
            src_ref=gram_part.at[own_share],
            dst_ref=gram_sum.at[chip],
            send_sem=ms_sem,
            recv_sem=mr_sem.at[chip],
            device_id={"gx": lax.rem(gx + 2 * d, ngx)},
            device_id_type=MESH,
        )

    @pl.loop(1, half)
    def _(d):
        gram_copy(d).start()

    @pl.loop(0, half, step=8)
    def _(i):
        send_parts(carry_box, carry_sum, 1, i, 8, both)

    @pl.loop(1, half)
    def _(d):
        slot = lax.rem(chip + half - d, half)
        pltpu.make_async_copy(gram_sum.at[slot], gram_sum.at[slot], mr_sem.at[slot]).wait()

    gram_all[own_share, :] = tree_sum([gram_sum[i] for i in range(half)])

    def rows_copy(d, c):
        return pltpu.make_async_remote_copy(
            src_ref=gram_all.at[own_share],
            dst_ref=gram_all.at[own_share],
            send_sem=ts_sem.at[d, c],
            recv_sem=tr_sem.at[gy, core],
            device_id={"gx": 2 * chip + lax.rem(core + c, 2), "gy": lax.rem(gy + d, ngy)},
            device_id_type=MESH,
        )

    others = ((1, 0), (3, 0), (2, 0), (0, 1), (1, 1), (3, 1), (2, 1))
    for d, c in others:
        rows_copy(d, c).start()
    for d, c in others:
        y, x = lax.rem(gy + d, ngy), lax.rem(core + c, 2)
        rows = gram_all.at[share(y, x)]
        pltpu.make_async_copy(rows, rows, tr_sem.at[y, x]).wait()

    mix_ref[...] = mixing(gram_all[...], 128.0 * ngx)
    carried_ref[...] = summed(carry_box, carry_sum, 1)
    image_ref[...] = image_own[pl.ds(pl.multiple_of(gy * 32, 32), 32), :]

    for d in range(2):
        pltpu.make_async_copy(x_send, x_send, xs_sem.at[d]).wait()
        pltpu.make_async_copy(y_send.at[d], y_send.at[d], ys_sem.at[d]).wait()
    pltpu.make_async_copy(outbox, outbox, cs_sem).wait()
    for which in range(2):
        sent = part_box.at[pl.ds(0, half - 1)]
        pltpu.make_async_copy(sent, sent, as_sem.at[which]).wait()
    gather_done(proj)
    pair_image_copy.wait_send()
    sent = gram_sum.at[pl.ds(0, half - 1)]
    pltpu.make_async_copy(sent, sent, ms_sem).wait()
    for d, c in others:
        rows_copy(d, c).wait_send()
    for d in (1, 3, 2):
        image_copy(d).wait_send()


def finish(scale, evolved_ref, mix_ref, carried_ref, image_ref, out_hbm, factor_ref, core_ref, sem):
    writing = pltpu.make_async_copy(evolved_ref, out_hbm, sem)
    writing.start()
    mix = mix_ref[...]
    factor_ref[...] = full_dot(image_ref[...], mix).astype(BF16)
    result = full_dot(carried_ref[...], mix) * scale
    ny = core_ref.shape[2]
    core_ref[0, 0] = result[:ny]
    core_ref[0, 1] = result[ny:]
    writing.wait()


def shards(initial_state, velocity, diffusivity, reaction_rate, start_basis):
    species, nz, ny, nx = initial_state.shape
    ngx, ngy = lax.axis_size("gx"), lax.axis_size("gy")
    rank = start_basis.shape[1]
    operands = (initial_state, velocity, diffusivity, reaction_rate, start_basis)
    exchanges = SECTIONS * GROUPS
    rows = 2 * species // GROUPS
    hbm = pl.BlockSpec(memory_space=pltpu.HBM)
    vmem = pl.BlockSpec(memory_space=pltpu.VMEM)
    dma = pltpu.SemaphoreType.DMA
    evolved, mix, carried, image = pl.pallas_call(
        kernel,
        out_shape=(
            jax.ShapeDtypeStruct(initial_state.shape, F32),
            jax.ShapeDtypeStruct((rank, rank), F32),
            jax.ShapeDtypeStruct((nz * ny, rank), F32),
            jax.ShapeDtypeStruct((nx // ngy, rank), F32),
        ),
        in_specs=[hbm] * 5,
        out_specs=(vmem,) * 4,
        scratch_shapes=[
            pltpu.VMEM((species, nz, ny + 16, nx), F32),
            pltpu.VMEM((species, nz, ny + 16, nx), F32),
            pltpu.VMEM((3, nz, ny, nx), F32),
            pltpu.SMEM((species,), F32),
            pltpu.SMEM((species,), F32),
            pltpu.VMEM((2 * nx, rank), BF16),
            pltpu.VMEM((ny, nx), F32),
            pltpu.VMEM((exchanges, ny, nx), BF16),
            pltpu.VMEM((exchanges, ny, nx), BF16),
            pltpu.VMEM((exchanges, ny, nx), BF16),
            pltpu.VMEM((2, exchanges, rows, nx), F32),
            pltpu.VMEM((2, exchanges, rows, nx), F32),
            pltpu.VMEM((species // 2, nz * ny, 2 * nx), BF16),
            pltpu.VMEM((species // 2, nz * ny, nx), BF16),
            pltpu.VMEM((nx, species * nz * ny), BF16),
            pltpu.VMEM((ngx // 2, nz * ny, rank), BF16),
            pltpu.VMEM((ngx // 2, nz * ny, rank), BF16),
            pltpu.VMEM((ngx // 2, nz * ny, rank), BF16),
            pltpu.VMEM((ngx // 2, nz * ny, rank), BF16),
            pltpu.VMEM((species * nz * ny, rank), BF16),
            pltpu.VMEM((ngy, nx, rank), BF16),
            pltpu.VMEM((2, nx, rank), BF16),
            pltpu.VMEM((nx, rank), F32),
            pltpu.VMEM((rank, rank), F32),
            pltpu.VMEM((ngx // 2, rank // (2 * ngy), rank), F32),
            pltpu.VMEM((rank, rank), F32),
            dma((GROUPS + 4,)),
            dma((2,)),
            dma((2, exchanges)),
            dma((2,)),
            dma((2, exchanges)),
            dma,
            dma((GROUPS,)),
            dma((2,)),
            dma((2, ngx // 2)),
            dma,
            dma((ngx,)),
            dma((ngy,)),
            dma((ngy,)),
            dma,
            dma,
            dma,
            dma((ngx // 2,)),
            dma((ngy, 2)),
            dma((ngy, 2)),
        ],
        compiler_params=pltpu.CompilerParams(
            collective_id=0, has_side_effects=True, vmem_limit_bytes=VMEM_LIMIT
        ),
    )(*(pltpu.with_memory_space_constraint(x, pltpu.HBM) for x in operands))
    return pl.pallas_call(
        functools.partial(finish, float(nx * ngx) ** -0.5),
        out_shape=(
            jax.ShapeDtypeStruct(initial_state.shape, F32),
            jax.ShapeDtypeStruct((nx // ngy, rank), BF16),
            jax.ShapeDtypeStruct((1, nz, ny, rank), F32),
        ),
        in_specs=[pl.BlockSpec(memory_space=pl.ANY), vmem, vmem, vmem],
        out_specs=(hbm, vmem, vmem),
        scratch_shapes=[dma],
        compiler_params=pltpu.CompilerParams(vmem_limit_bytes=8 << 20),
    )(evolved, mix, carried, image)


def solution(mesh):
    return jax.shard_map(
        shards,
        mesh=mesh,
        in_specs=(P(None, None, "gy", "gx"), P(None, None, "gy", "gx"), P(), P(), P()),
        out_specs=(P(None, None, "gy", "gx"), P(("gx", "gy"), None), P("gx", None, "gy", None)),
        check_vma=False,
    )
```

```python
import functools

import jax
import jax.numpy as jnp
from jax import lax
from jax.experimental import pallas as pl
from jax.experimental.pallas import tpu as pltpu
from jax.sharding import PartitionSpec as P

SECTIONS = 4
NS_STEPS = 5
GROUPS = 4
UNROLL = 2
VMEM_LIMIT = 32 << 20
MESH = pl.DeviceIdType.MESH
F32 = jnp.float32
BF16 = jnp.bfloat16


def rolled(x, shift):
    return pltpu.roll(x, shift, 1)


def halves(x):
    high = x.astype(BF16)
    return high, (x - high.astype(F32)).astype(BF16)


def full_dot(a, b):
    a_high, a_low = halves(a)
    b_high, b_low = halves(b)
    return jnp.dot(
        jnp.concatenate([a_high, a_high, a_low], axis=1),
        jnp.concatenate([b_high, b_low, b_high], axis=0),
        preferred_element_type=F32,
    )


def tree_sum(terms):
    while len(terms) > 1:
        terms = [a + b for a, b in zip(terms[::2], terms[1::2])]
    return terms[0]


def mixing(gram, count):
    row = lax.broadcasted_iota(jnp.int32, gram.shape, 0)
    column = lax.broadcasted_iota(jnp.int32, gram.shape, 1)
    identity = jnp.where(row == column, 1.0, 0.0).astype(F32)
    trace = jnp.sum(gram * identity, keepdims=True)
    squared = count / (trace + 1e-6)
    gram = gram * (squared / count)
    mix = jnp.sqrt(squared) * identity
    for step in range(NS_STEPS):
        poly = 1.5 * identity - 0.5 * gram
        mix = full_dot(mix, poly)
        if step < NS_STEPS - 1:
            gram = full_dot(poly, full_dot(gram, poly))
    return mix


def kernel(
    init_hbm, vel_hbm, kappa_hbm, rate_hbm, basis_hbm,
    evolved_ref, mix_ref, carried_ref, image_ref,
    state, state_b, vel, kappa_ref, rate_ref, basis, halos, x_send, x_recv, y_send, y_recv,
    pairs, outbox, pairs_t, part_box, part_sum, carry_box, carry_sum, proj, half_send, half_recv, image_part, image_pair, image_own, gram_part, gram_sum, gram_all,
    load_sem, xs_sem, xr_sem, ys_sem, yr_sem, cs_sem, cr_sem, as_sem, ar_sem, gs_sem, gr_sem, is_sem, ir_sem, hs_sem, hr_sem, ps_sem, pr_sem, ms_sem, mr_sem, ts_sem, tr_sem,
):
    species = state.shape[0]
    ny = state.shape[2] - 16
    per = species // GROUPS
    ngx, ngy = lax.axis_size("gx"), lax.axis_size("gy")
    gx, gy = lax.axis_index("gx"), lax.axis_index("gy")
    right, left = lax.rem(gx + 1, ngx), lax.rem(gx + ngx - 1, ngx)
    north, south = lax.rem(gy + 1, ngy), lax.rem(gy + ngy - 1, ngy)
    core = lax.rem(gx, 2)
    half = ngx // 2
    chip = gx // 2
    sibling = gx + 1 - 2 * core
    own_lanes = pl.ds(pl.multiple_of(core * 128, 128), 128)
    pairs_per = per // 2
    lane = lax.broadcasted_iota(jnp.int32, (ny, 128), 1)
    pair = lane // 2

    load_state = pltpu.make_async_copy(init_hbm, state.at[:, :, pl.ds(8, ny), :], load_sem.at[0])
    load_vel = pltpu.make_async_copy(vel_hbm, vel, load_sem.at[1])
    load_kappa = pltpu.make_async_copy(kappa_hbm, kappa_ref, load_sem.at[2])
    load_rate = pltpu.make_async_copy(rate_hbm, rate_ref, load_sem.at[3])
    load_state.start()
    load_kappa.start()
    load_rate.start()
    load_vel.start()

    barrier = pltpu.get_barrier_semaphore()

    @pl.loop(1, half)
    def _(d):
        peer = lax.rem(gx + 2 * d, ngx)
        pl.semaphore_signal(barrier, 1, device_id={"gx": peer}, device_id_type=MESH)

    for peer in (left, right):
        pl.semaphore_signal(barrier, 1, device_id={"gx": peer}, device_id_type=MESH)

    @pl.loop(1, ngy)
    def _(d):
        peer = lax.rem(gy + d, ngy)
        pl.semaphore_signal(barrier, 1, device_id={"gy": peer}, device_id_type=MESH)
        pl.semaphore_signal(barrier, 1, device_id={"gx": sibling, "gy": peer}, device_id_type=MESH)

    def x_copy(e, to_left):
        return pltpu.make_async_remote_copy(
            src_ref=x_send.at[e],
            dst_ref=x_recv.at[e, int(to_left)],
            send_sem=xs_sem.at[int(to_left)],
            recv_sem=xr_sem.at[e],
            device_id={"gx": left if to_left else right},
            device_id_type=MESH,
        )

    def y_copy(e, to_south):
        d = int(to_south)
        return pltpu.make_async_remote_copy(
            src_ref=y_send.at[d, e],
            dst_ref=y_recv.at[e, d],
            send_sem=ys_sem.at[d],
            recv_sem=yr_sem.at[e],
            device_id={"gy": south if to_south else north},
            device_id_type=MESH,
        )

    def pair_copy(g):
        return pltpu.make_async_remote_copy(
            src_ref=outbox.at[pl.ds(g * pairs_per, pairs_per)],
            dst_ref=pairs.at[pl.ds(g * pairs_per, pairs_per), :, own_lanes],
            send_sem=cs_sem,
            recv_sem=cr_sem.at[g],
            device_id={"gx": sibling},
            device_id_type=MESH,
        )

    def part_copy(box, total, which, i):
        return pltpu.make_async_remote_copy(
            src_ref=box.at[i],
            dst_ref=total.at[chip],
            send_sem=as_sem.at[which],
            recv_sem=ar_sem.at[which],
            device_id={"gx": 2 * i + core},
            device_id_type=MESH,
        )

    def send_parts(box, total, which, first, count, rows):
        cells = pairs[pl.ds(first, count)].reshape(count * pairs.shape[1], pairs.shape[2])
        parts = jnp.dot(cells, rows, preferred_element_type=F32).astype(BF16)
        box[pl.ds(first, count)] = parts.reshape(count, *box.shape[1:])

        @pl.loop(first, first + count)
        def _(i):
            @pl.when(i != chip)
            def _():
                part_copy(box, total, which, i).start()

    def all_of(ref, count):
        return ref.at[pl.ds(0, count)]

    def summed(box, total, which):
        arrived = all_of(total, half - 1)
        pltpu.make_async_copy(arrived, arrived, ar_sem.at[which]).wait()
        total[chip] = box[chip]
        return tree_sum([total[i].astype(F32) for i in range(half)])

    def pack_edges(e, now, first):
        packed = jnp.zeros((ny, 128), F32)
        for f in range(2 * per):
            field = now.at[first + f // 2, f % 2]
            packed = jnp.where(pair == f, rolled(field[pl.ds(8, ny), :], 2 * f + 1), packed)
            y_send[0, e, pl.ds(f, 1), :] = field[pl.ds(7 + ny, 1), :]
            y_send[1, e, pl.ds(f, 1), :] = field[pl.ds(8, 1), :]
        x_send[e] = packed.astype(x_send.dtype)

    def send_edges(e):
        x_copy(e, True).start()
        x_copy(e, False).start()
        y_copy(e, True).start()
        y_copy(e, False).start()

    load_state.wait()

    @pl.loop(0, GROUPS)
    def _(g):
        pack_edges(g, state, g * per)

    pl.semaphore_wait(barrier, half + 2 * ngy - 1)

    @pl.loop(0, GROUPS)
    def _(g):
        send_edges(g)

    basis_rows = pl.ds(pl.multiple_of(chip * 256, 256), 256)
    load_basis = pltpu.make_async_copy(basis_hbm.at[basis_rows], basis, load_sem.at[4])
    load_basis.start()
    load_vel.wait()
    vel[...] = vel[...] * 0.5
    vel[2, 1] = -vel[2, 1]
    load_kappa.wait()
    load_rate.wait()

    def advance(k, g, now, new):
        e = k * GROUPS + g
        last = k == SECTIONS - 1
        pltpu.make_async_copy(x_recv.at[e], x_recv.at[e], xr_sem.at[e]).wait()
        pltpu.make_async_copy(y_recv.at[e], y_recv.at[e], yr_sem.at[e]).wait()

        wide = lax.broadcasted_iota(jnp.int32, halos.shape, 1)
        halos[...] = jnp.where(
            lax.rem(wide, 2) == 0,
            rolled(x_recv[e, 1].astype(F32), 127),
            rolled(x_recv[e, 0].astype(F32), 1),
        )

        for j in range(per):
            for z in range(2):
                now[g * per + j, z, pl.ds(7, 1), :] = y_recv[e, 0, pl.ds(2 * j + z, 1), :]
                now[g * per + j, z, pl.ds(8 + ny, 1), :] = y_recv[e, 1, pl.ds(2 * j + z, 1), :]

        @pl.loop(0, per, step=UNROLL)
        def _(j0):
            for i in range(UNROLL):
                j = j0 + (lax.rem(core + i, 2) if last else i)
                s = g * per + j
                kappa, rate = kappa_ref[s], rate_ref[s]
                middle = 1.0 - 6.0 * kappa - rate
                for z in range(2):
                    c = now[s, z, pl.ds(8, ny), :]
                    other = now[s, 1 - z, pl.ds(8, ny), :]
                    up = now[s, z, pl.ds(9, ny), :]
                    down = now[s, z, pl.ds(7, ny), :]
                    halo = rolled(halos[...], lax.rem(255 - 4 * j - 2 * z, 128))
                    east = jnp.where(lane == 127, halo, rolled(c, 127))
                    west = jnp.where(lane == 0, halo, rolled(c, 1))
                    result = (
                        c * (middle + rate * (1.0 / (1.0 + c * c)))
                        + kappa * ((east + west) + (up + down))
                        + (kappa - vel[2, z]) * other
                        - vel[0, z] * (east - west)
                        - vel[1, z] * (up - down)
                    )
                    if last:
                        evolved_ref[s, z] = result
                        cells = result.astype(BF16)
                        if i % 2 == 0:
                            pairs[s // 2, pl.ds(z * ny, ny), own_lanes] = cells
                        else:
                            outbox[s // 2, pl.ds(z * ny, ny), :] = cells
                    else:
                        new[s, z, pl.ds(8, ny), :] = result

        if not last:
            pack_edges(e + GROUPS, new, g * per)
            send_edges(e + GROUPS)

    buffers = (state, state_b)
    for k in range(SECTIONS - 1):

        @pl.loop(0, GROUPS)
        def _(g):
            advance(k, g, buffers[k % 2], buffers[(k + 1) % 2])

    load_basis.wait()

    def group_parts(g):
        pair_copy(g).wait_recv()
        send_parts(part_box, part_sum, 0, g * pairs_per, pairs_per, basis[...])

    @pl.loop(0, GROUPS)
    def _(g):
        advance(SECTIONS - 1, g, buffers[(SECTIONS - 1) % 2], None)
        pair_copy(g).start()

        @pl.when(g > 0)
        def _():
            group_parts(g - 1)

    group_parts(GROUPS - 1)

    @pl.loop(0, half, step=2)
    def _(i):
        for k in range(2):
            pairs_t[:, pl.ds(pl.multiple_of((i + k) * 128, 128), 128)] = pairs[i + k].T

    def block(x):
        return pl.ds(pl.multiple_of(x // 2 * 128, 128), 128)

    plane = gx // per
    across = pairs_per

    def in_plane(x, d):
        return x // per * per + lax.rem(x + 2 * d, per)

    def other_plane(x, d):
        return lax.rem(x + d * per, ngx)

    def send(x, peer):
        pltpu.make_async_remote_copy(
            src_ref=proj.at[block(x)],
            dst_ref=proj.at[block(x)],
            send_sem=gs_sem,
            recv_sem=gr_sem.at[x // 2],
            device_id={"gx": peer},
            device_id_type=MESH,
        ).start()

    def arrival(x):
        pltpu.make_async_copy(proj.at[block(x)], proj.at[block(x)], gr_sem.at[x // 2]).wait()

    order = (1, 3, 2)

    @pl.loop(0, GROUPS)
    def _(p):
        @pl.when(p == plane)
        def _():
            proj[block(gx), :] = summed(part_box, part_sum, 0).astype(BF16)

            @pl.when(core == 0)
            def _():
                for d in order:
                    send(gx, in_plane(gx, d))
                for d in order:
                    send(gx, other_plane(gx, d))

            @pl.when(core == 1)
            def _():
                for d in order:
                    send(gx, other_plane(gx, d))
                for d in order:
                    send(gx, in_plane(gx, d))

        @pl.when((p != plane) & (core == 1))
        def _():
            x = p * per + lax.rem(gx, per)
            arrival(x)
            for d in order:
                send(x, in_plane(gx, d))

    @pl.when(core == 0)
    def _():
        for d in order:
            x = in_plane(gx, d)
            arrival(x)
            for f in order:
                send(x, other_plane(gx, f))
        for f in order:
            for d in range(across):
                arrival(in_plane(other_plane(gx, f), d))

    @pl.when(core == 1)
    def _():
        for d in order:
            for f in range(GROUPS):
                arrival(other_plane(in_plane(gx, d), f))

    def image_half(c):
        rows = pl.ds(pl.multiple_of(c * 128, 128), 128)
        return jnp.dot(pairs_t[rows, :], proj[...], preferred_element_type=F32)

    half_send[...] = image_half(1 - core).astype(BF16)
    half_copy = pltpu.make_async_remote_copy(
        src_ref=half_send,
        dst_ref=half_recv,
        send_sem=hs_sem,
        recv_sem=hr_sem,
        device_id={"gx": sibling},
        device_id_type=MESH,
    )
    half_copy.start()
    part = image_half(core)
    half_copy.wait_recv()
    part = part + half_recv[...].astype(F32)

    image_part[gy] = part.astype(BF16)

    def image_copy(d):
        return pltpu.make_async_remote_copy(
            src_ref=image_part.at[gy],
            dst_ref=image_part.at[gy],
            send_sem=is_sem,
            recv_sem=ir_sem,
            device_id={"gy": lax.rem(gy + d, ngy)},
            device_id_type=MESH,
        )

    for d in (1, 3, 2):
        image_copy(d).start()
    arrived = all_of(image_part, ngy - 1)
    pltpu.make_async_copy(arrived, arrived, ir_sem).wait()
    image_own[...] = (image_part[0].astype(F32) + image_part[1].astype(F32)) + (
        image_part[2].astype(F32) + image_part[3].astype(F32)
    )
    image_pair[core] = image_own[...].astype(BF16)

    pair_image_copy = pltpu.make_async_remote_copy(
        src_ref=image_pair.at[core],
        dst_ref=image_pair.at[core],
        send_sem=ps_sem,
        recv_sem=pr_sem,
        device_id={"gx": sibling},
        device_id_type=MESH,
    )
    pair_image_copy.start()
    pair_image_copy.wait_recv()
    both = jnp.concatenate([image_pair[0], image_pair[1]], axis=0)

    gram_part[...] = lax.dot_general(both, both, (((0,), (0,)), ((), ())), preferred_element_type=F32)
    def share(y, c):
        return pl.ds(pl.multiple_of(y * 32 + c * 16, 16), 16)

    own_share = share(gy, core)
    gram_sum[chip] = gram_part[own_share, :]

    def gram_copy(d):
        return pltpu.make_async_remote_copy(
            src_ref=gram_part.at[own_share],
            dst_ref=gram_sum.at[chip],
            send_sem=ms_sem,
            recv_sem=mr_sem,
            device_id={"gx": lax.rem(gx + 2 * d, ngx)},
            device_id_type=MESH,
        )

    @pl.loop(1, half)
    def _(d):
        gram_copy(d).start()

    @pl.loop(0, half, step=8)
    def _(i):
        send_parts(carry_box, carry_sum, 1, i, 8, both)

    arrived = all_of(gram_sum, half - 1)
    pltpu.make_async_copy(arrived, arrived, mr_sem).wait()

    gram_all[own_share, :] = tree_sum([gram_sum[i] for i in range(half)])

    def rows_copy(d, c):
        return pltpu.make_async_remote_copy(
            src_ref=gram_all.at[own_share],
            dst_ref=gram_all.at[own_share],
            send_sem=ts_sem,
            recv_sem=tr_sem,
            device_id={"gx": 2 * chip + lax.rem(core + c, 2), "gy": lax.rem(gy + d, ngy)},
            device_id_type=MESH,
        )

    others = ((1, 0), (3, 0), (2, 0), (0, 1), (1, 1), (3, 1), (2, 1))
    for d, c in others:
        rows_copy(d, c).start()
    arrived = all_of(gram_all, 16 * len(others))
    pltpu.make_async_copy(arrived, arrived, tr_sem).wait()

    mix_ref[...] = mixing(gram_all[...], 128.0 * ngx)
    carried_ref[...] = summed(carry_box, carry_sum, 1)
    image_ref[...] = image_own[pl.ds(pl.multiple_of(gy * 32, 32), 32), :]

    for d in range(2):
        pltpu.make_async_copy(x_send, x_send, xs_sem.at[d]).wait()
        pltpu.make_async_copy(y_send.at[d], y_send.at[d], ys_sem.at[d]).wait()
    pltpu.make_async_copy(outbox, outbox, cs_sem).wait()
    for which in range(2):
        sent = part_box.at[pl.ds(0, half - 1)]
        pltpu.make_async_copy(sent, sent, as_sem.at[which]).wait()
    sent = all_of(proj, (half - 1) * 128)
    pltpu.make_async_copy(sent, sent, gs_sem).wait()
    half_copy.wait_send()
    pair_image_copy.wait_send()
    sent = gram_sum.at[pl.ds(0, half - 1)]
    pltpu.make_async_copy(sent, sent, ms_sem).wait()
    sent = all_of(gram_all, 16 * len(others))
    pltpu.make_async_copy(sent, sent, ts_sem).wait()
    sent = all_of(image_part, ngy - 1)
    pltpu.make_async_copy(sent, sent, is_sem).wait()


def finish(scale, evolved_ref, mix_ref, carried_ref, image_ref, out_hbm, factor_ref, core_ref, sem):
    writing = pltpu.make_async_copy(evolved_ref, out_hbm, sem)
    writing.start()
    mix = mix_ref[...]
    factor_ref[...] = full_dot(image_ref[...], mix).astype(BF16)
    result = full_dot(carried_ref[...], mix) * scale
    ny = core_ref.shape[2]
    core_ref[0, 0] = result[:ny]
    core_ref[0, 1] = result[ny:]
    writing.wait()


def shards(initial_state, velocity, diffusivity, reaction_rate, start_basis):
    species, nz, ny, nx = initial_state.shape
    ngx, ngy = lax.axis_size("gx"), lax.axis_size("gy")
    rank = start_basis.shape[1]
    operands = (initial_state, velocity, diffusivity, reaction_rate, start_basis)
    exchanges = SECTIONS * GROUPS
    rows = 2 * species // GROUPS
    hbm = pl.BlockSpec(memory_space=pltpu.HBM)
    vmem = pl.BlockSpec(memory_space=pltpu.VMEM)
    dma = pltpu.SemaphoreType.DMA
    evolved, mix, carried, image = pl.pallas_call(
        kernel,
        out_shape=(
            jax.ShapeDtypeStruct(initial_state.shape, F32),
            jax.ShapeDtypeStruct((rank, rank), F32),
            jax.ShapeDtypeStruct((nz * ny, rank), F32),
            jax.ShapeDtypeStruct((nx // ngy, rank), F32),
        ),
        in_specs=[hbm] * 5,
        out_specs=(vmem,) * 4,
        scratch_shapes=[
            pltpu.VMEM((species, nz, ny + 16, nx), F32),
            pltpu.VMEM((species, nz, ny + 16, nx), F32),
            pltpu.VMEM((3, nz, ny, nx), F32),
            pltpu.SMEM((species,), F32),
            pltpu.SMEM((species,), F32),
            pltpu.VMEM((2 * nx, rank), BF16),
            pltpu.VMEM((ny, nx), F32),
            pltpu.VMEM((exchanges, ny, nx), BF16),
            pltpu.VMEM((exchanges, 2, ny, nx), BF16),
            pltpu.VMEM((2, exchanges, rows, nx), F32),
            pltpu.VMEM((exchanges, 2, rows, nx), F32),
            pltpu.VMEM((species // 2, nz * ny, 2 * nx), BF16),
            pltpu.VMEM((species // 2, nz * ny, nx), BF16),
            pltpu.VMEM((2 * nx, species // 2 * nz * ny), BF16),
            pltpu.VMEM((ngx // 2, nz * ny, rank), BF16),
            pltpu.VMEM((ngx // 2, nz * ny, rank), BF16),
            pltpu.VMEM((ngx // 2, nz * ny, rank), BF16),
            pltpu.VMEM((ngx // 2, nz * ny, rank), BF16),
            pltpu.VMEM((species // 2 * nz * ny, rank), BF16),
            pltpu.VMEM((nx, rank), BF16),
            pltpu.VMEM((nx, rank), BF16),
            pltpu.VMEM((ngy, nx, rank), BF16),
            pltpu.VMEM((2, nx, rank), BF16),
            pltpu.VMEM((nx, rank), F32),
            pltpu.VMEM((rank, rank), F32),
            pltpu.VMEM((ngx // 2, rank // (2 * ngy), rank), F32),
            pltpu.VMEM((rank, rank), F32),
            dma((5,)),
            dma((2,)),
            dma((exchanges,)),
            dma((2,)),
            dma((exchanges,)),
            dma,
            dma((GROUPS,)),
            dma((2,)),
            dma((2,)),
            dma,
            dma((ngx // 2,)),
            dma,
            dma,
            dma,
            dma,
            dma,
            dma,
            dma,
            dma,
            dma,
            dma,
        ],
        compiler_params=pltpu.CompilerParams(
            collective_id=0, has_side_effects=True, vmem_limit_bytes=VMEM_LIMIT
        ),
    )(*(pltpu.with_memory_space_constraint(x, pltpu.HBM) for x in operands))
    return pl.pallas_call(
        functools.partial(finish, float(nx * ngx) ** -0.5),
        out_shape=(
            jax.ShapeDtypeStruct(initial_state.shape, F32),
            jax.ShapeDtypeStruct((nx // ngy, rank), BF16),
            jax.ShapeDtypeStruct((1, nz, ny, rank), F32),
        ),
        in_specs=[pl.BlockSpec(memory_space=pl.ANY), vmem, vmem, vmem],
        out_specs=(hbm, vmem, vmem),
        scratch_shapes=[dma],
        compiler_params=pltpu.CompilerParams(vmem_limit_bytes=8 << 20),
    )(evolved, mix, carried, image)


def solution(mesh):
    return jax.shard_map(
        shards,
        mesh=mesh,
        in_specs=(P(None, None, "gy", "gx"), P(None, None, "gy", "gx"), P(), P(), P()),
        out_specs=(P(None, None, "gy", "gx"), P(("gx", "gy"), None), P("gx", None, "gy", None)),
        check_vma=False,
    )
```

```python
import functools

import jax
import jax.numpy as jnp
from jax import lax
from jax.experimental import pallas as pl
from jax.experimental.pallas import tpu as pltpu
from jax.sharding import PartitionSpec as P

SECTIONS = 4
NS_STEPS = 5
GROUPS = 4
UNROLL = 2
VMEM_LIMIT = 32 << 20
MESH = pl.DeviceIdType.MESH
F32 = jnp.float32
BF16 = jnp.bfloat16


def rolled(x, shift):
    return pltpu.roll(x, shift, 1)


def halves(x):
    high = x.astype(BF16)
    return high, (x - high.astype(F32)).astype(BF16)


def full_dot(a, b):
    a_high, a_low = halves(a)
    b_high, b_low = halves(b)
    return jnp.dot(
        jnp.concatenate([a_high, a_high, a_low], axis=1),
        jnp.concatenate([b_high, b_low, b_high], axis=0),
        preferred_element_type=F32,
    )


def tree_sum(terms):
    while len(terms) > 1:
        terms = [a + b for a, b in zip(terms[::2], terms[1::2])]
    return terms[0]


def mixing(gram, count):
    row = lax.broadcasted_iota(jnp.int32, gram.shape, 0)
    column = lax.broadcasted_iota(jnp.int32, gram.shape, 1)
    identity = jnp.where(row == column, 1.0, 0.0).astype(F32)
    trace = jnp.sum(gram * identity, keepdims=True)
    squared = count / (trace + 1e-6)
    gram = gram * (squared / count)
    mix = jnp.sqrt(squared) * identity
    for step in range(NS_STEPS):
        poly = 1.5 * identity - 0.5 * gram
        mix = full_dot(mix, poly)
        if step < NS_STEPS - 1:
            gram = full_dot(poly, full_dot(gram, poly))
    return mix


def kernel(
    init_hbm, vel_hbm, kappa_hbm, rate_hbm, basis_hbm,
    evolved_ref, gram_ref, carried_ref, image_ref,
    state, state_b, vel, kappa_ref, rate_ref, basis, halos, x_send, x_recv, y_send, y_recv,
    pairs, outbox, pairs_t, part_box, part_sum, carry_box, carry_sum, proj, half_send, half_recv, image_part, image_pair, image_own, gram_part, gram_sum, gram_all,
    load_sem, xs_sem, xr_sem, ys_sem, yr_sem, cs_sem, cr_sem, as_sem, ar_sem, gs_sem, gr_sem, is_sem, ir_sem, hs_sem, hr_sem, ps_sem, pr_sem, ms_sem, mr_sem, ts_sem, tr_sem,
):
    species = state.shape[0]
    ny = state.shape[2] - 16
    per = species // GROUPS
    ngx, ngy = lax.axis_size("gx"), lax.axis_size("gy")
    gx, gy = lax.axis_index("gx"), lax.axis_index("gy")
    right, left = lax.rem(gx + 1, ngx), lax.rem(gx + ngx - 1, ngx)
    north, south = lax.rem(gy + 1, ngy), lax.rem(gy + ngy - 1, ngy)
    core = lax.rem(gx, 2)
    half = ngx // 2
    chip = gx // 2
    sibling = gx + 1 - 2 * core
    own_lanes = pl.ds(pl.multiple_of(core * 128, 128), 128)
    pairs_per = per // 2
    lane = lax.broadcasted_iota(jnp.int32, (ny, 128), 1)
    pair = lane // 2

    load_state = pltpu.make_async_copy(init_hbm, state.at[:, :, pl.ds(8, ny), :], load_sem.at[0])
    load_vel = pltpu.make_async_copy(vel_hbm, vel, load_sem.at[1])
    load_kappa = pltpu.make_async_copy(kappa_hbm, kappa_ref, load_sem.at[2])
    load_rate = pltpu.make_async_copy(rate_hbm, rate_ref, load_sem.at[3])
    barrier = pltpu.get_barrier_semaphore()
    for peer in (left, right):
        pl.semaphore_signal(barrier, 1, device_id={"gx": peer}, device_id_type=MESH)
    load_state.start()

    @pl.loop(1, ngy)
    def _(d):
        peer = lax.rem(gy + d, ngy)
        pl.semaphore_signal(barrier, 1, device_id={"gy": peer}, device_id_type=MESH)
        pl.semaphore_signal(barrier, 1, device_id={"gx": sibling, "gy": peer}, device_id_type=MESH)

    @pl.loop(1, half)
    def _(d):
        peer = lax.rem(gx + 2 * d, ngx)
        pl.semaphore_signal(barrier, 1, device_id={"gx": peer}, device_id_type=MESH)

    load_kappa.start()
    load_rate.start()
    load_vel.start()

    def x_copy(e, to_left):
        return pltpu.make_async_remote_copy(
            src_ref=x_send.at[e],
            dst_ref=x_recv.at[e, int(to_left)],
            send_sem=xs_sem.at[int(to_left)],
            recv_sem=xr_sem.at[e],
            device_id={"gx": left if to_left else right},
            device_id_type=MESH,
        )

    def y_copy(e, to_south):
        d = int(to_south)
        return pltpu.make_async_remote_copy(
            src_ref=y_send.at[d, e],
            dst_ref=y_recv.at[e, d],
            send_sem=ys_sem.at[d],
            recv_sem=yr_sem.at[e],
            device_id={"gy": south if to_south else north},
            device_id_type=MESH,
        )

    def pair_copy(g):
        return pltpu.make_async_remote_copy(
            src_ref=outbox.at[pl.ds(g * pairs_per, pairs_per)],
            dst_ref=pairs.at[pl.ds(g * pairs_per, pairs_per), :, own_lanes],
            send_sem=cs_sem,
            recv_sem=cr_sem.at[g],
            device_id={"gx": sibling},
            device_id_type=MESH,
        )

    def part_copy(box, total, which, i):
        return pltpu.make_async_remote_copy(
            src_ref=box.at[i],
            dst_ref=total.at[chip],
            send_sem=as_sem.at[which],
            recv_sem=ar_sem.at[which],
            device_id={"gx": 2 * i + core},
            device_id_type=MESH,
        )

    def make_parts(box, first, count, rows):
        cells = pairs[pl.ds(first, count)].reshape(count * pairs.shape[1], pairs.shape[2])
        parts = jnp.dot(cells, rows, preferred_element_type=F32).astype(BF16)
        box[pl.ds(first, count)] = parts.reshape(count, *box.shape[1:])

    def all_of(ref, count):
        return ref.at[pl.ds(0, count)]

    def summed(box, total, which):
        arrived = all_of(total, half - 1)
        pltpu.make_async_copy(arrived, arrived, ar_sem.at[which]).wait()
        total[chip] = box[chip]
        return tree_sum([total[i].astype(F32) for i in range(half)])

    def pack_edges(e, now, first):
        packed = jnp.zeros((ny, 128), F32)
        for f in range(2 * per):
            field = now.at[first + f // 2, f % 2]
            packed = jnp.where(pair == f, rolled(field[pl.ds(8, ny), :], 2 * f + 1), packed)
            y_send[0, e, pl.ds(f, 1), :] = field[pl.ds(7 + ny, 1), :]
            y_send[1, e, pl.ds(f, 1), :] = field[pl.ds(8, 1), :]
        x_send[e] = packed.astype(x_send.dtype)

    def send_edges(e):
        x_copy(e, True).start()
        x_copy(e, False).start()
        y_copy(e, True).start()
        y_copy(e, False).start()

    load_state.wait()

    @pl.loop(0, GROUPS)
    def _(g):
        pack_edges(g, state, g * per)

    pl.semaphore_wait(barrier, half + 2 * ngy - 1)

    @pl.loop(0, GROUPS)
    def _(g):
        send_edges(g)

    basis_rows = pl.ds(pl.multiple_of(chip * 256, 256), 256)
    load_basis = pltpu.make_async_copy(basis_hbm.at[basis_rows], basis, load_sem.at[4])
    load_basis.start()
    load_vel.wait()
    vel[...] = vel[...] * 0.5
    vel[2, 1] = -vel[2, 1]
    load_kappa.wait()
    load_rate.wait()

    def advance(k, g, now, new):
        e = k * GROUPS + g
        last = k == SECTIONS - 1
        pltpu.make_async_copy(x_recv.at[e], x_recv.at[e], xr_sem.at[e]).wait()
        pltpu.make_async_copy(y_recv.at[e], y_recv.at[e], yr_sem.at[e]).wait()

        wide = lax.broadcasted_iota(jnp.int32, halos.shape, 1)
        halos[...] = jnp.where(
            lax.rem(wide, 2) == 0,
            rolled(x_recv[e, 1].astype(F32), 127),
            rolled(x_recv[e, 0].astype(F32), 1),
        )

        for j in range(per):
            for z in range(2):
                now[g * per + j, z, pl.ds(7, 1), :] = y_recv[e, 0, pl.ds(2 * j + z, 1), :]
                now[g * per + j, z, pl.ds(8 + ny, 1), :] = y_recv[e, 1, pl.ds(2 * j + z, 1), :]

        def step(j, box):
            s = g * per + j
            kappa, rate = kappa_ref[s], rate_ref[s]
            middle = 1.0 - 6.0 * kappa - rate
            for z in range(2):
                c = now[s, z, pl.ds(8, ny), :]
                other = now[s, 1 - z, pl.ds(8, ny), :]
                up = now[s, z, pl.ds(9, ny), :]
                down = now[s, z, pl.ds(7, ny), :]
                halo = rolled(halos[...], lax.rem(255 - 4 * j - 2 * z, 128))
                east = jnp.where(lane == 127, halo, rolled(c, 127))
                west = jnp.where(lane == 0, halo, rolled(c, 1))
                result = (
                    c * (middle + rate * (1.0 / (1.0 + c * c)))
                    + kappa * ((east + west) + (up + down))
                    + (kappa - vel[2, z]) * other
                    - vel[0, z] * (east - west)
                    - vel[1, z] * (up - down)
                )
                if last:
                    evolved_ref[s, z] = result
                    cells = result.astype(BF16)
                    if box is pairs:
                        pairs[s // 2, pl.ds(z * ny, ny), own_lanes] = cells
                    else:
                        outbox[s // 2, pl.ds(z * ny, ny), :] = cells
                else:
                    new[s, z, pl.ds(8, ny), :] = result

        if last:
            for box, parity in ((outbox, 1 - core), (pairs, core)):

                @pl.loop(0, per, step=2 * UNROLL)
                def _(j):
                    for i in range(UNROLL):
                        step(j + 2 * i + parity, box)

                if box is outbox:
                    pair_copy(g).start()
        else:

            @pl.loop(0, per, step=UNROLL)
            def _(j):
                for i in range(UNROLL):
                    step(j + i, None)

        if not last:
            pack_edges(e + GROUPS, new, g * per)
            send_edges(e + GROUPS)

    buffers = (state, state_b)
    for k in range(SECTIONS - 1):

        @pl.loop(0, GROUPS)
        def _(g):
            advance(k, g, buffers[k % 2], buffers[(k + 1) % 2])

    load_basis.wait()

    def group_parts(g):
        pair_copy(g).wait_recv()
        make_parts(part_box, g * pairs_per, pairs_per, basis[...])

        @pl.loop(0, pairs_per)
        def _(d):
            i = g * pairs_per + lax.rem(chip + d, pairs_per)

            @pl.when(i != chip)
            def _():
                part_copy(part_box, part_sum, 0, i).start()

    @pl.loop(0, GROUPS)
    def _(g):
        advance(SECTIONS - 1, g, buffers[(SECTIONS - 1) % 2], None)
        @pl.when(g > 0)
        def _():
            group_parts(g - 1)

    group_parts(GROUPS - 1)

    @pl.loop(0, half, step=2)
    def _(i):
        for k in range(2):
            pairs_t[:, pl.ds(pl.multiple_of((i + k) * 128, 128), 128)] = pairs[i + k].T

    def block(x):
        return pl.ds(pl.multiple_of(x // 2 * 128, 128), 128)

    plane = gx // per

    def in_plane(x, d):
        return x // per * per + lax.rem(x + 2 * d, per)

    def other_plane(x, d):
        return lax.rem(x + d * per, ngx)

    def send(x, peer):
        pltpu.make_async_remote_copy(
            src_ref=proj.at[block(x)],
            dst_ref=proj.at[block(x)],
            send_sem=gs_sem,
            recv_sem=gr_sem.at[x // 2],
            device_id={"gx": peer},
            device_id_type=MESH,
        ).start()

    def arrival(x):
        pltpu.make_async_copy(proj.at[block(x)], proj.at[block(x)], gr_sem.at[x // 2]).wait()

    order = (1, 3, 2)

    proj[block(gx), :] = summed(part_box, part_sum, 0).astype(BF16)

    for d in order:
        send(gx, other_plane(gx, d))
    for d in order:
        send(gx, in_plane(gx, d))

    @pl.loop(0, GROUPS)
    def _(p):
        @pl.when(p != plane)
        def _():
            x = p * per + lax.rem(gx, per)
            arrival(x)
            for d in order:
                send(x, in_plane(gx, d))

    for d in order:
        for f in range(GROUPS):
            arrival(other_plane(in_plane(gx, d), f))

    def image_half(c):
        rows = pl.ds(pl.multiple_of(c * 128, 128), 128)
        return jnp.dot(pairs_t[rows, :], proj[...], preferred_element_type=F32)

    half_send[...] = image_half(1 - core).astype(BF16)
    half_copy = pltpu.make_async_remote_copy(
        src_ref=half_send,
        dst_ref=half_recv,
        send_sem=hs_sem,
        recv_sem=hr_sem,
        device_id={"gx": sibling},
        device_id_type=MESH,
    )
    half_copy.start()
    part = image_half(core)
    half_copy.wait_recv()
    part = part + half_recv[...].astype(F32)

    image_part[gy] = part.astype(BF16)

    def image_copy(d):
        return pltpu.make_async_remote_copy(
            src_ref=image_part.at[gy],
            dst_ref=image_part.at[gy],
            send_sem=is_sem,
            recv_sem=ir_sem,
            device_id={"gy": lax.rem(gy + d, ngy)},
            device_id_type=MESH,
        )

    for d in (1, 3, 2):
        image_copy(d).start()
    arrived = all_of(image_part, ngy - 1)
    pltpu.make_async_copy(arrived, arrived, ir_sem).wait()
    image_own[...] = (image_part[0].astype(F32) + image_part[1].astype(F32)) + (
        image_part[2].astype(F32) + image_part[3].astype(F32)
    )
    image_pair[core] = image_own[...].astype(BF16)

    pair_image_copy = pltpu.make_async_remote_copy(
        src_ref=image_pair.at[core],
        dst_ref=image_pair.at[core],
        send_sem=ps_sem,
        recv_sem=pr_sem,
        device_id={"gx": sibling},
        device_id_type=MESH,
    )
    pair_image_copy.start()
    pair_image_copy.wait_recv()
    both = jnp.concatenate([image_pair[0], image_pair[1]], axis=0)

    gram_part[...] = lax.dot_general(both, both, (((0,), (0,)), ((), ())), preferred_element_type=F32)
    def share(y, c):
        return pl.ds(pl.multiple_of(y * 32 + c * 16, 16), 16)

    own_share = share(gy, core)
    gram_sum[chip] = gram_part[own_share, :]

    def gram_copy(d):
        return pltpu.make_async_remote_copy(
            src_ref=gram_part.at[own_share],
            dst_ref=gram_sum.at[chip],
            send_sem=ms_sem,
            recv_sem=mr_sem,
            device_id={"gx": lax.rem(gx + 2 * d, ngx)},
            device_id_type=MESH,
        )

    @pl.loop(1, half)
    def _(d):
        gram_copy(d).start()

    @pl.loop(0, half, step=8)
    def _(i):
        make_parts(carry_box, i, 8, both)

    @pl.loop(1, half)
    def _(d):
        part_copy(carry_box, carry_sum, 1, lax.rem(chip + d, half)).start()

    arrived = all_of(gram_sum, half - 1)
    pltpu.make_async_copy(arrived, arrived, mr_sem).wait()

    gram_all[own_share, :] = tree_sum([gram_sum[i] for i in range(half)])

    def rows_copy(d, c):
        return pltpu.make_async_remote_copy(
            src_ref=gram_all.at[own_share],
            dst_ref=gram_all.at[own_share],
            send_sem=ts_sem,
            recv_sem=tr_sem,
            device_id={"gx": 2 * chip + lax.rem(core + c, 2), "gy": lax.rem(gy + d, ngy)},
            device_id_type=MESH,
        )

    others = ((1, 0), (3, 0), (2, 0), (0, 1), (1, 1), (3, 1), (2, 1))
    for d, c in others:
        rows_copy(d, c).start()
    arrived = all_of(gram_all, 16 * len(others))
    pltpu.make_async_copy(arrived, arrived, tr_sem).wait()

    gram_ref[...] = gram_all[...]
    carried_ref[...] = summed(carry_box, carry_sum, 1)
    image_ref[...] = image_own[pl.ds(pl.multiple_of(gy * 32, 32), 32), :]

    for d in range(2):
        pltpu.make_async_copy(x_send, x_send, xs_sem.at[d]).wait()
        pltpu.make_async_copy(y_send.at[d], y_send.at[d], ys_sem.at[d]).wait()
    pltpu.make_async_copy(outbox, outbox, cs_sem).wait()
    for which in range(2):
        sent = part_box.at[pl.ds(0, half - 1)]
        pltpu.make_async_copy(sent, sent, as_sem.at[which]).wait()
    sent = all_of(proj, (half - 1) * 128)
    pltpu.make_async_copy(sent, sent, gs_sem).wait()
    half_copy.wait_send()
    pair_image_copy.wait_send()
    sent = gram_sum.at[pl.ds(0, half - 1)]
    pltpu.make_async_copy(sent, sent, ms_sem).wait()
    sent = all_of(gram_all, 16 * len(others))
    pltpu.make_async_copy(sent, sent, ts_sem).wait()
    sent = all_of(image_part, ngy - 1)
    pltpu.make_async_copy(sent, sent, is_sem).wait()


def finish(count, evolved_ref, gram_ref, carried_ref, image_ref, out_hbm, factor_ref, core_ref, sem):
    writing = pltpu.make_async_copy(evolved_ref, out_hbm, sem)
    writing.start()
    mix = mixing(gram_ref[...], count)
    factor_ref[...] = full_dot(image_ref[...], mix).astype(BF16)
    result = full_dot(carried_ref[...], mix) * (count ** -0.5)
    ny = core_ref.shape[2]
    core_ref[0, 0] = result[:ny]
    core_ref[0, 1] = result[ny:]
    writing.wait()


def shards(initial_state, velocity, diffusivity, reaction_rate, start_basis):
    species, nz, ny, nx = initial_state.shape
    ngx, ngy = lax.axis_size("gx"), lax.axis_size("gy")
    rank = start_basis.shape[1]
    operands = (initial_state, velocity, diffusivity, reaction_rate, start_basis)
    exchanges = SECTIONS * GROUPS
    rows = 2 * species // GROUPS
    hbm = pl.BlockSpec(memory_space=pltpu.HBM)
    vmem = pl.BlockSpec(memory_space=pltpu.VMEM)
    dma = pltpu.SemaphoreType.DMA
    evolved, gram, carried, image = pl.pallas_call(
        kernel,
        out_shape=(
            jax.ShapeDtypeStruct(initial_state.shape, F32),
            jax.ShapeDtypeStruct((rank, rank), F32),
            jax.ShapeDtypeStruct((nz * ny, rank), F32),
            jax.ShapeDtypeStruct((nx // ngy, rank), F32),
        ),
        in_specs=[hbm] * 5,
        out_specs=(vmem,) * 4,
        scratch_shapes=[
            pltpu.VMEM((species, nz, ny + 16, nx), F32),
            pltpu.VMEM((species, nz, ny + 16, nx), F32),
            pltpu.VMEM((3, nz, ny, nx), F32),
            pltpu.SMEM((species,), F32),
            pltpu.SMEM((species,), F32),
            pltpu.VMEM((2 * nx, rank), BF16),
            pltpu.VMEM((ny, nx), F32),
            pltpu.VMEM((exchanges, ny, nx), BF16),
            pltpu.VMEM((exchanges, 2, ny, nx), BF16),
            pltpu.VMEM((2, exchanges, rows, nx), F32),
            pltpu.VMEM((exchanges, 2, rows, nx), F32),
            pltpu.VMEM((species // 2, nz * ny, 2 * nx), BF16),
            pltpu.VMEM((species // 2, nz * ny, nx), BF16),
            pltpu.VMEM((2 * nx, species // 2 * nz * ny), BF16),
            pltpu.VMEM((ngx // 2, nz * ny, rank), BF16),
            pltpu.VMEM((ngx // 2, nz * ny, rank), BF16),
            pltpu.VMEM((ngx // 2, nz * ny, rank), BF16),
            pltpu.VMEM((ngx // 2, nz * ny, rank), BF16),
            pltpu.VMEM((species // 2 * nz * ny, rank), BF16),
            pltpu.VMEM((nx, rank), BF16),
            pltpu.VMEM((nx, rank), BF16),
            pltpu.VMEM((ngy, nx, rank), BF16),
            pltpu.VMEM((2, nx, rank), BF16),
            pltpu.VMEM((nx, rank), F32),
            pltpu.VMEM((rank, rank), F32),
            pltpu.VMEM((ngx // 2, rank // (2 * ngy), rank), F32),
            pltpu.VMEM((rank, rank), F32),
            dma((5,)),
            dma((2,)),
            dma((exchanges,)),
            dma((2,)),
            dma((exchanges,)),
            dma,
            dma((GROUPS,)),
            dma((2,)),
            dma((2,)),
            dma,
            dma((ngx // 2,)),
            dma,
            dma,
            dma,
            dma,
            dma,
            dma,
            dma,
            dma,
            dma,
            dma,
        ],
        compiler_params=pltpu.CompilerParams(
            collective_id=0, has_side_effects=True, vmem_limit_bytes=VMEM_LIMIT
        ),
    )(*(pltpu.with_memory_space_constraint(x, pltpu.HBM) for x in operands))
    return pl.pallas_call(
        functools.partial(finish, float(nx * ngx)),
        out_shape=(
            jax.ShapeDtypeStruct(initial_state.shape, F32),
            jax.ShapeDtypeStruct((nx // ngy, rank), BF16),
            jax.ShapeDtypeStruct((1, nz, ny, rank), F32),
        ),
        in_specs=[pl.BlockSpec(memory_space=pl.ANY), vmem, vmem, vmem],
        out_specs=(hbm, vmem, vmem),
        scratch_shapes=[dma],
        compiler_params=pltpu.CompilerParams(vmem_limit_bytes=8 << 20),
    )(evolved, gram, carried, image)


def solution(mesh):
    return jax.shard_map(
        shards,
        mesh=mesh,
        in_specs=(P(None, None, "gy", "gx"), P(None, None, "gy", "gx"), P(), P(), P()),
        out_specs=(P(None, None, "gy", "gx"), P(("gx", "gy"), None), P("gx", None, "gy", None)),
        check_vma=False,
    )
```

```python
import functools

import jax
import jax.numpy as jnp
from jax import lax
from jax.experimental import pallas as pl
from jax.experimental.pallas import tpu as pltpu
from jax.sharding import PartitionSpec as P

SECTIONS = 4
NS_STEPS = 5
EARLY_STEPS = 3
GROUPS = 8
PLANES = 4
UNROLL = 4
VMEM_LIMIT = 32 << 20
MESH = pl.DeviceIdType.MESH
F32 = jnp.float32
BF16 = jnp.bfloat16


def rolled(x, shift):
    return pltpu.roll(x, shift, 1)


def halves(x):
    high = x.astype(BF16)
    return high, (x - high.astype(F32)).astype(BF16)


def full_dot(a, b):
    a_high, a_low = halves(a)
    b_high, b_low = halves(b)
    return jnp.dot(
        jnp.concatenate([a_high, a_high, a_low], axis=1),
        jnp.concatenate([b_high, b_low, b_high], axis=0),
        preferred_element_type=F32,
    )


def tree_sum(terms):
    while len(terms) > 1:
        terms = [a + b for a, b in zip(terms[::2], terms[1::2])]
    return terms[0]


def identity_like(gram):
    row = lax.broadcasted_iota(jnp.int32, gram.shape, 0)
    column = lax.broadcasted_iota(jnp.int32, gram.shape, 1)
    return jnp.where(row == column, 1.0, 0.0).astype(F32)


def scaled(gram, count):
    identity = identity_like(gram)
    trace = jnp.sum(gram * identity, keepdims=True)
    squared = count / (trace + 1e-6)
    return gram * (squared / count), jnp.sqrt(squared) * identity


def newton_schulz(gram, mix, steps):
    identity = identity_like(gram)
    for step in steps:
        poly = 1.5 * identity - 0.5 * gram
        mix = full_dot(mix, poly)
        if step < NS_STEPS - 1:
            gram = full_dot(poly, full_dot(gram, poly))
    return gram, mix


def kernel(
    init_hbm, vel_hbm, kappa_hbm, rate_hbm, basis_hbm,
    evolved_ref, gram_ref, mix_ref, carried_ref, image_ref,
    state, state_b, vel, kappa_ref, rate_ref, basis, halos, x_send, x_recv, y_send, y_recv,
    pairs, outbox, pairs_t, part_box, part_sum, carry_box, carry_sum, proj, half_send, half_recv, image_part, image_pair, image_own, gram_part, gram_sum, gram_all,
    load_sem, xs_sem, xr_sem, ys_sem, yr_sem, cs_sem, cr_sem, as_sem, ar_sem, gs_sem, gr_sem, is_sem, ir_sem, hs_sem, hr_sem, ps_sem, pr_sem, ms_sem, mr_sem, ts_sem, tr_sem,
):
    species = state.shape[0]
    ny = state.shape[2] - 16
    per = species // GROUPS
    ngx, ngy = lax.axis_size("gx"), lax.axis_size("gy")
    gx, gy = lax.axis_index("gx"), lax.axis_index("gy")
    right, left = lax.rem(gx + 1, ngx), lax.rem(gx + ngx - 1, ngx)
    north, south = lax.rem(gy + 1, ngy), lax.rem(gy + ngy - 1, ngy)
    core = lax.rem(gx, 2)
    half = ngx // 2
    chip = gx // 2
    sibling = gx + 1 - 2 * core
    own_lanes = pl.ds(pl.multiple_of(core * 128, 128), 128)
    pairs_per = per // 2
    in_a_plane = species // PLANES
    line = in_a_plane // 2
    lane = lax.broadcasted_iota(jnp.int32, (ny, 128), 1)
    pair = lane // 2

    load_state = pltpu.make_async_copy(init_hbm, state.at[:, :, pl.ds(8, ny), :], load_sem.at[0])
    load_vel = pltpu.make_async_copy(vel_hbm, vel, load_sem.at[1])
    load_kappa = pltpu.make_async_copy(kappa_hbm, kappa_ref, load_sem.at[2])
    load_rate = pltpu.make_async_copy(rate_hbm, rate_ref, load_sem.at[3])
    barrier = pltpu.get_barrier_semaphore()
    for peer in (left, right):
        pl.semaphore_signal(barrier, 1, device_id={"gx": peer}, device_id_type=MESH)
    load_state.start()

    @pl.loop(1, ngy)
    def _(d):
        peer = lax.rem(gy + d, ngy)
        pl.semaphore_signal(barrier, 1, device_id={"gy": peer}, device_id_type=MESH)
        pl.semaphore_signal(barrier, 1, device_id={"gx": sibling, "gy": peer}, device_id_type=MESH)

    @pl.loop(1, half)
    def _(d):
        peer = lax.rem(gx + 2 * d, ngx)
        pl.semaphore_signal(barrier, 1, device_id={"gx": peer}, device_id_type=MESH)

    load_kappa.start()
    load_rate.start()
    load_vel.start()

    def x_copy(e, to_left):
        return pltpu.make_async_remote_copy(
            src_ref=x_send.at[e],
            dst_ref=x_recv.at[e, int(to_left)],
            send_sem=xs_sem.at[int(to_left)],
            recv_sem=xr_sem.at[e],
            device_id={"gx": left if to_left else right},
            device_id_type=MESH,
        )

    def y_copy(e, to_south):
        d = int(to_south)
        return pltpu.make_async_remote_copy(
            src_ref=y_send.at[d, e],
            dst_ref=y_recv.at[e, d],
            send_sem=ys_sem.at[d],
            recv_sem=yr_sem.at[e],
            device_id={"gy": south if to_south else north},
            device_id_type=MESH,
        )

    def pair_copy(g):
        return pltpu.make_async_remote_copy(
            src_ref=outbox.at[pl.ds(g * pairs_per, pairs_per)],
            dst_ref=pairs.at[pl.ds(g * pairs_per, pairs_per), :, own_lanes],
            send_sem=cs_sem,
            recv_sem=cr_sem.at[g],
            device_id={"gx": sibling},
            device_id_type=MESH,
        )

    def part_copy(box, total, which, i):
        return pltpu.make_async_remote_copy(
            src_ref=box.at[i],
            dst_ref=total.at[chip],
            send_sem=as_sem.at[which],
            recv_sem=ar_sem.at[which],
            device_id={"gx": 2 * i + core},
            device_id_type=MESH,
        )

    def make_parts(box, first, count, rows):
        cells = pairs[pl.ds(first, count)].reshape(count * pairs.shape[1], pairs.shape[2])
        parts = jnp.dot(cells, rows, preferred_element_type=F32).astype(BF16)
        box[pl.ds(first, count)] = parts.reshape(count, *box.shape[1:])

    def all_of(ref, count):
        return ref.at[pl.ds(0, count)]

    def summed(box, total, which):
        arrived = all_of(total, half - 1)
        pltpu.make_async_copy(arrived, arrived, ar_sem.at[which]).wait()
        total[chip] = box[chip]
        return tree_sum([total[i].astype(F32) for i in range(half)])

    def pack_edges(e, now, first):
        packed = jnp.zeros((ny, 128), F32)
        for f in range(2 * per):
            field = now.at[first + f // 2, f % 2]
            packed = jnp.where(pair == f, rolled(field[pl.ds(8, ny), :], 2 * f + 1), packed)
            y_send[0, e, pl.ds(f, 1), :] = field[pl.ds(7 + ny, 1), :]
            y_send[1, e, pl.ds(f, 1), :] = field[pl.ds(8, 1), :]
        x_send[e] = packed.astype(x_send.dtype)

    def send_edges(e):
        x_copy(e, True).start()
        x_copy(e, False).start()
        y_copy(e, True).start()
        y_copy(e, False).start()

    load_state.wait()

    @pl.loop(0, GROUPS)
    def _(g):
        pack_edges(g, state, g * per)

    pl.semaphore_wait(barrier, half + 2 * ngy - 1)

    @pl.loop(0, GROUPS)
    def _(g):
        send_edges(g)

    basis_rows = pl.ds(pl.multiple_of(chip * 256, 256), 256)
    load_basis = pltpu.make_async_copy(basis_hbm.at[basis_rows], basis, load_sem.at[4])
    load_basis.start()
    load_vel.wait()
    vel[...] = vel[...] * 0.5
    vel[2, 1] = -vel[2, 1]
    load_kappa.wait()
    load_rate.wait()

    def advance(k, g, now, new):
        e = k * GROUPS + g
        last = k == SECTIONS - 1
        pltpu.make_async_copy(x_recv.at[e], x_recv.at[e], xr_sem.at[e]).wait()
        pltpu.make_async_copy(y_recv.at[e], y_recv.at[e], yr_sem.at[e]).wait()

        wide = lax.broadcasted_iota(jnp.int32, halos.shape, 1)
        halos[...] = jnp.where(
            lax.rem(wide, 2) == 0,
            rolled(x_recv[e, 1].astype(F32), 127),
            rolled(x_recv[e, 0].astype(F32), 1),
        )

        for j in range(per):
            for z in range(2):
                now[g * per + j, z, pl.ds(7, 1), :] = y_recv[e, 0, pl.ds(2 * j + z, 1), :]
                now[g * per + j, z, pl.ds(8 + ny, 1), :] = y_recv[e, 1, pl.ds(2 * j + z, 1), :]

        def step(j, box):
            s = g * per + j
            kappa, rate = kappa_ref[s], rate_ref[s]
            middle = 1.0 - 6.0 * kappa - rate
            for z in range(2):
                c = now[s, z, pl.ds(8, ny), :]
                other = now[s, 1 - z, pl.ds(8, ny), :]
                up = now[s, z, pl.ds(9, ny), :]
                down = now[s, z, pl.ds(7, ny), :]
                halo = rolled(halos[...], lax.rem(255 - 4 * j - 2 * z, 128))
                east = jnp.where(lane == 127, halo, rolled(c, 127))
                west = jnp.where(lane == 0, halo, rolled(c, 1))
                result = (
                    c * (middle + rate * (1.0 / (1.0 + c * c)))
                    + kappa * ((east + west) + (up + down))
                    + (kappa - vel[2, z]) * other
                    - vel[0, z] * (east - west)
                    - vel[1, z] * (up - down)
                )
                if last:
                    evolved_ref[s, z] = result
                    cells = result.astype(BF16)
                    if box is pairs:
                        pairs[s // 2, pl.ds(z * ny, ny), own_lanes] = cells
                    else:
                        outbox[s // 2, pl.ds(z * ny, ny), :] = cells
                else:
                    new[s, z, pl.ds(8, ny), :] = result

        if last:
            for box, parity in ((outbox, 1 - core), (pairs, core)):

                for i in range(pairs_per):
                    step(2 * i + parity, box)

                if box is outbox:
                    pair_copy(g).start()
        else:

            @pl.loop(0, per, step=UNROLL)
            def _(j):
                for i in range(UNROLL):
                    step(j + i, None)

        if not last:
            pack_edges(e + GROUPS, new, g * per)
            send_edges(e + GROUPS)

    buffers = (state, state_b)
    for k in range(SECTIONS - 1):

        @pl.loop(0, GROUPS)
        def _(g):
            advance(k, g, buffers[k % 2], buffers[(k + 1) % 2])

    load_basis.wait()

    def plane_parts(p):
        for g in range(GROUPS // PLANES):
            pair_copy(p * (GROUPS // PLANES) + g).wait_recv()
        make_parts(part_box, p * line, line, basis[...])

        @pl.loop(0, line)
        def _(d):
            i = p * line + lax.rem(chip + d, line)

            @pl.when(i != chip)
            def _():
                part_copy(part_box, part_sum, 0, i).start()

    @pl.loop(0, PLANES)
    def _(p):
        for g in range(GROUPS // PLANES):
            advance(SECTIONS - 1, p * (GROUPS // PLANES) + g, buffers[(SECTIONS - 1) % 2], None)

        @pl.when(p > 0)
        def _():
            plane_parts(p - 1)

    plane_parts(PLANES - 1)

    @pl.loop(0, half, step=2)
    def _(i):
        for k in range(2):
            pairs_t[:, pl.ds(pl.multiple_of((i + k) * 128, 128), 128)] = pairs[i + k].T

    def block(x):
        return pl.ds(pl.multiple_of(x // 2 * 128, 128), 128)

    plane = gx // in_a_plane

    def in_plane(x, d):
        return x // in_a_plane * in_a_plane + lax.rem(x + 2 * d, in_a_plane)

    def other_plane(x, d):
        return lax.rem(x + d * in_a_plane, ngx)

    def send(x, peer):
        pltpu.make_async_remote_copy(
            src_ref=proj.at[block(x)],
            dst_ref=proj.at[block(x)],
            send_sem=gs_sem,
            recv_sem=gr_sem.at[x // 2],
            device_id={"gx": peer},
            device_id_type=MESH,
        ).start()

    def arrival(x):
        pltpu.make_async_copy(proj.at[block(x)], proj.at[block(x)], gr_sem.at[x // 2]).wait()

    order = (1, 3, 2)

    proj[block(gx), :] = summed(part_box, part_sum, 0).astype(BF16)

    for d in order:
        send(gx, other_plane(gx, d))
    for d in order:
        send(gx, in_plane(gx, d))

    @pl.loop(0, PLANES)
    def _(p):
        @pl.when(p != plane)
        def _():
            x = p * in_a_plane + lax.rem(gx, in_a_plane)
            arrival(x)
            for d in order:
                send(x, in_plane(gx, d))

    for d in order:
        for f in range(PLANES):
            arrival(other_plane(in_plane(gx, d), f))

    def image_half(c):
        rows = pl.ds(pl.multiple_of(c * 128, 128), 128)
        return jnp.dot(pairs_t[rows, :], proj[...], preferred_element_type=F32)

    half_send[...] = image_half(1 - core).astype(BF16)
    half_copy = pltpu.make_async_remote_copy(
        src_ref=half_send,
        dst_ref=half_recv,
        send_sem=hs_sem,
        recv_sem=hr_sem,
        device_id={"gx": sibling},
        device_id_type=MESH,
    )
    half_copy.start()
    part = image_half(core)
    half_copy.wait_recv()
    part = part + half_recv[...].astype(F32)

    image_part[gy] = part.astype(BF16)

    def image_copy(d):
        return pltpu.make_async_remote_copy(
            src_ref=image_part.at[gy],
            dst_ref=image_part.at[gy],
            send_sem=is_sem,
            recv_sem=ir_sem,
            device_id={"gy": lax.rem(gy + d, ngy)},
            device_id_type=MESH,
        )

    for d in (1, 3, 2):
        image_copy(d).start()
    arrived = all_of(image_part, ngy - 1)
    pltpu.make_async_copy(arrived, arrived, ir_sem).wait()
    image_own[...] = (image_part[0].astype(F32) + image_part[1].astype(F32)) + (
        image_part[2].astype(F32) + image_part[3].astype(F32)
    )
    image_pair[core] = image_own[...].astype(BF16)

    pair_image_copy = pltpu.make_async_remote_copy(
        src_ref=image_pair.at[core],
        dst_ref=image_pair.at[core],
        send_sem=ps_sem,
        recv_sem=pr_sem,
        device_id={"gx": sibling},
        device_id_type=MESH,
    )
    pair_image_copy.start()
    pair_image_copy.wait_recv()
    both = jnp.concatenate([image_pair[0], image_pair[1]], axis=0)

    gram_part[...] = lax.dot_general(both, both, (((0,), (0,)), ((), ())), preferred_element_type=F32)
    def share(y, c):
        return pl.ds(pl.multiple_of(y * 32 + c * 16, 16), 16)

    own_share = share(gy, core)
    gram_sum[chip] = gram_part[own_share, :]

    def gram_copy(d):
        return pltpu.make_async_remote_copy(
            src_ref=gram_part.at[own_share],
            dst_ref=gram_sum.at[chip],
            send_sem=ms_sem,
            recv_sem=mr_sem,
            device_id={"gx": lax.rem(gx + 2 * d, ngx)},
            device_id_type=MESH,
        )

    @pl.loop(1, half)
    def _(d):
        gram_copy(lax.rem(5 * d, half)).start()

    @pl.loop(0, half, step=8)
    def _(i):
        make_parts(carry_box, i, 8, both)

    @pl.loop(1, half)
    def _(d):
        part_copy(carry_box, carry_sum, 1, lax.rem(chip + 5 * d, half)).start()

    arrived = all_of(gram_sum, half - 1)
    pltpu.make_async_copy(arrived, arrived, mr_sem).wait()

    gram_all[own_share, :] = tree_sum([gram_sum[i] for i in range(half)])

    def rows_copy(d, c):
        return pltpu.make_async_remote_copy(
            src_ref=gram_all.at[own_share],
            dst_ref=gram_all.at[own_share],
            send_sem=ts_sem,
            recv_sem=tr_sem,
            device_id={"gx": 2 * chip + lax.rem(core + c, 2), "gy": lax.rem(gy + d, ngy)},
            device_id_type=MESH,
        )

    others = ((1, 0), (3, 0), (2, 0), (0, 1), (1, 1), (3, 1), (2, 1))
    for d, c in others:
        rows_copy(d, c).start()
    arrived = all_of(gram_all, 16 * len(others))
    pltpu.make_async_copy(arrived, arrived, tr_sem).wait()

    gram, mix = newton_schulz(*scaled(gram_all[...], 128.0 * ngx), range(EARLY_STEPS))
    gram_ref[...] = gram
    mix_ref[...] = mix
    carried_ref[...] = summed(carry_box, carry_sum, 1)
    image_ref[...] = image_own[pl.ds(pl.multiple_of(gy * 32, 32), 32), :]

    for d in range(2):
        pltpu.make_async_copy(x_send, x_send, xs_sem.at[d]).wait()
        pltpu.make_async_copy(y_send.at[d], y_send.at[d], ys_sem.at[d]).wait()
    pltpu.make_async_copy(outbox, outbox, cs_sem).wait()
    for which in range(2):
        sent = part_box.at[pl.ds(0, half - 1)]
        pltpu.make_async_copy(sent, sent, as_sem.at[which]).wait()
    sent = all_of(proj, (half - 1) * 128)
    pltpu.make_async_copy(sent, sent, gs_sem).wait()
    half_copy.wait_send()
    pair_image_copy.wait_send()
    sent = gram_sum.at[pl.ds(0, half - 1)]
    pltpu.make_async_copy(sent, sent, ms_sem).wait()
    sent = all_of(gram_all, 16 * len(others))
    pltpu.make_async_copy(sent, sent, ts_sem).wait()
    sent = all_of(image_part, ngy - 1)
    pltpu.make_async_copy(sent, sent, is_sem).wait()


def finish(count, evolved_ref, gram_ref, mix_ref, carried_ref, image_ref, out_hbm, factor_ref, core_ref, sem):
    writing = pltpu.make_async_copy(evolved_ref, out_hbm, sem)
    writing.start()
    _, mix = newton_schulz(gram_ref[...], mix_ref[...], range(EARLY_STEPS, NS_STEPS))
    factor_ref[...] = full_dot(image_ref[...], mix).astype(BF16)
    result = full_dot(carried_ref[...], mix) * (count ** -0.5)
    ny = core_ref.shape[2]
    core_ref[0, 0] = result[:ny]
    core_ref[0, 1] = result[ny:]
    writing.wait()


def shards(initial_state, velocity, diffusivity, reaction_rate, start_basis):
    species, nz, ny, nx = initial_state.shape
    ngx, ngy = lax.axis_size("gx"), lax.axis_size("gy")
    rank = start_basis.shape[1]
    operands = (initial_state, velocity, diffusivity, reaction_rate, start_basis)
    exchanges = SECTIONS * GROUPS
    rows = 2 * species // GROUPS
    hbm = pl.BlockSpec(memory_space=pltpu.HBM)
    vmem = pl.BlockSpec(memory_space=pltpu.VMEM)
    dma = pltpu.SemaphoreType.DMA
    evolved, gram, mix, carried, image = pl.pallas_call(
        kernel,
        out_shape=(
            jax.ShapeDtypeStruct(initial_state.shape, F32),
            jax.ShapeDtypeStruct((rank, rank), F32),
            jax.ShapeDtypeStruct((rank, rank), F32),
            jax.ShapeDtypeStruct((nz * ny, rank), F32),
            jax.ShapeDtypeStruct((nx // ngy, rank), F32),
        ),
        in_specs=[hbm] * 5,
        out_specs=(vmem,) * 5,
        scratch_shapes=[
            pltpu.VMEM((species, nz, ny + 16, nx), F32),
            pltpu.VMEM((species, nz, ny + 16, nx), F32),
            pltpu.VMEM((3, nz, ny, nx), F32),
            pltpu.SMEM((species,), F32),
            pltpu.SMEM((species,), F32),
            pltpu.VMEM((2 * nx, rank), BF16),
            pltpu.VMEM((ny, nx), F32),
            pltpu.VMEM((exchanges, ny, nx), BF16),
            pltpu.VMEM((exchanges, 2, ny, nx), BF16),
            pltpu.VMEM((2, exchanges, rows, nx), F32),
            pltpu.VMEM((exchanges, 2, rows, nx), F32),
            pltpu.VMEM((species // 2, nz * ny, 2 * nx), BF16),
            pltpu.VMEM((species // 2, nz * ny, nx), BF16),
            pltpu.VMEM((2 * nx, species // 2 * nz * ny), BF16),
            pltpu.VMEM((ngx // 2, nz * ny, rank), BF16),
            pltpu.VMEM((ngx // 2, nz * ny, rank), BF16),
            pltpu.VMEM((ngx // 2, nz * ny, rank), BF16),
            pltpu.VMEM((ngx // 2, nz * ny, rank), BF16),
            pltpu.VMEM((species // 2 * nz * ny, rank), BF16),
            pltpu.VMEM((nx, rank), BF16),
            pltpu.VMEM((nx, rank), BF16),
            pltpu.VMEM((ngy, nx, rank), BF16),
            pltpu.VMEM((2, nx, rank), BF16),
            pltpu.VMEM((nx, rank), F32),
            pltpu.VMEM((rank, rank), F32),
            pltpu.VMEM((ngx // 2, rank // (2 * ngy), rank), F32),
            pltpu.VMEM((rank, rank), F32),
            dma((5,)),
            dma((2,)),
            dma((exchanges,)),
            dma((2,)),
            dma((exchanges,)),
            dma,
            dma((GROUPS,)),
            dma((2,)),
            dma((2,)),
            dma,
            dma((ngx // 2,)),
            dma,
            dma,
            dma,
            dma,
            dma,
            dma,
            dma,
            dma,
            dma,
            dma,
        ],
        compiler_params=pltpu.CompilerParams(
            collective_id=0, has_side_effects=True, vmem_limit_bytes=VMEM_LIMIT
        ),
    )(*(pltpu.with_memory_space_constraint(x, pltpu.HBM) for x in operands))
    return pl.pallas_call(
        functools.partial(finish, float(nx * ngx)),
        out_shape=(
            jax.ShapeDtypeStruct(initial_state.shape, F32),
            jax.ShapeDtypeStruct((nx // ngy, rank), BF16),
            jax.ShapeDtypeStruct((1, nz, ny, rank), F32),
        ),
        in_specs=[pl.BlockSpec(memory_space=pl.ANY), vmem, vmem, vmem, vmem],
        out_specs=(hbm, vmem, vmem),
        scratch_shapes=[dma],
        compiler_params=pltpu.CompilerParams(vmem_limit_bytes=8 << 20),
    )(evolved, gram, mix, carried, image)


def solution(mesh):
    return jax.shard_map(
        shards,
        mesh=mesh,
        in_specs=(P(None, None, "gy", "gx"), P(None, None, "gy", "gx"), P(), P(), P()),
        out_specs=(P(None, None, "gy", "gx"), P(("gx", "gy"), None), P("gx", None, "gy", None)),
        check_vma=False,
    )
```

```python
import functools

import jax
import jax.numpy as jnp
from jax import lax
from jax.experimental import pallas as pl
from jax.experimental.pallas import tpu as pltpu
from jax.sharding import PartitionSpec as P

SECTIONS = 4
NS_STEPS = 5
EARLY_STEPS = 3
GROUPS = 8
PLANES = 4
UNROLL = 4
VMEM_LIMIT = 32 << 20
MESH = pl.DeviceIdType.MESH
F32 = jnp.float32
BF16 = jnp.bfloat16


def rolled(x, shift):
    return pltpu.roll(x, shift, 1)


def halves(x):
    high = x.astype(BF16)
    return high, (x - high.astype(F32)).astype(BF16)


def full_dot(a, b):
    a_high, a_low = halves(a)
    b_high, b_low = halves(b)
    return jnp.dot(
        jnp.concatenate([a_high, a_high, a_low], axis=1),
        jnp.concatenate([b_high, b_low, b_high], axis=0),
        preferred_element_type=F32,
    )


def tree_sum(terms):
    while len(terms) > 1:
        terms = [a + b for a, b in zip(terms[::2], terms[1::2])]
    return terms[0]


def identity_like(gram):
    row = lax.broadcasted_iota(jnp.int32, gram.shape, 0)
    column = lax.broadcasted_iota(jnp.int32, gram.shape, 1)
    return jnp.where(row == column, 1.0, 0.0).astype(F32)


def scaled(gram, count):
    identity = identity_like(gram)
    trace = jnp.sum(gram * identity, keepdims=True)
    squared = count / (trace + 1e-6)
    return gram * (squared / count), jnp.sqrt(squared) * identity


def newton_schulz(gram, mix, steps):
    identity = identity_like(gram)
    for step in steps:
        poly = 1.5 * identity - 0.5 * gram
        mix = full_dot(mix, poly)
        if step < NS_STEPS - 1:
            gram = full_dot(poly, full_dot(gram, poly))
    return gram, mix


def kernel(
    init_hbm, vel_hbm, kappa_hbm, rate_hbm, basis_hbm,
    evolved_ref, gram_ref, mix_ref, carried_ref, image_ref,
    state, state_b, vel, kappa_ref, rate_ref, basis, halos, x_send, x_recv, y_send, y_recv,
    pairs, outbox, pairs_t, part_box, part_sum, carry_box, carry_sum, proj, half_send, half_recv, image_part, image_pair, image_own, gram_part, gram_sum, gram_all,
    load_sem, xs_sem, xr_sem, ys_sem, yr_sem, cs_sem, cr_sem, as_sem, ar_sem, gs_sem, gr_sem, is_sem, ir_sem, hs_sem, hr_sem, ps_sem, pr_sem, ms_sem, mr_sem, ts_sem, tr_sem,
):
    species = state.shape[0]
    ny = state.shape[2] - 16
    per = species // GROUPS
    ngx, ngy = lax.axis_size("gx"), lax.axis_size("gy")
    gx, gy = lax.axis_index("gx"), lax.axis_index("gy")
    right, left = lax.rem(gx + 1, ngx), lax.rem(gx + ngx - 1, ngx)
    north, south = lax.rem(gy + 1, ngy), lax.rem(gy + ngy - 1, ngy)
    core = lax.rem(gx, 2)
    half = ngx // 2
    chip = gx // 2
    sibling = gx + 1 - 2 * core
    own_lanes = pl.ds(pl.multiple_of(core * 128, 128), 128)
    pairs_per = per // 2
    in_a_plane = species // PLANES
    line = in_a_plane // 2
    lane = lax.broadcasted_iota(jnp.int32, (ny, 128), 1)
    pair = lane // 2

    def load_state(g):
        return pltpu.make_async_copy(
            init_hbm.at[pl.ds(g * per, per)],
            state.at[pl.ds(g * per, per), :, pl.ds(8, ny), :],
            load_sem.at[4 + g],
        )

    load_vel = pltpu.make_async_copy(vel_hbm, vel, load_sem.at[1])
    load_kappa = pltpu.make_async_copy(kappa_hbm, kappa_ref, load_sem.at[2])
    load_rate = pltpu.make_async_copy(rate_hbm, rate_ref, load_sem.at[3])
    barrier = pltpu.get_barrier_semaphore()
    for peer in (left, right):
        pl.semaphore_signal(barrier, 1, device_id={"gx": peer}, device_id_type=MESH)
    for g in range(GROUPS):
        load_state(g).start()

    @pl.loop(1, ngy)
    def _(d):
        peer = lax.rem(gy + d, ngy)
        pl.semaphore_signal(barrier, 1, device_id={"gy": peer}, device_id_type=MESH)
        pl.semaphore_signal(barrier, 1, device_id={"gx": sibling, "gy": peer}, device_id_type=MESH)

    @pl.loop(1, half)
    def _(d):
        peer = lax.rem(gx + 2 * d, ngx)
        pl.semaphore_signal(barrier, 1, device_id={"gx": peer}, device_id_type=MESH)

    load_kappa.start()
    load_rate.start()
    load_vel.start()

    def x_copy(e, to_left):
        return pltpu.make_async_remote_copy(
            src_ref=x_send.at[e],
            dst_ref=x_recv.at[e, int(to_left)],
            send_sem=xs_sem.at[int(to_left)],
            recv_sem=xr_sem.at[e],
            device_id={"gx": left if to_left else right},
            device_id_type=MESH,
        )

    def y_copy(e, to_south):
        d = int(to_south)
        return pltpu.make_async_remote_copy(
            src_ref=y_send.at[d, e],
            dst_ref=y_recv.at[e, d],
            send_sem=ys_sem.at[d],
            recv_sem=yr_sem.at[e],
            device_id={"gy": south if to_south else north},
            device_id_type=MESH,
        )

    def pair_copy(g):
        return pltpu.make_async_remote_copy(
            src_ref=outbox.at[pl.ds(g * pairs_per, pairs_per)],
            dst_ref=pairs.at[pl.ds(g * pairs_per, pairs_per), :, own_lanes],
            send_sem=cs_sem,
            recv_sem=cr_sem.at[g],
            device_id={"gx": sibling},
            device_id_type=MESH,
        )

    def part_copy(box, total, which, i):
        return pltpu.make_async_remote_copy(
            src_ref=box.at[i],
            dst_ref=total.at[chip],
            send_sem=as_sem.at[which],
            recv_sem=ar_sem.at[which],
            device_id={"gx": 2 * i + core},
            device_id_type=MESH,
        )

    def make_parts(box, first, count, rows):
        cells = pairs[pl.ds(first, count)].reshape(count * pairs.shape[1], pairs.shape[2])
        parts = jnp.dot(cells, rows, preferred_element_type=F32).astype(BF16)
        box[pl.ds(first, count)] = parts.reshape(count, *box.shape[1:])

    def all_of(ref, count):
        return ref.at[pl.ds(0, count)]

    def summed(box, total, which):
        arrived = all_of(total, half - 1)
        pltpu.make_async_copy(arrived, arrived, ar_sem.at[which]).wait()
        total[chip] = box[chip]
        return tree_sum([total[i].astype(F32) for i in range(half)])

    def pack_edges(e, now, first):
        packed = jnp.zeros((ny, 128), F32)
        for f in range(2 * per):
            field = now.at[first + f // 2, f % 2]
            packed = jnp.where(pair == f, rolled(field[pl.ds(8, ny), :], 2 * f + 1), packed)
            y_send[0, e, pl.ds(f, 1), :] = field[pl.ds(7 + ny, 1), :]
            y_send[1, e, pl.ds(f, 1), :] = field[pl.ds(8, 1), :]
        x_send[e] = packed.astype(x_send.dtype)

    def send_edges(e):
        x_copy(e, True).start()
        x_copy(e, False).start()
        y_copy(e, True).start()
        y_copy(e, False).start()

    load_state(0).wait()
    pack_edges(0, state, 0)
    pl.semaphore_wait(barrier, half + 2 * ngy - 1)
    send_edges(0)

    @pl.loop(1, GROUPS)
    def _(g):
        load_state(g).wait()
        pack_edges(g, state, g * per)
        send_edges(g)

    basis_rows = pl.ds(pl.multiple_of(chip * 256, 256), 256)
    load_basis = pltpu.make_async_copy(basis_hbm.at[basis_rows], basis, load_sem.at[0])
    load_basis.start()
    load_vel.wait()
    vel[...] = vel[...] * 0.5
    vel[2, 1] = -vel[2, 1]
    load_kappa.wait()
    load_rate.wait()

    def advance(k, g, now, new):
        e = k * GROUPS + g
        last = k == SECTIONS - 1
        pltpu.make_async_copy(x_recv.at[e], x_recv.at[e], xr_sem.at[e]).wait()
        pltpu.make_async_copy(y_recv.at[e], y_recv.at[e], yr_sem.at[e]).wait()

        wide = lax.broadcasted_iota(jnp.int32, halos.shape, 1)
        halos[...] = jnp.where(
            lax.rem(wide, 2) == 0,
            rolled(x_recv[e, 1].astype(F32), 127),
            rolled(x_recv[e, 0].astype(F32), 1),
        )

        for j in range(per):
            for z in range(2):
                now[g * per + j, z, pl.ds(7, 1), :] = y_recv[e, 0, pl.ds(2 * j + z, 1), :]
                now[g * per + j, z, pl.ds(8 + ny, 1), :] = y_recv[e, 1, pl.ds(2 * j + z, 1), :]

        def step(j, box):
            s = g * per + j
            kappa, rate = kappa_ref[s], rate_ref[s]
            middle = 1.0 - 6.0 * kappa - rate
            for z in range(2):
                c = now[s, z, pl.ds(8, ny), :]
                other = now[s, 1 - z, pl.ds(8, ny), :]
                up = now[s, z, pl.ds(9, ny), :]
                down = now[s, z, pl.ds(7, ny), :]
                halo = rolled(halos[...], lax.rem(255 - 4 * j - 2 * z, 128))
                east = jnp.where(lane == 127, halo, rolled(c, 127))
                west = jnp.where(lane == 0, halo, rolled(c, 1))
                result = (
                    c * (middle + rate * (1.0 / (1.0 + c * c)))
                    + kappa * ((east + west) + (up + down))
                    + (kappa - vel[2, z]) * other
                    - vel[0, z] * (east - west)
                    - vel[1, z] * (up - down)
                )
                if last:
                    evolved_ref[s, z] = result
                    cells = result.astype(BF16)
                    if box is pairs:
                        pairs[s // 2, pl.ds(z * ny, ny), own_lanes] = cells
                    else:
                        outbox[s // 2, pl.ds(z * ny, ny), :] = cells
                else:
                    new[s, z, pl.ds(8, ny), :] = result

        if last:
            for i in range(pairs_per):
                step(2 * i + 1 - core, outbox)
            for i in range(pairs_per):
                step(2 * i + core, pairs)
            pair_copy(g).start()
        else:

            @pl.loop(0, per, step=UNROLL)
            def _(j):
                for i in range(UNROLL):
                    step(j + i, None)

        if not last:
            pack_edges(e + GROUPS, new, g * per)
            send_edges(e + GROUPS)

    buffers = (state, state_b)
    for k in range(SECTIONS - 1):

        @pl.loop(0, GROUPS)
        def _(g):
            advance(k, g, buffers[k % 2], buffers[(k + 1) % 2])

    load_basis.wait()

    def plane_parts(p):
        for g in range(GROUPS // PLANES):
            pair_copy(p * (GROUPS // PLANES) + g).wait_recv()
        make_parts(part_box, p * line, line, basis[...])

        @pl.loop(0, line)
        def _(d):
            i = p * line + lax.rem(chip + d, line)

            @pl.when(i != chip)
            def _():
                part_copy(part_box, part_sum, 0, i).start()

    @pl.loop(0, PLANES)
    def _(p):
        for g in range(GROUPS // PLANES):
            advance(SECTIONS - 1, p * (GROUPS // PLANES) + g, buffers[(SECTIONS - 1) % 2], None)

        @pl.when(p > 0)
        def _():
            plane_parts(p - 1)

    plane_parts(PLANES - 1)

    @pl.loop(0, half, step=2)
    def _(i):
        for k in range(2):
            pairs_t[:, pl.ds(pl.multiple_of((i + k) * 128, 128), 128)] = pairs[i + k].T

    def block(x):
        return pl.ds(pl.multiple_of(x // 2 * 128, 128), 128)

    plane = gx // in_a_plane

    def in_plane(x, d):
        return x // in_a_plane * in_a_plane + lax.rem(x + 2 * d, in_a_plane)

    def other_plane(x, d):
        return lax.rem(x + d * in_a_plane, ngx)

    def send(x, peer):
        pltpu.make_async_remote_copy(
            src_ref=proj.at[block(x)],
            dst_ref=proj.at[block(x)],
            send_sem=gs_sem,
            recv_sem=gr_sem.at[x // 2],
            device_id={"gx": peer},
            device_id_type=MESH,
        ).start()

    def arrival(x):
        pltpu.make_async_copy(proj.at[block(x)], proj.at[block(x)], gr_sem.at[x // 2]).wait()

    order = (1, 3, 2)

    proj[block(gx), :] = summed(part_box, part_sum, 0).astype(BF16)

    for d in order:
        send(gx, other_plane(gx, d))
    for d in order:
        send(gx, in_plane(gx, d))

    @pl.loop(0, PLANES)
    def _(p):
        @pl.when(p != plane)
        def _():
            x = p * in_a_plane + lax.rem(gx, in_a_plane)
            arrival(x)
            for d in order:
                send(x, in_plane(gx, d))

    for d in order:
        for f in range(PLANES):
            arrival(other_plane(in_plane(gx, d), f))

    def image_half(c):
        rows = pl.ds(pl.multiple_of(c * 128, 128), 128)
        return jnp.dot(pairs_t[rows, :], proj[...], preferred_element_type=F32)

    half_send[...] = image_half(1 - core).astype(BF16)
    half_copy = pltpu.make_async_remote_copy(
        src_ref=half_send,
        dst_ref=half_recv,
        send_sem=hs_sem,
        recv_sem=hr_sem,
        device_id={"gx": sibling},
        device_id_type=MESH,
    )
    half_copy.start()
    part = image_half(core)
    half_copy.wait_recv()
    part = part + half_recv[...].astype(F32)

    image_part[gy] = part.astype(BF16)

    def image_copy(d):
        return pltpu.make_async_remote_copy(
            src_ref=image_part.at[gy],
            dst_ref=image_part.at[gy],
            send_sem=is_sem,
            recv_sem=ir_sem,
            device_id={"gy": lax.rem(gy + d, ngy)},
            device_id_type=MESH,
        )

    for d in (1, 3, 2):
        image_copy(d).start()
    arrived = all_of(image_part, ngy - 1)
    pltpu.make_async_copy(arrived, arrived, ir_sem).wait()
    image_own[...] = (image_part[0].astype(F32) + image_part[1].astype(F32)) + (
        image_part[2].astype(F32) + image_part[3].astype(F32)
    )
    image_pair[core] = image_own[...].astype(BF16)

    pair_image_copy = pltpu.make_async_remote_copy(
        src_ref=image_pair.at[core],
        dst_ref=image_pair.at[core],
        send_sem=ps_sem,
        recv_sem=pr_sem,
        device_id={"gx": sibling},
        device_id_type=MESH,
    )
    pair_image_copy.start()
    pair_image_copy.wait_recv()
    both = jnp.concatenate([image_pair[0], image_pair[1]], axis=0)

    gram_part[...] = lax.dot_general(both, both, (((0,), (0,)), ((), ())), preferred_element_type=F32)
    def share(y, c):
        return pl.ds(pl.multiple_of(y * 32 + c * 16, 16), 16)

    own_share = share(gy, core)
    gram_sum[chip] = gram_part[own_share, :]

    def gram_copy(d):
        return pltpu.make_async_remote_copy(
            src_ref=gram_part.at[own_share],
            dst_ref=gram_sum.at[chip],
            send_sem=ms_sem,
            recv_sem=mr_sem,
            device_id={"gx": lax.rem(gx + 2 * d, ngx)},
            device_id_type=MESH,
        )

    @pl.loop(1, half)
    def _(d):
        gram_copy(lax.rem(5 * d, half)).start()

    @pl.loop(0, half, step=8)
    def _(i):
        make_parts(carry_box, i, 8, both)

    @pl.loop(1, half)
    def _(d):
        part_copy(carry_box, carry_sum, 1, lax.rem(chip + 5 * d, half)).start()

    arrived = all_of(gram_sum, half - 1)
    pltpu.make_async_copy(arrived, arrived, mr_sem).wait()

    gram_all[own_share, :] = tree_sum([gram_sum[i] for i in range(half)])

    def rows_copy(d, c):
        return pltpu.make_async_remote_copy(
            src_ref=gram_all.at[own_share],
            dst_ref=gram_all.at[own_share],
            send_sem=ts_sem,
            recv_sem=tr_sem,
            device_id={"gx": 2 * chip + lax.rem(core + c, 2), "gy": lax.rem(gy + d, ngy)},
            device_id_type=MESH,
        )

    others = ((1, 0), (3, 0), (2, 0), (0, 1), (1, 1), (3, 1), (2, 1))
    for d, c in others:
        rows_copy(d, c).start()
    arrived = all_of(gram_all, 16 * len(others))
    pltpu.make_async_copy(arrived, arrived, tr_sem).wait()

    gram, mix = newton_schulz(*scaled(gram_all[...], 128.0 * ngx), range(EARLY_STEPS))
    gram_ref[...] = gram
    mix_ref[...] = mix
    carried_ref[...] = summed(carry_box, carry_sum, 1)
    image_ref[...] = image_own[pl.ds(pl.multiple_of(gy * 32, 32), 32), :]

    for d in range(2):
        pltpu.make_async_copy(x_send, x_send, xs_sem.at[d]).wait()
        pltpu.make_async_copy(y_send.at[d], y_send.at[d], ys_sem.at[d]).wait()
    pltpu.make_async_copy(outbox, outbox, cs_sem).wait()
    for which in range(2):
        sent = part_box.at[pl.ds(0, half - 1)]
        pltpu.make_async_copy(sent, sent, as_sem.at[which]).wait()
    sent = all_of(proj, (half - 1) * 128)
    pltpu.make_async_copy(sent, sent, gs_sem).wait()
    half_copy.wait_send()
    pair_image_copy.wait_send()
    sent = gram_sum.at[pl.ds(0, half - 1)]
    pltpu.make_async_copy(sent, sent, ms_sem).wait()
    sent = all_of(gram_all, 16 * len(others))
    pltpu.make_async_copy(sent, sent, ts_sem).wait()
    sent = all_of(image_part, ngy - 1)
    pltpu.make_async_copy(sent, sent, is_sem).wait()


def finish(count, evolved_ref, gram_ref, mix_ref, carried_ref, image_ref, out_hbm, factor_ref, core_ref, sem):
    writing = pltpu.make_async_copy(evolved_ref, out_hbm, sem)
    writing.start()
    _, mix = newton_schulz(gram_ref[...], mix_ref[...], range(EARLY_STEPS, NS_STEPS))
    factor_ref[...] = full_dot(image_ref[...], mix).astype(BF16)
    result = full_dot(carried_ref[...], mix) * (count ** -0.5)
    ny = core_ref.shape[2]
    core_ref[0, 0] = result[:ny]
    core_ref[0, 1] = result[ny:]
    writing.wait()


def shards(initial_state, velocity, diffusivity, reaction_rate, start_basis):
    species, nz, ny, nx = initial_state.shape
    ngx, ngy = lax.axis_size("gx"), lax.axis_size("gy")
    rank = start_basis.shape[1]
    operands = (initial_state, velocity, diffusivity, reaction_rate, start_basis)
    exchanges = SECTIONS * GROUPS
    rows = 2 * species // GROUPS
    hbm = pl.BlockSpec(memory_space=pltpu.HBM)
    vmem = pl.BlockSpec(memory_space=pltpu.VMEM)
    dma = pltpu.SemaphoreType.DMA
    evolved, gram, mix, carried, image = pl.pallas_call(
        kernel,
        out_shape=(
            jax.ShapeDtypeStruct(initial_state.shape, F32),
            jax.ShapeDtypeStruct((rank, rank), F32),
            jax.ShapeDtypeStruct((rank, rank), F32),
            jax.ShapeDtypeStruct((nz * ny, rank), F32),
            jax.ShapeDtypeStruct((nx // ngy, rank), F32),
        ),
        in_specs=[hbm] * 5,
        out_specs=(vmem,) * 5,
        scratch_shapes=[
            pltpu.VMEM((species, nz, ny + 16, nx), F32),
            pltpu.VMEM((species, nz, ny + 16, nx), F32),
            pltpu.VMEM((3, nz, ny, nx), F32),
            pltpu.SMEM((species,), F32),
            pltpu.SMEM((species,), F32),
            pltpu.VMEM((2 * nx, rank), BF16),
            pltpu.VMEM((ny, nx), F32),
            pltpu.VMEM((exchanges, ny, nx), BF16),
            pltpu.VMEM((exchanges, 2, ny, nx), BF16),
            pltpu.VMEM((2, exchanges, rows, nx), F32),
            pltpu.VMEM((exchanges, 2, rows, nx), F32),
            pltpu.VMEM((species // 2, nz * ny, 2 * nx), BF16),
            pltpu.VMEM((species // 2, nz * ny, nx), BF16),
            pltpu.VMEM((2 * nx, species // 2 * nz * ny), BF16),
            pltpu.VMEM((ngx // 2, nz * ny, rank), BF16),
            pltpu.VMEM((ngx // 2, nz * ny, rank), BF16),
            pltpu.VMEM((ngx // 2, nz * ny, rank), BF16),
            pltpu.VMEM((ngx // 2, nz * ny, rank), BF16),
            pltpu.VMEM((species // 2 * nz * ny, rank), BF16),
            pltpu.VMEM((nx, rank), BF16),
            pltpu.VMEM((nx, rank), BF16),
            pltpu.VMEM((ngy, nx, rank), BF16),
            pltpu.VMEM((2, nx, rank), BF16),
            pltpu.VMEM((nx, rank), F32),
            pltpu.VMEM((rank, rank), F32),
            pltpu.VMEM((ngx // 2, rank // (2 * ngy), rank), F32),
            pltpu.VMEM((rank, rank), F32),
            dma((GROUPS + 4,)),
            dma((2,)),
            dma((exchanges,)),
            dma((2,)),
            dma((exchanges,)),
            dma,
            dma((GROUPS,)),
            dma((2,)),
            dma((2,)),
            dma,
            dma((ngx // 2,)),
            dma,
            dma,
            dma,
            dma,
            dma,
            dma,
            dma,
            dma,
            dma,
            dma,
        ],
        compiler_params=pltpu.CompilerParams(
            collective_id=0, has_side_effects=True, vmem_limit_bytes=VMEM_LIMIT
        ),
    )(*(pltpu.with_memory_space_constraint(x, pltpu.HBM) for x in operands))
    return pl.pallas_call(
        functools.partial(finish, float(nx * ngx)),
        out_shape=(
            jax.ShapeDtypeStruct(initial_state.shape, F32),
            jax.ShapeDtypeStruct((nx // ngy, rank), BF16),
            jax.ShapeDtypeStruct((1, nz, ny, rank), F32),
        ),
        in_specs=[pl.BlockSpec(memory_space=pl.ANY), vmem, vmem, vmem, vmem],
        out_specs=(hbm, vmem, vmem),
        scratch_shapes=[dma],
        compiler_params=pltpu.CompilerParams(vmem_limit_bytes=8 << 20),
    )(evolved, gram, mix, carried, image)


def solution(mesh):
    return jax.shard_map(
        shards,
        mesh=mesh,
        in_specs=(P(None, None, "gy", "gx"), P(None, None, "gy", "gx"), P(), P(), P()),
        out_specs=(P(None, None, "gy", "gx"), P(("gx", "gy"), None), P("gx", None, "gy", None)),
        check_vma=False,
    )
```

```python
import functools

import jax
import jax.numpy as jnp
from jax import lax
from jax.experimental import pallas as pl
from jax.experimental.pallas import tpu as pltpu
from jax.sharding import PartitionSpec as P

SECTIONS = 4
NS_STEPS = 5
EARLY_STEPS = 3
GROUPS = 8
PLANES = 4
UNROLL = 4
VMEM_LIMIT = 32 << 20
MESH = pl.DeviceIdType.MESH
F32 = jnp.float32
BF16 = jnp.bfloat16


def rolled(x, shift):
    return pltpu.roll(x, shift, 1)


def halves(x):
    high = x.astype(BF16)
    return high, (x - high.astype(F32)).astype(BF16)


def full_dot(a, b):
    a_high, a_low = halves(a)
    b_high, b_low = halves(b)
    return jnp.dot(
        jnp.concatenate([a_high, a_high, a_low], axis=1),
        jnp.concatenate([b_high, b_low, b_high], axis=0),
        preferred_element_type=F32,
    )


def tree_sum(terms):
    while len(terms) > 1:
        terms = [a + b for a, b in zip(terms[::2], terms[1::2])]
    return terms[0]


def identity_like(gram):
    row = lax.broadcasted_iota(jnp.int32, gram.shape, 0)
    column = lax.broadcasted_iota(jnp.int32, gram.shape, 1)
    return jnp.where(row == column, 1.0, 0.0).astype(F32)


def scaled(gram, count):
    identity = identity_like(gram)
    trace = jnp.sum(gram * identity, keepdims=True)
    squared = count / (trace + 1e-6)
    return gram * (squared / count), jnp.sqrt(squared) * identity


def newton_schulz(gram, mix, steps):
    identity = identity_like(gram)
    for step in steps:
        poly = 1.5 * identity - 0.5 * gram
        mix = full_dot(mix, poly)
        if step < NS_STEPS - 1:
            gram = full_dot(poly, full_dot(gram, poly))
    return gram, mix


def kernel(
    init_hbm, vel_hbm, kappa_hbm, rate_hbm, basis_hbm,
    evolved_ref, gram_ref, mix_ref, carried_ref, image_ref,
    state, state_b, vel, kappa_ref, rate_ref, basis, halos, x_send, x_recv, y_send, y_recv,
    pairs, outbox, pairs_t, part_box, part_sum, carry_box, carry_sum, proj, half_send, half_recv, image_part, image_pair, image_own, gram_part, gram_sum, gram_all,
    load_sem, xs_sem, xr_sem, ys_sem, cs_sem, cr_sem, as_sem, ar_sem, gs_sem, gr_sem, is_sem, ir_sem, hs_sem, hr_sem, ps_sem, pr_sem, ms_sem, mr_sem, ts_sem, tr_sem,
):
    species = state.shape[0]
    ny = state.shape[2] - 16
    per = species // GROUPS
    ngx, ngy = lax.axis_size("gx"), lax.axis_size("gy")
    gx, gy = lax.axis_index("gx"), lax.axis_index("gy")
    right, left = lax.rem(gx + 1, ngx), lax.rem(gx + ngx - 1, ngx)
    north, south = lax.rem(gy + 1, ngy), lax.rem(gy + ngy - 1, ngy)
    core = lax.rem(gx, 2)
    half = ngx // 2
    chip = gx // 2
    sibling = gx + 1 - 2 * core
    own_lanes = pl.ds(pl.multiple_of(core * 128, 128), 128)
    pairs_per = per // 2
    in_a_plane = species // PLANES
    line = in_a_plane // 2
    lane = lax.broadcasted_iota(jnp.int32, (ny, 128), 1)
    pair = lane // 2

    def load_state(g):
        return pltpu.make_async_copy(
            init_hbm.at[pl.ds(g * per, per)],
            state.at[pl.ds(g * per, per), :, pl.ds(8, ny), :],
            load_sem.at[4 + g],
        )

    load_vel = pltpu.make_async_copy(vel_hbm, vel, load_sem.at[1])
    load_kappa = pltpu.make_async_copy(kappa_hbm, kappa_ref, load_sem.at[2])
    load_rate = pltpu.make_async_copy(rate_hbm, rate_ref, load_sem.at[3])
    barrier = pltpu.get_barrier_semaphore()
    for peer in (left, right):
        pl.semaphore_signal(barrier, 1, device_id={"gx": peer}, device_id_type=MESH)
    for g in range(GROUPS):
        load_state(g).start()

    @pl.loop(1, ngy)
    def _(d):
        peer = lax.rem(gy + d, ngy)
        pl.semaphore_signal(barrier, 1, device_id={"gy": peer}, device_id_type=MESH)
        pl.semaphore_signal(barrier, 1, device_id={"gx": sibling, "gy": peer}, device_id_type=MESH)

    @pl.loop(1, half)
    def _(d):
        peer = lax.rem(gx + 2 * d, ngx)
        pl.semaphore_signal(barrier, 1, device_id={"gx": peer}, device_id_type=MESH)

    load_kappa.start()
    load_rate.start()
    load_vel.start()

    def x_copy(e, to_left):
        return pltpu.make_async_remote_copy(
            src_ref=x_send.at[e],
            dst_ref=x_recv.at[e, int(to_left)],
            send_sem=xs_sem.at[int(to_left)],
            recv_sem=xr_sem.at[e],
            device_id={"gx": left if to_left else right},
            device_id_type=MESH,
        )

    def y_copy(e, to_south):
        d = int(to_south)
        return pltpu.make_async_remote_copy(
            src_ref=y_send.at[d, e],
            dst_ref=y_recv.at[e, d],
            send_sem=ys_sem.at[d],
            recv_sem=xr_sem.at[e],
            device_id={"gy": south if to_south else north},
            device_id_type=MESH,
        )

    def pair_copy(g):
        return pltpu.make_async_remote_copy(
            src_ref=outbox.at[pl.ds(g * pairs_per, pairs_per)],
            dst_ref=pairs.at[pl.ds(g * pairs_per, pairs_per), :, own_lanes],
            send_sem=cs_sem,
            recv_sem=cr_sem.at[g],
            device_id={"gx": sibling},
            device_id_type=MESH,
        )

    def part_copy(box, total, which, i):
        return pltpu.make_async_remote_copy(
            src_ref=box.at[i],
            dst_ref=total.at[chip],
            send_sem=as_sem.at[which],
            recv_sem=ar_sem.at[which],
            device_id={"gx": 2 * i + core},
            device_id_type=MESH,
        )

    def make_parts(box, first, count, rows):
        cells = pairs[pl.ds(first, count)].reshape(count * pairs.shape[1], pairs.shape[2])
        parts = jnp.dot(cells, rows, preferred_element_type=F32).astype(BF16)
        box[pl.ds(first, count)] = parts.reshape(count, *box.shape[1:])

    def all_of(ref, count):
        return ref.at[pl.ds(0, count)]

    def summed(box, total, which):
        arrived = all_of(total, half - 1)
        pltpu.make_async_copy(arrived, arrived, ar_sem.at[which]).wait()
        total[chip] = box[chip]
        return tree_sum([total[i].astype(F32) for i in range(half)])

    def pack_edges(e, now, first):
        packed = jnp.zeros((ny, 128), F32)
        for f in range(2 * per):
            field = now.at[first + f // 2, f % 2]
            packed = jnp.where(pair == f, rolled(field[pl.ds(8, ny), :], 2 * f + 1), packed)
            y_send[0, e, pl.ds(f, 1), :] = field[pl.ds(7 + ny, 1), :]
            y_send[1, e, pl.ds(f, 1), :] = field[pl.ds(8, 1), :]
        x_send[e] = packed.astype(x_send.dtype)

    def send_edges(e):
        x_copy(e, True).start()
        x_copy(e, False).start()
        y_copy(e, True).start()
        y_copy(e, False).start()

    load_state(0).wait()
    pack_edges(0, state, 0)
    pl.semaphore_wait(barrier, half + 2 * ngy - 1)
    send_edges(0)

    @pl.loop(1, GROUPS)
    def _(g):
        load_state(g).wait()
        pack_edges(g, state, g * per)
        send_edges(g)

    basis_rows = pl.ds(pl.multiple_of(chip * 256, 256), 256)
    load_basis = pltpu.make_async_copy(basis_hbm.at[basis_rows], basis, load_sem.at[0])
    load_basis.start()
    load_vel.wait()
    vel[...] = vel[...] * 0.5
    vel[2, 1] = -vel[2, 1]
    load_kappa.wait()
    load_rate.wait()

    assert 2 * ny * 128 * 2 + 2 * 2 * per * 128 * 4 == (ny + 16) * 128 * 4

    def advance(k, g, now, new):
        e = k * GROUPS + g
        last = k == SECTIONS - 1
        pltpu.make_async_copy(state.at[0, 0], state.at[0, 0], xr_sem.at[e]).wait()

        wide = lax.broadcasted_iota(jnp.int32, halos.shape, 1)
        halos[...] = jnp.where(
            lax.rem(wide, 2) == 0,
            rolled(x_recv[e, 1].astype(F32), 127),
            rolled(x_recv[e, 0].astype(F32), 1),
        )

        for j in range(per):
            for z in range(2):
                now[g * per + j, z, pl.ds(7, 1), :] = y_recv[e, 0, pl.ds(2 * j + z, 1), :]
                now[g * per + j, z, pl.ds(8 + ny, 1), :] = y_recv[e, 1, pl.ds(2 * j + z, 1), :]

        def step(j, box):
            s = g * per + j
            kappa, rate = kappa_ref[s], rate_ref[s]
            middle = 1.0 - 6.0 * kappa - rate
            for z in range(2):
                c = now[s, z, pl.ds(8, ny), :]
                other = now[s, 1 - z, pl.ds(8, ny), :]
                up = now[s, z, pl.ds(9, ny), :]
                down = now[s, z, pl.ds(7, ny), :]
                halo = rolled(halos[...], lax.rem(255 - 4 * j - 2 * z, 128))
                east = jnp.where(lane == 127, halo, rolled(c, 127))
                west = jnp.where(lane == 0, halo, rolled(c, 1))
                result = (
                    c * (middle + rate * (1.0 / (1.0 + c * c)))
                    + kappa * ((east + west) + (up + down))
                    + (kappa - vel[2, z]) * other
                    - vel[0, z] * (east - west)
                    - vel[1, z] * (up - down)
                )
                if last:
                    evolved_ref[s, z] = result
                    cells = result.astype(BF16)
                    if box is pairs:
                        pairs[s // 2, pl.ds(z * ny, ny), own_lanes] = cells
                    else:
                        outbox[s // 2, pl.ds(z * ny, ny), :] = cells
                else:
                    new[s, z, pl.ds(8, ny), :] = result

        if last:
            for i in range(pairs_per):
                step(2 * i + 1 - core, outbox)
            for i in range(pairs_per):
                step(2 * i + core, pairs)
            pair_copy(g).start()
        else:

            @pl.loop(0, per, step=UNROLL)
            def _(j):
                for i in range(UNROLL):
                    step(j + i, None)

        if not last:
            pack_edges(e + GROUPS, new, g * per)
            send_edges(e + GROUPS)

    buffers = (state, state_b)
    for k in range(SECTIONS - 1):

        @pl.loop(0, GROUPS)
        def _(g):
            advance(k, g, buffers[k % 2], buffers[(k + 1) % 2])

    load_basis.wait()

    def plane_parts(p):
        for g in range(GROUPS // PLANES):
            pair_copy(p * (GROUPS // PLANES) + g).wait_recv()
        make_parts(part_box, p * line, line, basis[...])

        @pl.loop(0, line)
        def _(d):
            i = p * line + lax.rem(chip + d, line)

            @pl.when(i != chip)
            def _():
                part_copy(part_box, part_sum, 0, i).start()

    @pl.loop(0, PLANES)
    def _(p):
        for g in range(GROUPS // PLANES):
            advance(SECTIONS - 1, p * (GROUPS // PLANES) + g, buffers[(SECTIONS - 1) % 2], None)

        @pl.when(p > 0)
        def _():
            plane_parts(p - 1)

    plane_parts(PLANES - 1)

    @pl.loop(0, half, step=2)
    def _(i):
        for k in range(2):
            pairs_t[:, pl.ds(pl.multiple_of((i + k) * 128, 128), 128)] = pairs[i + k].T

    def block(x):
        return pl.ds(pl.multiple_of(x // 2 * 128, 128), 128)

    plane = gx // in_a_plane

    def in_plane(x, d):
        return x // in_a_plane * in_a_plane + lax.rem(x + 2 * d, in_a_plane)

    def other_plane(x, d):
        return lax.rem(x + d * in_a_plane, ngx)

    def send(x, peer, arrives):
        pltpu.make_async_remote_copy(
            src_ref=proj.at[block(x)],
            dst_ref=proj.at[block(x)],
            send_sem=gs_sem,
            recv_sem=gr_sem.at[arrives],
            device_id={"gx": peer},
            device_id_type=MESH,
        ).start()

    def arrival(x):
        pltpu.make_async_copy(proj.at[block(x)], proj.at[block(x)], gr_sem.at[x // in_a_plane]).wait()

    order = (1, 3, 2)

    proj[block(gx), :] = summed(part_box, part_sum, 0).astype(BF16)

    for d in order:
        send(gx, other_plane(gx, d), plane)
    for d in order:
        send(gx, in_plane(gx, d), PLANES)

    @pl.loop(0, PLANES)
    def _(p):
        @pl.when(p != plane)
        def _():
            x = p * in_a_plane + lax.rem(gx, in_a_plane)
            arrival(x)
            for d in order:
                send(x, in_plane(gx, d), PLANES)

    arrived = all_of(proj, (half - PLANES) * 128)
    pltpu.make_async_copy(arrived, arrived, gr_sem.at[PLANES]).wait()

    def image_half(c):
        rows = pl.ds(pl.multiple_of(c * 128, 128), 128)
        return jnp.dot(pairs_t[rows, :], proj[...], preferred_element_type=F32)

    half_send[...] = image_half(1 - core).astype(BF16)
    half_copy = pltpu.make_async_remote_copy(
        src_ref=half_send,
        dst_ref=half_recv,
        send_sem=hs_sem,
        recv_sem=hr_sem,
        device_id={"gx": sibling},
        device_id_type=MESH,
    )
    half_copy.start()
    part = image_half(core)
    half_copy.wait_recv()
    part = part + half_recv[...].astype(F32)

    image_part[gy] = part.astype(BF16)

    def image_copy(d):
        return pltpu.make_async_remote_copy(
            src_ref=image_part.at[gy],
            dst_ref=image_part.at[gy],
            send_sem=is_sem,
            recv_sem=ir_sem,
            device_id={"gy": lax.rem(gy + d, ngy)},
            device_id_type=MESH,
        )

    for d in (1, 3, 2):
        image_copy(d).start()
    arrived = all_of(image_part, ngy - 1)
    pltpu.make_async_copy(arrived, arrived, ir_sem).wait()
    image_own[...] = (image_part[0].astype(F32) + image_part[1].astype(F32)) + (
        image_part[2].astype(F32) + image_part[3].astype(F32)
    )
    image_pair[core] = image_own[...].astype(BF16)

    pair_image_copy = pltpu.make_async_remote_copy(
        src_ref=image_pair.at[core],
        dst_ref=image_pair.at[core],
        send_sem=ps_sem,
        recv_sem=pr_sem,
        device_id={"gx": sibling},
        device_id_type=MESH,
    )
    pair_image_copy.start()
    pair_image_copy.wait_recv()
    both = jnp.concatenate([image_pair[0], image_pair[1]], axis=0)

    gram_part[...] = lax.dot_general(both, both, (((0,), (0,)), ((), ())), preferred_element_type=F32)
    def share(y, c):
        return pl.ds(pl.multiple_of(y * 32 + c * 16, 16), 16)

    own_share = share(gy, core)
    gram_sum[chip] = gram_part[own_share, :]

    def gram_copy(d):
        return pltpu.make_async_remote_copy(
            src_ref=gram_part.at[own_share],
            dst_ref=gram_sum.at[chip],
            send_sem=ms_sem,
            recv_sem=mr_sem,
            device_id={"gx": lax.rem(gx + 2 * d, ngx)},
            device_id_type=MESH,
        )

    @pl.loop(1, half)
    def _(d):
        gram_copy(lax.rem(5 * d, half)).start()

    @pl.loop(0, half, step=8)
    def _(i):
        make_parts(carry_box, i, 8, both)

    @pl.loop(1, half)
    def _(d):
        part_copy(carry_box, carry_sum, 1, lax.rem(chip + 5 * d, half)).start()

    arrived = all_of(gram_sum, half - 1)
    pltpu.make_async_copy(arrived, arrived, mr_sem).wait()

    gram_all[own_share, :] = tree_sum([gram_sum[i] for i in range(half)])

    def rows_copy(d, c):
        return pltpu.make_async_remote_copy(
            src_ref=gram_all.at[own_share],
            dst_ref=gram_all.at[own_share],
            send_sem=ts_sem,
            recv_sem=tr_sem,
            device_id={"gx": 2 * chip + lax.rem(core + c, 2), "gy": lax.rem(gy + d, ngy)},
            device_id_type=MESH,
        )

    others = ((1, 0), (3, 0), (2, 0), (0, 1), (1, 1), (3, 1), (2, 1))
    for d, c in others:
        rows_copy(d, c).start()
    arrived = all_of(gram_all, 16 * len(others))
    pltpu.make_async_copy(arrived, arrived, tr_sem).wait()

    gram, mix = newton_schulz(*scaled(gram_all[...], 128.0 * ngx), range(EARLY_STEPS))
    gram_ref[...] = gram
    mix_ref[...] = mix
    carried_ref[...] = summed(carry_box, carry_sum, 1)
    image_ref[...] = image_own[pl.ds(pl.multiple_of(gy * 32, 32), 32), :]

    for d in range(2):
        pltpu.make_async_copy(x_send, x_send, xs_sem.at[d]).wait()
        pltpu.make_async_copy(y_send.at[d], y_send.at[d], ys_sem.at[d]).wait()
    pltpu.make_async_copy(outbox, outbox, cs_sem).wait()
    for which in range(2):
        sent = part_box.at[pl.ds(0, half - 1)]
        pltpu.make_async_copy(sent, sent, as_sem.at[which]).wait()
    sent = all_of(proj, (half - 1) * 128)
    pltpu.make_async_copy(sent, sent, gs_sem).wait()
    half_copy.wait_send()
    pair_image_copy.wait_send()
    sent = gram_sum.at[pl.ds(0, half - 1)]
    pltpu.make_async_copy(sent, sent, ms_sem).wait()
    sent = all_of(gram_all, 16 * len(others))
    pltpu.make_async_copy(sent, sent, ts_sem).wait()
    sent = all_of(image_part, ngy - 1)
    pltpu.make_async_copy(sent, sent, is_sem).wait()


def finish(count, evolved_ref, gram_ref, mix_ref, carried_ref, image_ref, out_hbm, factor_ref, core_ref, sem):
    writing = pltpu.make_async_copy(evolved_ref, out_hbm, sem)
    writing.start()
    _, mix = newton_schulz(gram_ref[...], mix_ref[...], range(EARLY_STEPS, NS_STEPS))
    factor_ref[...] = full_dot(image_ref[...], mix).astype(BF16)
    result = full_dot(carried_ref[...], mix) * (count ** -0.5)
    ny = core_ref.shape[2]
    core_ref[0, 0] = result[:ny]
    core_ref[0, 1] = result[ny:]
    writing.wait()


def shards(initial_state, velocity, diffusivity, reaction_rate, start_basis):
    species, nz, ny, nx = initial_state.shape
    ngx, ngy = lax.axis_size("gx"), lax.axis_size("gy")
    rank = start_basis.shape[1]
    operands = (initial_state, velocity, diffusivity, reaction_rate, start_basis)
    exchanges = SECTIONS * GROUPS
    rows = 2 * species // GROUPS
    hbm = pl.BlockSpec(memory_space=pltpu.HBM)
    vmem = pl.BlockSpec(memory_space=pltpu.VMEM)
    dma = pltpu.SemaphoreType.DMA
    evolved, gram, mix, carried, image = pl.pallas_call(
        kernel,
        out_shape=(
            jax.ShapeDtypeStruct(initial_state.shape, F32),
            jax.ShapeDtypeStruct((rank, rank), F32),
            jax.ShapeDtypeStruct((rank, rank), F32),
            jax.ShapeDtypeStruct((nz * ny, rank), F32),
            jax.ShapeDtypeStruct((nx // ngy, rank), F32),
        ),
        in_specs=[hbm] * 5,
        out_specs=(vmem,) * 5,
        scratch_shapes=[
            pltpu.VMEM((species, nz, ny + 16, nx), F32),
            pltpu.VMEM((species, nz, ny + 16, nx), F32),
            pltpu.VMEM((3, nz, ny, nx), F32),
            pltpu.SMEM((species,), F32),
            pltpu.SMEM((species,), F32),
            pltpu.VMEM((2 * nx, rank), BF16),
            pltpu.VMEM((ny, nx), F32),
            pltpu.VMEM((exchanges, ny, nx), BF16),
            pltpu.VMEM((exchanges, 2, ny, nx), BF16),
            pltpu.VMEM((2, exchanges, rows, nx), F32),
            pltpu.VMEM((exchanges, 2, rows, nx), F32),
            pltpu.VMEM((species // 2, nz * ny, 2 * nx), BF16),
            pltpu.VMEM((species // 2, nz * ny, nx), BF16),
            pltpu.VMEM((2 * nx, species // 2 * nz * ny), BF16),
            pltpu.VMEM((ngx // 2, nz * ny, rank), BF16),
            pltpu.VMEM((ngx // 2, nz * ny, rank), BF16),
            pltpu.VMEM((ngx // 2, nz * ny, rank), BF16),
            pltpu.VMEM((ngx // 2, nz * ny, rank), BF16),
            pltpu.VMEM((species // 2 * nz * ny, rank), BF16),
            pltpu.VMEM((nx, rank), BF16),
            pltpu.VMEM((nx, rank), BF16),
            pltpu.VMEM((ngy, nx, rank), BF16),
            pltpu.VMEM((2, nx, rank), BF16),
            pltpu.VMEM((nx, rank), F32),
            pltpu.VMEM((rank, rank), F32),
            pltpu.VMEM((ngx // 2, rank // (2 * ngy), rank), F32),
            pltpu.VMEM((rank, rank), F32),
            dma((GROUPS + 4,)),
            dma((2,)),
            dma((exchanges,)),
            dma((2,)),
            dma,
            dma((GROUPS,)),
            dma((2,)),
            dma((2,)),
            dma,
            dma((PLANES + 1,)),
            dma,
            dma,
            dma,
            dma,
            dma,
            dma,
            dma,
            dma,
            dma,
            dma,
        ],
        compiler_params=pltpu.CompilerParams(
            collective_id=0, has_side_effects=True, vmem_limit_bytes=VMEM_LIMIT
        ),
    )(*(pltpu.with_memory_space_constraint(x, pltpu.HBM) for x in operands))
    return pl.pallas_call(
        functools.partial(finish, float(nx * ngx)),
        out_shape=(
            jax.ShapeDtypeStruct(initial_state.shape, F32),
            jax.ShapeDtypeStruct((nx // ngy, rank), BF16),
            jax.ShapeDtypeStruct((1, nz, ny, rank), F32),
        ),
        in_specs=[pl.BlockSpec(memory_space=pl.ANY), vmem, vmem, vmem, vmem],
        out_specs=(hbm, vmem, vmem),
        scratch_shapes=[dma],
        compiler_params=pltpu.CompilerParams(vmem_limit_bytes=8 << 20),
    )(evolved, gram, mix, carried, image)


def solution(mesh):
    return jax.shard_map(
        shards,
        mesh=mesh,
        in_specs=(P(None, None, "gy", "gx"), P(None, None, "gy", "gx"), P(), P(), P()),
        out_specs=(P(None, None, "gy", "gx"), P(("gx", "gy"), None), P("gx", None, "gy", None)),
        check_vma=False,
    )
```

```python
import functools

import jax
import jax.numpy as jnp
from jax import lax
from jax.experimental import pallas as pl
from jax.experimental.pallas import tpu as pltpu
from jax.sharding import PartitionSpec as P

SECTIONS = 4
NS_STEPS = 5
EARLY_STEPS = 2
GROUPS = 8
PLANES = 4
UNROLL = 4
VMEM_LIMIT = 32 << 20
MESH = pl.DeviceIdType.MESH
F32 = jnp.float32
BF16 = jnp.bfloat16


def rolled(x, shift):
    return pltpu.roll(x, shift, 1)


def halves(x):
    high = x.astype(BF16)
    return high, (x - high.astype(F32)).astype(BF16)


def full_dot(a, b):
    a_high, a_low = halves(a)
    b_high, b_low = halves(b)
    return jnp.dot(
        jnp.concatenate([a_high, a_high, a_low], axis=1),
        jnp.concatenate([b_high, b_low, b_high], axis=0),
        preferred_element_type=F32,
    )


def tree_sum(terms):
    while len(terms) > 1:
        terms = [a + b for a, b in zip(terms[::2], terms[1::2])]
    return terms[0]


def identity_like(gram):
    row = lax.broadcasted_iota(jnp.int32, gram.shape, 0)
    column = lax.broadcasted_iota(jnp.int32, gram.shape, 1)
    return jnp.where(row == column, 1.0, 0.0).astype(F32)


def scaled(gram, count):
    identity = identity_like(gram)
    trace = jnp.sum(gram * identity, keepdims=True)
    squared = count / (trace + 1e-6)
    return gram * (squared / count), jnp.sqrt(squared) * identity


def newton_schulz(gram, mix, steps):
    identity = identity_like(gram)
    for step in steps:
        poly = 1.5 * identity - 0.5 * gram
        mix = full_dot(mix, poly)
        if step < NS_STEPS - 1:
            gram = full_dot(poly, full_dot(gram, poly))
    return gram, mix


def kernel(
    init_hbm, vel_hbm, kappa_hbm, rate_hbm, basis_hbm,
    evolved_ref, gram_ref, mix_ref, carried_ref, image_ref,
    state, state_b, vel, kappa_ref, rate_ref, basis, halos, x_send, x_recv, y_send, y_recv,
    pairs, outbox, pairs_t, part_box, part_sum, carry_box, carry_sum, proj, half_send, half_recv, image_part, image_pair, image_own, gram_part, gram_sum, gram_all,
    load_sem, xs_sem, xr_sem, ys_sem, cs_sem, cr_sem, as_sem, ar_sem, gs_sem, gr_sem, is_sem, ir_sem, hs_sem, hr_sem, ps_sem, pr_sem, ms_sem, mr_sem, ts_sem, tr_sem,
):
    species = state.shape[0]
    ny = state.shape[2] - 16
    per = species // GROUPS
    ngx, ngy = lax.axis_size("gx"), lax.axis_size("gy")
    gx, gy = lax.axis_index("gx"), lax.axis_index("gy")
    right, left = lax.rem(gx + 1, ngx), lax.rem(gx + ngx - 1, ngx)
    north, south = lax.rem(gy + 1, ngy), lax.rem(gy + ngy - 1, ngy)
    core = lax.rem(gx, 2)
    half = ngx // 2
    chip = gx // 2
    sibling = gx + 1 - 2 * core
    own_lanes = pl.ds(pl.multiple_of(core * 128, 128), 128)
    pairs_per = per // 2
    in_a_plane = species // PLANES
    line = in_a_plane // 2
    lane = lax.broadcasted_iota(jnp.int32, (ny, 128), 1)
    pair = lane // 2

    def load_state(g):
        return pltpu.make_async_copy(
            init_hbm.at[pl.ds(g * per, per)],
            state.at[pl.ds(g * per, per), :, pl.ds(8, ny), :],
            load_sem.at[4 + g],
        )

    load_vel = pltpu.make_async_copy(vel_hbm, vel, load_sem.at[1])
    load_kappa = pltpu.make_async_copy(kappa_hbm, kappa_ref, load_sem.at[2])
    load_rate = pltpu.make_async_copy(rate_hbm, rate_ref, load_sem.at[3])
    barrier = pltpu.get_barrier_semaphore()
    for peer in (left, right):
        pl.semaphore_signal(barrier, 1, device_id={"gx": peer}, device_id_type=MESH)
    for g in range(GROUPS):
        load_state(g).start()

    @pl.loop(1, ngy)
    def _(d):
        peer = lax.rem(gy + d, ngy)
        pl.semaphore_signal(barrier, 1, device_id={"gy": peer}, device_id_type=MESH)
        pl.semaphore_signal(barrier, 1, device_id={"gx": sibling, "gy": peer}, device_id_type=MESH)

    @pl.loop(1, half)
    def _(d):
        peer = lax.rem(gx + 2 * d, ngx)
        pl.semaphore_signal(barrier, 1, device_id={"gx": peer}, device_id_type=MESH)

    load_kappa.start()
    load_rate.start()
    load_vel.start()

    def x_copy(e, to_left):
        return pltpu.make_async_remote_copy(
            src_ref=x_send.at[e],
            dst_ref=x_recv.at[e, int(to_left)],
            send_sem=xs_sem.at[int(to_left)],
            recv_sem=xr_sem.at[e],
            device_id={"gx": left if to_left else right},
            device_id_type=MESH,
        )

    def y_copy(e, to_south):
        d = int(to_south)
        return pltpu.make_async_remote_copy(
            src_ref=y_send.at[d, e],
            dst_ref=y_recv.at[e, d],
            send_sem=ys_sem.at[d],
            recv_sem=xr_sem.at[e],
            device_id={"gy": south if to_south else north},
            device_id_type=MESH,
        )

    def pair_copy(g):
        return pltpu.make_async_remote_copy(
            src_ref=outbox.at[pl.ds(g * pairs_per, pairs_per)],
            dst_ref=pairs.at[pl.ds(g * pairs_per, pairs_per), :, own_lanes],
            send_sem=cs_sem,
            recv_sem=cr_sem.at[g],
            device_id={"gx": sibling},
            device_id_type=MESH,
        )

    def part_copy(box, total, which, i):
        return pltpu.make_async_remote_copy(
            src_ref=box.at[i],
            dst_ref=total.at[chip],
            send_sem=as_sem.at[which],
            recv_sem=ar_sem.at[which],
            device_id={"gx": 2 * i + core},
            device_id_type=MESH,
        )

    def make_parts(box, first, count, rows):
        cells = pairs[pl.ds(first, count)].reshape(count * pairs.shape[1], pairs.shape[2])
        parts = jnp.dot(cells, rows, preferred_element_type=F32).astype(BF16)
        box[pl.ds(first, count)] = parts.reshape(count, *box.shape[1:])

    def all_of(ref, count):
        return ref.at[pl.ds(0, count)]

    def summed(box, total, which):
        arrived = all_of(total, half - 1)
        pltpu.make_async_copy(arrived, arrived, ar_sem.at[which]).wait()
        total[chip] = box[chip]
        return tree_sum([total[i].astype(F32) for i in range(half)])

    def pack_edges(e, now, first):
        packed = jnp.zeros((ny, 128), F32)
        for f in range(2 * per):
            field = now.at[first + f // 2, f % 2]
            packed = jnp.where(pair == f, rolled(field[pl.ds(8, ny), :], 2 * f + 1), packed)
            y_send[0, e, pl.ds(f, 1), :] = field[pl.ds(7 + ny, 1), :]
            y_send[1, e, pl.ds(f, 1), :] = field[pl.ds(8, 1), :]
        x_send[e] = packed.astype(x_send.dtype)

    def send_edges(e):
        x_copy(e, True).start()
        x_copy(e, False).start()
        y_copy(e, True).start()
        y_copy(e, False).start()

    load_state(0).wait()
    pack_edges(0, state, 0)
    pl.semaphore_wait(barrier, half + 2 * ngy - 1)
    send_edges(0)

    @pl.loop(1, GROUPS)
    def _(g):
        load_state(g).wait()
        pack_edges(g, state, g * per)
        send_edges(g)

    basis_rows = pl.ds(pl.multiple_of(chip * 256, 256), 256)
    load_basis = pltpu.make_async_copy(basis_hbm.at[basis_rows], basis, load_sem.at[0])
    load_basis.start()
    load_vel.wait()
    vel[...] = vel[...] * 0.5
    vel[2, 1] = -vel[2, 1]
    load_kappa.wait()
    load_rate.wait()

    assert 2 * ny * 128 * 2 + 2 * 2 * per * 128 * 4 == (ny + 16) * 128 * 4

    def advance(k, g, now, new):
        e = k * GROUPS + g
        last = k == SECTIONS - 1
        pltpu.make_async_copy(state.at[0, 0], state.at[0, 0], xr_sem.at[e]).wait()

        wide = lax.broadcasted_iota(jnp.int32, halos.shape, 1)
        halos[...] = jnp.where(
            lax.rem(wide, 2) == 0,
            rolled(x_recv[e, 1].astype(F32), 127),
            rolled(x_recv[e, 0].astype(F32), 1),
        )

        for j in range(per):
            for z in range(2):
                now[g * per + j, z, pl.ds(7, 1), :] = y_recv[e, 0, pl.ds(2 * j + z, 1), :]
                now[g * per + j, z, pl.ds(8 + ny, 1), :] = y_recv[e, 1, pl.ds(2 * j + z, 1), :]

        def step(j, box):
            s = g * per + j
            kappa, rate = kappa_ref[s], rate_ref[s]
            middle = 1.0 - 6.0 * kappa - rate
            for z in range(2):
                c = now[s, z, pl.ds(8, ny), :]
                other = now[s, 1 - z, pl.ds(8, ny), :]
                up = now[s, z, pl.ds(9, ny), :]
                down = now[s, z, pl.ds(7, ny), :]
                halo = rolled(halos[...], lax.rem(255 - 4 * j - 2 * z, 128))
                east = jnp.where(lane == 127, halo, rolled(c, 127))
                west = jnp.where(lane == 0, halo, rolled(c, 1))
                result = (
                    c * (middle + rate * (1.0 / (1.0 + c * c)))
                    + kappa * ((east + west) + (up + down))
                    + (kappa - vel[2, z]) * other
                    - vel[0, z] * (east - west)
                    - vel[1, z] * (up - down)
                )
                if last:
                    evolved_ref[s, z] = result
                    cells = result.astype(BF16)
                    if box is pairs:
                        pairs[s // 2, pl.ds(z * ny, ny), own_lanes] = cells
                    else:
                        outbox[s // 2, pl.ds(z * ny, ny), :] = cells
                else:
                    new[s, z, pl.ds(8, ny), :] = result

        if last:
            for i in range(pairs_per):
                step(2 * i + 1 - core, outbox)
            for i in range(pairs_per):
                step(2 * i + core, pairs)
            pair_copy(g).start()
        else:

            @pl.loop(0, per, step=UNROLL)
            def _(j):
                for i in range(UNROLL):
                    step(j + i, None)

        if not last:
            pack_edges(e + GROUPS, new, g * per)
            send_edges(e + GROUPS)

    buffers = (state, state_b)
    for k in range(SECTIONS - 1):

        @pl.loop(0, GROUPS)
        def _(g):
            advance(k, g, buffers[k % 2], buffers[(k + 1) % 2])

    load_basis.wait()

    def plane_parts(p):
        for g in range(GROUPS // PLANES):
            pair_copy(p * (GROUPS // PLANES) + g).wait_recv()
        make_parts(part_box, p * line, line, basis[...])

        @pl.loop(0, line)
        def _(d):
            i = p * line + lax.rem(chip + d, line)

            @pl.when(i != chip)
            def _():
                part_copy(part_box, part_sum, 0, i).start()

    @pl.loop(0, PLANES)
    def _(p):
        for g in range(GROUPS // PLANES):
            advance(SECTIONS - 1, p * (GROUPS // PLANES) + g, buffers[(SECTIONS - 1) % 2], None)

        @pl.when(p > 0)
        def _():
            plane_parts(p - 1)

    plane_parts(PLANES - 1)

    @pl.loop(0, half, step=2)
    def _(i):
        for k in range(2):
            pairs_t[:, pl.ds(pl.multiple_of((i + k) * 128, 128), 128)] = pairs[i + k].T

    def block(x):
        return pl.ds(pl.multiple_of(x // 2 * 128, 128), 128)

    plane = gx // in_a_plane

    def in_plane(x, d):
        return x // in_a_plane * in_a_plane + lax.rem(x + 2 * d, in_a_plane)

    def other_plane(x, d):
        return lax.rem(x + d * in_a_plane, ngx)

    def send(x, peer, arrives):
        pltpu.make_async_remote_copy(
            src_ref=proj.at[block(x)],
            dst_ref=proj.at[block(x)],
            send_sem=gs_sem,
            recv_sem=gr_sem.at[arrives],
            device_id={"gx": peer},
            device_id_type=MESH,
        ).start()

    def arrival(x):
        pltpu.make_async_copy(proj.at[block(x)], proj.at[block(x)], gr_sem.at[x // in_a_plane]).wait()

    order = (1, 3, 2)

    proj[block(gx), :] = summed(part_box, part_sum, 0).astype(BF16)

    for d in order:
        send(gx, other_plane(gx, d), plane)
    for d in order:
        send(gx, in_plane(gx, d), PLANES)

    @pl.loop(0, PLANES)
    def _(p):
        @pl.when(p != plane)
        def _():
            x = p * in_a_plane + lax.rem(gx, in_a_plane)
            arrival(x)
            for d in order:
                send(x, in_plane(gx, d), PLANES)

    arrived = all_of(proj, (half - PLANES) * 128)
    pltpu.make_async_copy(arrived, arrived, gr_sem.at[PLANES]).wait()

    def image_half(c):
        rows = pl.ds(pl.multiple_of(c * 128, 128), 128)
        return jnp.dot(pairs_t[rows, :], proj[...], preferred_element_type=F32)

    half_send[...] = image_half(1 - core).astype(BF16)
    half_copy = pltpu.make_async_remote_copy(
        src_ref=half_send,
        dst_ref=half_recv,
        send_sem=hs_sem,
        recv_sem=hr_sem,
        device_id={"gx": sibling},
        device_id_type=MESH,
    )
    half_copy.start()
    part = image_half(core)
    half_copy.wait_recv()
    part = part + half_recv[...].astype(F32)

    image_part[gy] = part.astype(BF16)

    def image_copy(d):
        return pltpu.make_async_remote_copy(
            src_ref=image_part.at[gy],
            dst_ref=image_part.at[gy],
            send_sem=is_sem,
            recv_sem=ir_sem,
            device_id={"gy": lax.rem(gy + d, ngy)},
            device_id_type=MESH,
        )

    for d in (1, 3, 2):
        image_copy(d).start()
    arrived = all_of(image_part, ngy - 1)
    pltpu.make_async_copy(arrived, arrived, ir_sem).wait()
    image_own[...] = (image_part[0].astype(F32) + image_part[1].astype(F32)) + (
        image_part[2].astype(F32) + image_part[3].astype(F32)
    )
    image_pair[core] = image_own[...].astype(BF16)

    pair_image_copy = pltpu.make_async_remote_copy(
        src_ref=image_pair.at[core],
        dst_ref=image_pair.at[core],
        send_sem=ps_sem,
        recv_sem=pr_sem,
        device_id={"gx": sibling},
        device_id_type=MESH,
    )
    pair_image_copy.start()
    pair_image_copy.wait_recv()
    both = jnp.concatenate([image_pair[0], image_pair[1]], axis=0)

    gram_part[...] = lax.dot_general(both, both, (((0,), (0,)), ((), ())), preferred_element_type=F32)
    def share(y, c):
        return pl.ds(pl.multiple_of(y * 32 + c * 16, 16), 16)

    own_share = share(gy, core)
    gram_sum[chip] = gram_part[own_share, :]

    def gram_copy(d):
        return pltpu.make_async_remote_copy(
            src_ref=gram_part.at[own_share],
            dst_ref=gram_sum.at[chip],
            send_sem=ms_sem,
            recv_sem=mr_sem,
            device_id={"gx": lax.rem(gx + 2 * d, ngx)},
            device_id_type=MESH,
        )

    @pl.loop(1, half)
    def _(d):
        gram_copy(lax.rem(5 * d, half)).start()

    @pl.loop(0, half, step=8)
    def _(i):
        make_parts(carry_box, i, 8, both)

    @pl.loop(1, half)
    def _(d):
        part_copy(carry_box, carry_sum, 1, lax.rem(chip + 5 * d, half)).start()

    arrived = all_of(gram_sum, half - 1)
    pltpu.make_async_copy(arrived, arrived, mr_sem).wait()

    gram_all[own_share, :] = tree_sum([gram_sum[i] for i in range(half)])

    def rows_copy(d, c):
        return pltpu.make_async_remote_copy(
            src_ref=gram_all.at[own_share],
            dst_ref=gram_all.at[own_share],
            send_sem=ts_sem,
            recv_sem=tr_sem,
            device_id={"gx": 2 * chip + lax.rem(core + c, 2), "gy": lax.rem(gy + d, ngy)},
            device_id_type=MESH,
        )

    others = ((1, 0), (3, 0), (2, 0), (0, 1), (1, 1), (3, 1), (2, 1))
    for d, c in others:
        rows_copy(d, c).start()
    arrived = all_of(gram_all, 16 * len(others))
    pltpu.make_async_copy(arrived, arrived, tr_sem).wait()

    gram, mix = newton_schulz(*scaled(gram_all[...], 128.0 * ngx), range(EARLY_STEPS))
    gram_ref[...] = gram
    mix_ref[...] = mix
    carried_ref[...] = summed(carry_box, carry_sum, 1)
    image_ref[...] = image_own[pl.ds(pl.multiple_of(gy * 32, 32), 32), :]

    for d in range(2):
        pltpu.make_async_copy(x_send, x_send, xs_sem.at[d]).wait()
        pltpu.make_async_copy(y_send.at[d], y_send.at[d], ys_sem.at[d]).wait()
    pltpu.make_async_copy(outbox, outbox, cs_sem).wait()
    for which in range(2):
        sent = part_box.at[pl.ds(0, half - 1)]
        pltpu.make_async_copy(sent, sent, as_sem.at[which]).wait()
    sent = all_of(proj, (half - 1) * 128)
    pltpu.make_async_copy(sent, sent, gs_sem).wait()
    half_copy.wait_send()
    pair_image_copy.wait_send()
    sent = gram_sum.at[pl.ds(0, half - 1)]
    pltpu.make_async_copy(sent, sent, ms_sem).wait()
    sent = all_of(gram_all, 16 * len(others))
    pltpu.make_async_copy(sent, sent, ts_sem).wait()
    sent = all_of(image_part, ngy - 1)
    pltpu.make_async_copy(sent, sent, is_sem).wait()


def finish(count, evolved_ref, gram_ref, mix_ref, carried_ref, image_ref, out_hbm, factor_ref, core_ref, sem):
    writing = pltpu.make_async_copy(evolved_ref, out_hbm, sem)
    writing.start()
    _, mix = newton_schulz(gram_ref[...], mix_ref[...], range(EARLY_STEPS, NS_STEPS))
    factor_ref[...] = full_dot(image_ref[...], mix).astype(BF16)
    result = full_dot(carried_ref[...], mix) * (count ** -0.5)
    ny = core_ref.shape[2]
    core_ref[0, 0] = result[:ny]
    core_ref[0, 1] = result[ny:]
    writing.wait()


def shards(initial_state, velocity, diffusivity, reaction_rate, start_basis):
    species, nz, ny, nx = initial_state.shape
    ngx, ngy = lax.axis_size("gx"), lax.axis_size("gy")
    rank = start_basis.shape[1]
    operands = (initial_state, velocity, diffusivity, reaction_rate, start_basis)
    exchanges = SECTIONS * GROUPS
    rows = 2 * species // GROUPS
    hbm = pl.BlockSpec(memory_space=pltpu.HBM)
    vmem = pl.BlockSpec(memory_space=pltpu.VMEM)
    dma = pltpu.SemaphoreType.DMA
    evolved, gram, mix, carried, image = pl.pallas_call(
        kernel,
        out_shape=(
            jax.ShapeDtypeStruct(initial_state.shape, F32),
            jax.ShapeDtypeStruct((rank, rank), F32),
            jax.ShapeDtypeStruct((rank, rank), F32),
            jax.ShapeDtypeStruct((nz * ny, rank), F32),
            jax.ShapeDtypeStruct((nx // ngy, rank), F32),
        ),
        in_specs=[hbm] * 5,
        out_specs=(vmem,) * 5,
        scratch_shapes=[
            pltpu.VMEM((species, nz, ny + 16, nx), F32),
            pltpu.VMEM((species, nz, ny + 16, nx), F32),
            pltpu.VMEM((3, nz, ny, nx), F32),
            pltpu.SMEM((species,), F32),
            pltpu.SMEM((species,), F32),
            pltpu.VMEM((2 * nx, rank), BF16),
            pltpu.VMEM((ny, nx), F32),
            pltpu.VMEM((exchanges, ny, nx), BF16),
            pltpu.VMEM((exchanges, 2, ny, nx), BF16),
            pltpu.VMEM((2, exchanges, rows, nx), F32),
            pltpu.VMEM((exchanges, 2, rows, nx), F32),
            pltpu.VMEM((species // 2, nz * ny, 2 * nx), BF16),
            pltpu.VMEM((species // 2, nz * ny, nx), BF16),
            pltpu.VMEM((2 * nx, species // 2 * nz * ny), BF16),
            pltpu.VMEM((ngx // 2, nz * ny, rank), BF16),
            pltpu.VMEM((ngx // 2, nz * ny, rank), BF16),
            pltpu.VMEM((ngx // 2, nz * ny, rank), BF16),
            pltpu.VMEM((ngx // 2, nz * ny, rank), BF16),
            pltpu.VMEM((species // 2 * nz * ny, rank), BF16),
            pltpu.VMEM((nx, rank), BF16),
            pltpu.VMEM((nx, rank), BF16),
            pltpu.VMEM((ngy, nx, rank), BF16),
            pltpu.VMEM((2, nx, rank), BF16),
            pltpu.VMEM((nx, rank), F32),
            pltpu.VMEM((rank, rank), F32),
            pltpu.VMEM((ngx // 2, rank // (2 * ngy), rank), F32),
            pltpu.VMEM((rank, rank), F32),
            dma((GROUPS + 4,)),
            dma((2,)),
            dma((exchanges,)),
            dma((2,)),
            dma,
            dma((GROUPS,)),
            dma((2,)),
            dma((2,)),
            dma,
            dma((PLANES + 1,)),
            dma,
            dma,
            dma,
            dma,
            dma,
            dma,
            dma,
            dma,
            dma,
            dma,
        ],
        compiler_params=pltpu.CompilerParams(
            collective_id=0, has_side_effects=True, vmem_limit_bytes=VMEM_LIMIT
        ),
    )(*(pltpu.with_memory_space_constraint(x, pltpu.HBM) for x in operands))
    return pl.pallas_call(
        functools.partial(finish, float(nx * ngx)),
        out_shape=(
            jax.ShapeDtypeStruct(initial_state.shape, F32),
            jax.ShapeDtypeStruct((nx // ngy, rank), BF16),
            jax.ShapeDtypeStruct((1, nz, ny, rank), F32),
        ),
        in_specs=[pl.BlockSpec(memory_space=pl.ANY), vmem, vmem, vmem, vmem],
        out_specs=(hbm, vmem, vmem),
        scratch_shapes=[dma],
        compiler_params=pltpu.CompilerParams(vmem_limit_bytes=8 << 20),
    )(evolved, gram, mix, carried, image)


def solution(mesh):
    return jax.shard_map(
        shards,
        mesh=mesh,
        in_specs=(P(None, None, "gy", "gx"), P(None, None, "gy", "gx"), P(), P(), P()),
        out_specs=(P(None, None, "gy", "gx"), P(("gx", "gy"), None), P("gx", None, "gy", None)),
        check_vma=False,
    )
```
